32 devices in a mesh: dp: 8 (over z, x), mp: 4 (over y, core).
Axes of the slice: x: 2, y: 2, z: 4, core: 2. Of those that a mesh axis runs over, the one named last changes fastest.
Arguments:
- latents: float32 [128, 4, 1024], P(('dp', 'mp')), may hold values from -6 to 6
- noises: float32 [128, 4, 1024], P(('dp', 'mp')), may hold values from -6 to 6
- timesteps: int32 [128], P('dp'), may hold values from 0 to 999, as said below
- labels: int32 [128], P('dp'), may hold values from 0 to 999
- dropped: int32 [128], P('dp'), may hold values 0 or 1
- buckets: int32 [8], P('dp'), may hold values from 0 to 19
- counts: int32 [8], P('dp'), may hold values from 1 to 16, as said below
- joined_weight: float32 [1152, 3456], P('dp', 'mp'), may hold values from -0.1875 to 0.1875
- joined_moment: float32 [1152, 3456], P('dp', 'mp'), may hold values from -1.1920929e-07 to 1.1920929e-07
- joined_second: float32 [1152, 3456], P('dp', 'mp'), may hold values from 1.5599667e-17 to 2.4959467e-16
- mixback_weight: float32 [1152, 1152], P('dp', 'mp'), may hold values from -0.375 to 0.375
- mixback_moment: float32 [1152, 1152], P('dp', 'mp'), may hold values from -1.1920929e-07 to 1.1920929e-07
- mixback_second: float32 [1152, 1152], P('dp', 'mp'), may hold values from 1.5599667e-17 to 2.4959467e-16
- expand_weight: float32 [1152, 4608], P('dp', 'mp'), may hold values from -0.1875 to 0.1875
- expand_moment: float32 [1152, 4608], P('dp', 'mp'), may hold values from -1.1920929e-07 to 1.1920929e-07
- expand_second: float32 [1152, 4608], P('dp', 'mp'), may hold values from 1.5599667e-17 to 2.4959467e-16
- narrow_weight: float32 [1152, 4608], P('dp', 'mp'), may hold values from -0.09375 to 0.09375
- narrow_moment: float32 [1152, 4608], P('dp', 'mp'), may hold values from -1.1920929e-07 to 1.1920929e-07
- narrow_second: float32 [1152, 4608], P('dp', 'mp'), may hold values from 1.5599667e-17 to 2.4959467e-16
- timeone_weight: float32 [256, 1152], P('dp', 'mp'), may hold values from -0.375 to 0.375
- timeone_moment: float32 [256, 1152], P('dp', 'mp'), may hold values from -1.1920929e-07 to 1.1920929e-07
- timeone_second: float32 [256, 1152], P('dp', 'mp'), may hold values from 1.5599667e-17 to 2.4959467e-16
- timetwo_weight: float32 [1152, 1152], P('dp', 'mp'), may hold values from -0.1875 to 0.1875
- timetwo_moment: float32 [1152, 1152], P('dp', 'mp'), may hold values from -1.1920929e-07 to 1.1920929e-07
- timetwo_second: float32 [1152, 1152], P('dp', 'mp'), may hold values from 1.5599667e-17 to 2.4959467e-16
- modulator_weight: float32 [1152, 11520], P('dp', 'mp'), may hold values from -0.1875 to 0.1875
- modulator_moment: float32 [1152, 11520], P('dp', 'mp'), may hold values from -1.1920929e-07 to 1.1920929e-07
- modulator_second: float32 [1152, 11520], P('dp', 'mp'), may hold values from 1.5599667e-17 to 2.4959467e-16
- classes_weight: float32 [1001, 1152], P(None, 'mp'), may hold values from -0.625 to 0.625
- classes_moment: float32 [1001, 1152], P(None, 'mp'), may hold values from -1.4901161e-08 to 1.4901161e-08
- classes_second: float32 [1001, 1152], P(None, 'mp'), may hold values from 2.437448e-19 to 3.8999167e-18
- smalls_weight: float32 [80512], replicated, may hold values from -0.3125 to 0.3125
- smalls_moment: float32 [80512], replicated, may hold values from -4.7683716e-07 to 4.7683716e-07
- smalls_second: float32 [80512], replicated, may hold values from 2.4959467e-16 to 3.9935147e-15
Outputs:
- loss_sum: float32 [], replicated
- token_count: float32 [], replicated
- grad_norm: float32 [], replicated
- joined_first: float32 [1152, 3456], P('dp', 'mp')
- joined_square: float32 [1152, 3456], P('dp', 'mp')
- joined_master: float32 [1152, 3456], P('dp', 'mp')
- mixback_first: float32 [1152, 1152], P('dp', 'mp')
- mixback_square: float32 [1152, 1152], P('dp', 'mp')
- mixback_master: float32 [1152, 1152], P('dp', 'mp')
- expand_first: float32 [1152, 4608], P('dp', 'mp')
- expand_square: float32 [1152, 4608], P('dp', 'mp')
- expand_master: float32 [1152, 4608], P('dp', 'mp')
- narrow_first: float32 [1152, 4608], P('dp', 'mp')
- narrow_square: float32 [1152, 4608], P('dp', 'mp')
- narrow_master: float32 [1152, 4608], P('dp', 'mp')
- timeone_first: float32 [256, 1152], P('dp', 'mp')
- timeone_square: float32 [256, 1152], P('dp', 'mp')
- timeone_master: float32 [256, 1152], P('dp', 'mp')
- timetwo_first: float32 [1152, 1152], P('dp', 'mp')
- timetwo_square: float32 [1152, 1152], P('dp', 'mp')
- timetwo_master: float32 [1152, 1152], P('dp', 'mp')
- modulator_first: float32 [1152, 11520], P('dp', 'mp')
- modulator_square: float32 [1152, 11520], P('dp', 'mp')
- modulator_master: float32 [1152, 11520], P('dp', 'mp')
- classes_first: float32 [1001, 1152], P(None, 'mp')
- classes_square: float32 [1001, 1152], P(None, 'mp')
- classes_master: float32 [1001, 1152], P(None, 'mp')
- smalls_first: float32 [80512], replicated
- smalls_square: float32 [80512], replicated
- smalls_master: float32 [80512], replicated
The draws below stay inside these ranges and needn't reach their ends.
Inputs may be any that keep to these rules, and one draw needn't show every extreme that they name: `timesteps`: each image's timestep lies in its group's bucket: from (50) times the bucket to that plus 1000 // 20 - 1. `counts`: the true images of a group are its last slots; some group is full.
All inputs are finite; a program needn't handle non-finite values. No bound on the sum of `dropped` on one device may be relied on, other than what follows from the above.
Results may differ from the reference program's by a relative error of at most 0.007.
Values may be sent and summed in bfloat16 or wider, within the bound.
No kernel may reach another device: no remote copies, remote signals or barrier semaphores. Data moves between devices by JAX's collectives and lax.ppermute only.
A program may use at most 320 MiB of HBM per device.

```python
import math
import jax
import jax.numpy as jnp
from jax import lax

D = 1152
H = 16
HD = 72
FF = 4608
FREQ = 256
NCLS = 1000
GRID = 16
NB = 20
STEP = 10
TOKS = 256
PIX = 1024
REL = 62
IMG_GRP = 16
IMAGES = 128
LB = 80512
NPARAM = 32051968


def group_draw(key):
    groups = IMAGES // IMG_GRP
    bucket_width = 1000 // NB
    bucket = jax.random.randint(jax.random.fold_in(key, 11), (groups,), 0, NB)
    offset = jax.random.randint(jax.random.fold_in(key, 12), (IMAGES,), 0, bucket_width)
    return (bucket.astype(jnp.int32), (jnp.repeat(bucket, IMG_GRP) * bucket_width + offset).astype(jnp.int32))


def draw_timesteps(key, part):
    return group_draw(key)[1]


def draw_buckets(key, part):
    return group_draw(key)[0]


def draw_counts(key, part):
    groups = IMAGES // IMG_GRP
    lowest = max(IMG_GRP // 3, 1)
    group_rank = jnp.arange(groups)
    baseline = lowest + (IMG_GRP - lowest) * group_rank // max(groups - 1, 1)
    jitter = jax.random.randint(jax.random.fold_in(key, 13), (groups,), -1, 2)
    result = jnp.clip(baseline + jitter, 1, IMG_GRP)
    return jnp.where(group_rank == groups - 1, IMG_GRP, result).astype(jnp.int32)


def plant(values, stream_key, least, largest):
    longest = values.shape.index(max(values.shape))
    spots = []
    for shift in (0, 1):
        where = [jax.random.randint(jax.random.fold_in(stream_key, axis), (), 0, length) for axis, length in enumerate(values.shape)]
        where[longest] = (where[longest] + shift) % values.shape[longest]
        spots.append(tuple(where))
    return values.at[spots[0]].set(least).at[spots[1]].set(largest)


def steps_of(rng, shape, cuts, least, high):
    loudness = 1.0
    for position, shards_of in cuts:
        draws = jax.random.uniform(jax.random.fold_in(jax.random.fold_in(rng, 6), position), (shards_of,), jnp.float32, least / len(cuts), high / len(cuts))
        loudness = loudness * jnp.repeat(jnp.exp(draws), shape[position] // shards_of).reshape((-1,) + (1,) * (len(shape) - 1 - position))
    return loudness


def normal_values(stream_key, extent, scale, bound, cuts=(), kind=jnp.bfloat16):
    level = steps_of(stream_key, extent, cuts, -0.22, 0.18) if cuts else 1.0
    values = jax.random.normal(stream_key, extent, jnp.float32) * scale * level
    return jnp.minimum(jnp.maximum(values, -bound), bound).astype(kind)


def setup_inputs(seed: int = 0) -> dict:
    keys = jax.random.split(jax.random.key(seed), 35)
    latents = normal_values(keys[0], (IMAGES, 4, PIX), 1.0, 6.0, ((0, 32),), jnp.float32)
    noises = normal_values(keys[1], (IMAGES, 4, PIX), 1.0, 6.0, ((0, 32),), jnp.float32)
    timesteps = draw_timesteps(jax.random.fold_in(keys[34], 71), 0)
    labels = plant(jax.random.randint(keys[3], (IMAGES,), 0, NCLS), jax.random.fold_in(keys[3], 1), 0, NCLS - 1).astype(jnp.int32)
    dropped = plant((jax.random.randint(keys[4], (IMAGES,), 0, 10) < 1).astype(jnp.int32), jax.random.fold_in(keys[4], 1), 0, 1)
    buckets = draw_buckets(jax.random.fold_in(keys[34], 71), 0)
    counts = draw_counts(jax.random.fold_in(keys[34], 71), 0)
    joined_weight = normal_values(keys[7], (D, 3 * D), D ** -0.5, 0.1875, ((0, 8), (1, 4)), jnp.float32)
    joined_moment = normal_values(keys[8], (D, 3 * D), (0.00011 * NPARAM ** -0.5), 1.1920928955078125e-07, ((0, 8), (1, 4)), jnp.float32)
    joined_second = jnp.clip(jnp.exp(math.log(2.4959466917183265e-16) - 2.7725887 * jax.random.uniform(keys[9], (D, 3 * D), jnp.float32) ** steps_of(keys[9], (D, 3 * D), ((0, 8), (1, 4)), -0.2, 0.2)), 1.559966682323954e-17, 2.4959466917183265e-16)
    mixback_weight = normal_values(keys[10], (D, D), (D // 4) ** -0.5, 0.375, ((0, 8), (1, 4)), jnp.float32)
    mixback_moment = normal_values(keys[11], (D, D), (0.00011 * NPARAM ** -0.5), 1.1920928955078125e-07, ((0, 8), (1, 4)), jnp.float32)
    mixback_second = jnp.clip(jnp.exp(math.log(2.4959466917183265e-16) - 2.7725887 * jax.random.uniform(keys[12], (D, D), jnp.float32) ** steps_of(keys[12], (D, D), ((0, 8), (1, 4)), -0.2, 0.2)), 1.559966682323954e-17, 2.4959466917183265e-16)
    expand_weight = normal_values(keys[13], (D, FF), D ** -0.5, 0.1875, ((0, 8), (1, 4)), jnp.float32)
    expand_moment = normal_values(keys[14], (D, FF), (0.00011 * NPARAM ** -0.5), 1.1920928955078125e-07, ((0, 8), (1, 4)), jnp.float32)
    expand_second = jnp.clip(jnp.exp(math.log(2.4959466917183265e-16) - 2.7725887 * jax.random.uniform(keys[15], (D, FF), jnp.float32) ** steps_of(keys[15], (D, FF), ((0, 8), (1, 4)), -0.2, 0.2)), 1.559966682323954e-17, 2.4959466917183265e-16)
    narrow_weight = normal_values(keys[16], (D, FF), FF ** -0.5, 0.09375, ((0, 8), (1, 4)), jnp.float32)
    narrow_moment = normal_values(keys[17], (D, FF), (0.00011 * NPARAM ** -0.5), 1.1920928955078125e-07, ((0, 8), (1, 4)), jnp.float32)
    narrow_second = jnp.clip(jnp.exp(math.log(2.4959466917183265e-16) - 2.7725887 * jax.random.uniform(keys[18], (D, FF), jnp.float32) ** steps_of(keys[18], (D, FF), ((0, 8), (1, 4)), -0.2, 0.2)), 1.559966682323954e-17, 2.4959466917183265e-16)
    timeone_weight = normal_values(keys[19], (FREQ, D), FREQ ** -0.5, 0.375, ((0, 8), (1, 4)), jnp.float32)
    timeone_moment = normal_values(keys[20], (FREQ, D), (0.00011 * NPARAM ** -0.5), 1.1920928955078125e-07, ((0, 8), (1, 4)), jnp.float32)
    timeone_second = jnp.clip(jnp.exp(math.log(2.4959466917183265e-16) - 2.7725887 * jax.random.uniform(keys[21], (FREQ, D), jnp.float32) ** steps_of(keys[21], (FREQ, D), ((0, 8), (1, 4)), -0.2, 0.2)), 1.559966682323954e-17, 2.4959466917183265e-16)
    timetwo_weight = normal_values(keys[22], (D, D), D ** -0.5, 0.1875, ((0, 8), (1, 4)), jnp.float32)
    timetwo_moment = normal_values(keys[23], (D, D), (0.00011 * NPARAM ** -0.5), 1.1920928955078125e-07, ((0, 8), (1, 4)), jnp.float32)
    timetwo_second = jnp.clip(jnp.exp(math.log(2.4959466917183265e-16) - 2.7725887 * jax.random.uniform(keys[24], (D, D), jnp.float32) ** steps_of(keys[24], (D, D), ((0, 8), (1, 4)), -0.2, 0.2)), 1.559966682323954e-17, 2.4959466917183265e-16)
    modulator_weight = normal_values(keys[25], (D, 10 * D), D ** -0.5, 0.1875, ((0, 8), (1, 4)), jnp.float32)
    modulator_moment = normal_values(keys[26], (D, 10 * D), (0.00011 * NPARAM ** -0.5), 1.1920928955078125e-07, ((0, 8), (1, 4)), jnp.float32)
    modulator_second = jnp.clip(jnp.exp(math.log(2.4959466917183265e-16) - 2.7725887 * jax.random.uniform(keys[27], (D, 10 * D), jnp.float32) ** steps_of(keys[27], (D, 10 * D), ((0, 8), (1, 4)), -0.2, 0.2)), 1.559966682323954e-17, 2.4959466917183265e-16)
    classes_weight = normal_values(keys[28], (NCLS + 1, D), 0.1, 0.625, ((1, 4),), jnp.float32)
    classes_moment = normal_values(keys[29], (NCLS + 1, D), (0.000014 * NPARAM ** -0.5), 1.4901161193847656e-08, ((1, 4),), jnp.float32)
    classes_second = jnp.clip(jnp.exp(math.log(3.899916705809885e-18) - 2.7725887 * jax.random.uniform(keys[30], (NCLS + 1, D), jnp.float32) ** steps_of(keys[30], (NCLS + 1, D), ((1, 4),), -0.2, 0.2)), 2.437447941131178e-19, 3.899916705809885e-18)
    smalls_weight = normal_values(keys[31], (LB,), 0.05, 0.3125, (), jnp.float32)
    smalls_moment = normal_values(keys[32], (LB,), (0.00044 * NPARAM ** -0.5), 4.76837158203125e-07, (), jnp.float32)
    smalls_second = jnp.clip(jnp.exp(jax.random.uniform(keys[33], (LB,), jnp.float32, math.log(2.4959466917183265e-16), math.log(3.993514706749322e-15))), 2.4959466917183265e-16, 3.993514706749322e-15)
    return dict(latents=latents, noises=noises, timesteps=timesteps, labels=labels, dropped=dropped, buckets=buckets, counts=counts, joined_weight=joined_weight, joined_moment=joined_moment, joined_second=joined_second, mixback_weight=mixback_weight, mixback_moment=mixback_moment, mixback_second=mixback_second, expand_weight=expand_weight, expand_moment=expand_moment, expand_second=expand_second, narrow_weight=narrow_weight, narrow_moment=narrow_moment, narrow_second=narrow_second, timeone_weight=timeone_weight, timeone_moment=timeone_moment, timeone_second=timeone_second, timetwo_weight=timetwo_weight, timetwo_moment=timetwo_moment, timetwo_second=timetwo_second, modulator_weight=modulator_weight, modulator_moment=modulator_moment, modulator_second=modulator_second, classes_weight=classes_weight, classes_moment=classes_moment, classes_second=classes_second, smalls_weight=smalls_weight, smalls_moment=smalls_moment, smalls_second=smalls_second)


@jax.custom_vjp
def low(v):
    return lax.optimization_barrier(v.astype(jnp.bfloat16)).astype(jnp.float32)

@jax.custom_vjp
def low_back(v):
    return v

def low_keep(v):
    return (low(v), None)

def low_pass(kept, grad):
    return (grad,)

def back_keep(v):
    return (v, None)

def back_low(kept, grad):
    return (low(grad),)
low.defvjp(low_keep, low_pass)
low_back.defvjp(back_keep, back_low)
norm_eps = 1e-06
beta_one = 0.9
beta_two = 0.999
learn_rate = 0.04
weight_decay = 0.01
adam_eps = 1e-12
clip_level = 0.001
highest = lax.Precision.HIGHEST

def layout():
    entries = [('embed_bias', D), ('time_bias_one', D), ('time_bias_two', D), ('cond_bias', 10 * D), ('query_bias', D), ('value_bias', D), ('out_bias', D), ('fc1_bias', FF), ('fc2_bias', D), ('final_bias', 32), ('embed_weight', 16 * D), ('final_weight', 32 * D), ('rel_bias', H * REL)]
    places = {}
    offset = 0
    for entry_name, length in entries:
        places[entry_name] = (offset, length)
        offset = offset + length
    return places

def product(left, right):
    return jnp.matmul(left, right, precision=highest)

def patchify(field):
    images, channels = (field.shape[0], field.shape[1])
    shaped = field.reshape(images, channels, GRID, 2, GRID, 2)
    return shaped.transpose(0, 2, 4, 1, 3, 5).reshape(images, GRID * GRID, channels * 4)

def frequencies(moments_in):
    half_freq = FREQ // 2
    omegas = jnp.exp(-math.log(10000.0) * jnp.arange(half_freq, dtype=jnp.float32) / half_freq)
    angles = moments_in[:, None] * omegas[None, :]
    return jnp.concatenate([jnp.cos(angles), jnp.sin(angles)], 1)

def position_table():
    quarter = D // 4
    omegas = 1.0 / 10000.0 ** (jnp.arange(quarter, dtype=jnp.float32) / quarter)
    coords = jnp.arange(GRID, dtype=jnp.float32)
    row_angle = jnp.repeat(coords, GRID)[:, None] * omegas[None, :]
    col_angle = jnp.tile(coords, GRID)[:, None] * omegas[None, :]
    return jnp.concatenate([jnp.sin(row_angle), jnp.cos(row_angle), jnp.sin(col_angle), jnp.cos(col_angle)], 1)

def relative_bias(rel_table):
    coords = jnp.arange(GRID)
    shifts = coords[:, None] - coords[None, :] + GRID - 1
    along_rows = rel_table[:, shifts]
    along_cols = rel_table[:, 2 * GRID - 1 + shifts]
    combined = along_rows[:, :, None, :, None] + along_cols[:, None, :, None, :]
    return combined.reshape(H, TOKS, TOKS)

def layernorm(values):
    center = values - lax.optimization_barrier(jnp.mean(values, -1, keepdims=True))
    return center * lax.rsqrt(lax.optimization_barrier(jnp.mean(center * center, -1, keepdims=True)) + norm_eps)

def block_loss(params, block_latent, block_noise, block_times, block_label, block_drop, block_bucket, block_valid):
    joined, mixback, expand, narrow, timeone, timetwo, modulator, classes, smalls = params
    places = layout()

    def small_piece(key_name):
        begin_at, length = places[key_name]
        return smalls[begin_at:begin_at + length]
    images = block_latent.shape[0]
    time_frac = (block_times.astype(jnp.float32) + 1.0) / 1000.0
    alpha_scale = jnp.cos(0.5 * math.pi * time_frac)[:, None, None]
    sigma_scale = jnp.sin(0.5 * math.pi * time_frac)[:, None, None]
    noisy_patch = patchify(alpha_scale * block_latent + sigma_scale * block_noise)
    target = patchify(jnp.concatenate([alpha_scale * block_noise - sigma_scale * block_latent, block_noise], 1))
    bucket_width = float(1000 // NB)
    bucket_time = block_bucket.astype(jnp.float32) * bucket_width + 0.5 * bucket_width
    rows_in = low(frequencies(jnp.concatenate([block_times.astype(jnp.float32), bucket_time])))
    hidden_time = low_back(product(rows_in, low(timeone)) + small_piece('time_bias_one'))
    time_embed = low_back(product(low(jax.nn.silu(hidden_time)), low(timetwo).T) + small_piece('time_bias_two'))
    class_index = jnp.where(block_drop > 0, NCLS, block_label)
    label_rows = jnp.concatenate([low(classes)[class_index], jnp.zeros((images, D), jnp.float32)], 0)
    condition = time_embed + label_rows
    mods_all = low_back(product(low(jax.nn.silu(condition)), low(modulator)) + small_piece('cond_bias'))
    modulation = jnp.concatenate([mods_all[:images, :8 * D], mods_all[images:, 8 * D:]], 1)

    def column_block(index_col):
        return modulation[:, None, index_col * D:(index_col + 1) * D]
    embed_weight = low(small_piece('embed_weight').reshape(16, D))
    stream_zero = product(low(noisy_patch), embed_weight) + small_piece('embed_bias') + position_table()
    first_in = low(layernorm(stream_zero) * (1.0 + column_block(1)) + column_block(0))
    joined_out = product(first_in, low(joined)).reshape(images, TOKS, H, 3, HD)
    query_time = column_block(8).reshape(images, 1, H, HD)
    value_time = column_block(9).reshape(images, 1, H, HD)
    query_rows = low_back(low(joined_out[:, :, :, 0] + small_piece('query_bias').reshape(H, HD) + query_time))
    key_rows = low_back(low(joined_out[:, :, :, 1]))
    value_rows = low_back(low(joined_out[:, :, :, 2] + small_piece('value_bias').reshape(H, HD) + value_time))
    scores = low_back(jnp.einsum('nthe,nshe->nhts', query_rows, key_rows, precision=highest) / math.sqrt(HD) + relative_bias(small_piece('rel_bias').reshape(H, REL)))
    attention = low(jax.nn.softmax(scores, -1))
    mixed_heads = low_back(low(jnp.einsum('nhts,nshe->nthe', attention, value_rows, precision=highest))).reshape(images, TOKS, D)
    branch = low_back(product(mixed_heads, low(mixback).T) + small_piece('out_bias'))
    stream_one = stream_zero + column_block(2) * branch
    second_in = low(layernorm(stream_one) * (1.0 + column_block(4)) + column_block(3))
    hidden = low_back(product(second_in, low(expand)) + small_piece('fc1_bias'))
    active = low(jax.nn.gelu(hidden, approximate=True))
    branch_two = low_back(product(active, low(narrow).T) + small_piece('fc2_bias'))
    stream_two = stream_one + column_block(5) * branch_two
    final_in = low(layernorm(stream_two) * (1.0 + column_block(7)) + column_block(6))
    output = low_back(product(final_in, low(small_piece('final_weight').reshape(D, 32))) + small_piece('final_bias'))
    residual_error = output - target
    return jnp.sum(block_valid[:, None] * lax.optimization_barrier(jnp.mean(residual_error * residual_error, -1)))

def adamw_update(master, moment, second, gradient):
    first_new = beta_one * moment + (1.0 - beta_one) * gradient
    square_new = beta_two * second + (1.0 - beta_two) * gradient * gradient
    first_hat = first_new / (1.0 - beta_one ** STEP)
    square_hat = square_new / (1.0 - beta_two ** STEP)
    master_new = master - learn_rate * (first_hat / (jnp.sqrt(square_hat) + adam_eps) + weight_decay * master)
    return (first_new, square_new, master_new)

def reference(latents, noises, timesteps, labels, dropped, buckets, counts, joined_weight, joined_moment, joined_second, mixback_weight, mixback_moment, mixback_second, expand_weight, expand_moment, expand_second, narrow_weight, narrow_moment, narrow_second, timeone_weight, timeone_moment, timeone_second, timetwo_weight, timetwo_moment, timetwo_second, modulator_weight, modulator_moment, modulator_second, classes_weight, classes_moment, classes_second, smalls_weight, smalls_moment, smalls_second):
    masters = (joined_weight, mixback_weight, expand_weight, narrow_weight, timeone_weight, timetwo_weight, modulator_weight, classes_weight, smalls_weight)
    moments = (joined_moment, mixback_moment, expand_moment, narrow_moment, timeone_moment, timetwo_moment, modulator_moment, classes_moment, smalls_moment)
    seconds = (joined_second, mixback_second, expand_second, narrow_second, timeone_second, timetwo_second, modulator_second, classes_second, smalls_second)
    slots = jnp.arange(IMAGES) % IMG_GRP
    valid_flags = (slots >= IMG_GRP - jnp.repeat(counts, IMG_GRP)).astype(jnp.float32)
    image_bucket = jnp.repeat(buckets, IMG_GRP)
    per_block = math.gcd(IMAGES, max(1, 4096 // TOKS))
    blocks = IMAGES // per_block

    def split(array):
        return array.reshape((blocks, per_block) + array.shape[1:])
    block_data = tuple((split(member) for member in (latents, noises, timesteps, labels, dropped, image_bucket, valid_flags)))

    def accumulate(carry, data_now):
        loss_total, grad_total = carry
        loss_block, pullback = jax.vjp(lambda params: block_loss(params, *data_now), masters)
        grad_block, = pullback(jnp.ones((), jnp.float32))
        return ((loss_total + loss_block, jax.tree.map(jnp.add, grad_total, grad_block)), None)
    start_grads = jax.tree.map(jnp.zeros_like, masters)
    (loss_sum, grad_sums), _ = lax.scan(accumulate, (jnp.zeros((), jnp.float32), start_grads), block_data)
    token_count = jnp.sum(counts).astype(jnp.float32) * TOKS
    gradients = [member / token_count for member in grad_sums]
    grad_norm = jnp.sqrt(sum((jnp.sum(member * member) for member in gradients)))
    factor = jnp.minimum(1.0, clip_level / grad_norm)
    updates = [adamw_update(masters[place], moments[place], seconds[place], gradients[place] * factor) for place in range(9)]
    return (loss_sum, token_count, grad_norm, updates[0][0], updates[0][1], updates[0][2], updates[1][0], updates[1][1], updates[1][2], updates[2][0], updates[2][1], updates[2][2], updates[3][0], updates[3][1], updates[3][2], updates[4][0], updates[4][1], updates[4][2], updates[5][0], updates[5][1], updates[5][2], updates[6][0], updates[6][1], updates[6][2], updates[7][0], updates[7][1], updates[7][2], updates[8][0], updates[8][1], updates[8][2])
```

```python
from functools import partial
import math

import jax
import jax.numpy as jnp
from jax import lax
from jax.experimental import pallas as pl
from jax.experimental.pallas import tpu as pltpu
from jax.sharding import Mesh
from jax.sharding import PartitionSpec as P

D = 1152
H = 16
HD = 72
FF = 4608
FREQ = 256
NCLS = 1000
GRID = 16
NB = 20
STEP = 10
TOKS = 256
REL = 62


norm_eps = 1e-06
beta_one = 0.9
beta_two = 0.999
learn_rate = 0.04
weight_decay = 0.01
adam_eps = 1e-12
clip_level = 0.001
highest = lax.Precision.HIGHEST


def layout():
    entries = [
        ("embed_bias", D),
        ("time_bias_one", D),
        ("time_bias_two", D),
        ("cond_bias", 10 * D),
        ("query_bias", D),
        ("value_bias", D),
        ("out_bias", D),
        ("fc1_bias", FF),
        ("fc2_bias", D),
        ("final_bias", 32),
        ("embed_weight", 16 * D),
        ("final_weight", 32 * D),
        ("rel_bias", H * REL),
    ]
    places = {}
    offset = 0
    for entry_name, length in entries:
        places[entry_name] = (offset, length)
        offset = offset + length
    return places


def patchify(field):
    images, channels = (field.shape[0], field.shape[1])
    shaped = field.reshape(images, channels, GRID, 2, GRID, 2)
    return shaped.transpose(0, 2, 4, 1, 3, 5).reshape(images, GRID * GRID, channels * 4)


def frequencies(moments_in):
    half_freq = FREQ // 2
    omegas = jnp.exp(-math.log(10000.0) * jnp.arange(half_freq, dtype=jnp.float32) / half_freq)
    angles = moments_in[:, None] * omegas[None, :]
    return jnp.concatenate([jnp.cos(angles), jnp.sin(angles)], 1)


def position_table():
    quarter = D // 4
    omegas = 1.0 / 10000.0 ** (jnp.arange(quarter, dtype=jnp.float32) / quarter)
    coords = jnp.arange(GRID, dtype=jnp.float32)
    row_angle = jnp.repeat(coords, GRID)[:, None] * omegas[None, :]
    col_angle = jnp.tile(coords, GRID)[:, None] * omegas[None, :]
    return jnp.concatenate(
        [jnp.sin(row_angle), jnp.cos(row_angle), jnp.sin(col_angle), jnp.cos(col_angle)], 1
    )


def offset_table():
    coords = jnp.arange(GRID)
    shifts = coords[:, None] - coords[None, :] + GRID - 1
    return (
        (shifts[None, :, :] == jnp.arange(2 * GRID - 1)[:, None, None])
        .astype(jnp.float32)
        .reshape(2 * GRID - 1, GRID * GRID)
    )


def layernorm_parts(values):
    center = values - jnp.mean(values, -1, keepdims=True)
    inverse = lax.rsqrt(jnp.mean(center * center, -1, keepdims=True) + norm_eps)
    return (center * inverse, inverse)


def layernorm_back(normed, inverse, gradient):
    return (
        gradient
        - jnp.mean(gradient, -1, keepdims=True)
        - normed * jnp.mean(gradient * normed, -1, keepdims=True)
    ) * inverse


def column_of(modulation, index_col):
    return modulation[:, None, index_col * D : (index_col + 1) * D]


SCALE = 1.0 / math.sqrt(HD)
JOIN = 3 * HD


def dot_nn(left, right):
    return jnp.dot(left, right, preferred_element_type=jnp.float32)


def dot_nt(left, right):
    return lax.dot_general(
        left, right, (((1,), (1,)), ((), ())), preferred_element_type=jnp.float32
    )


def dot_tn(left, right):
    return lax.dot_general(
        left, right, (((0,), (0,)), ((), ())), preferred_element_type=jnp.float32
    )


def attention_forward_kernel(joined_ref, table_ref, spots_ref, mixed_ref, total_ref):
    for head in range(H):
        base = head * JOIN
        query = joined_ref[0, :, base : base + HD]
        keys = joined_ref[0, :, base + HD : base + 2 * HD]
        values = joined_ref[0, :, base + 2 * HD : base + 3 * HD]
        scores = (dot_nt(keys, query) + dot_nt(spots_ref[...], table_ref[head])) * SCALE
        largest = jnp.max(scores, 0, keepdims=True)
        grown = jnp.exp(scores - largest)
        total = jnp.sum(grown, 0, keepdims=True)
        prob = (grown * (1.0 / total)).astype(jnp.bfloat16)
        mixed_ref[0, :, head * HD : (head + 1) * HD] = dot_tn(prob, values).astype(jnp.bfloat16)
        total_ref[0, head : head + 1, :] = largest + jnp.log(total)


def attention_forward(joined_rows, table, spots):
    images = joined_rows.shape[0]
    return pl.pallas_call(
        attention_forward_kernel,
        grid=(images,),
        in_specs=[
            pl.BlockSpec((1, TOKS, H * JOIN), lambda i: (i, 0, 0)),
            pl.BlockSpec(table.shape, lambda i: (0, 0, 0)),
            pl.BlockSpec(spots.shape, lambda i: (0, 0)),
        ],
        out_specs=[
            pl.BlockSpec((1, TOKS, D), lambda i: (i, 0, 0)),
            pl.BlockSpec((1, H, TOKS), lambda i: (i, 0, 0)),
        ],
        out_shape=[
            jax.ShapeDtypeStruct((images, TOKS, D), jnp.bfloat16),
            jax.ShapeDtypeStruct((images, H, TOKS), jnp.float32),
        ],
        cost_estimate=pl.CostEstimate(
            flops=images * H * 4 * TOKS * TOKS * 128,
            transcendentals=images * H * TOKS * TOKS,
            bytes_accessed=images * TOKS * D * 8,
        ),
        compiler_params=pltpu.CompilerParams(vmem_limit_bytes=48 * 1024 * 1024),
        name="attention_forward",
    )(joined_rows, table, spots)


def attention_backward_kernel(
    joined_ref, total_ref, mixed_grad_ref, table_ref, spots_ref, grad_ref, column_ref, shift_ref
):
    @pl.when(pl.program_id(0) == 0)
    def start():
        shift_ref[...] = jnp.zeros_like(shift_ref)

    for head in range(H):
        base = head * JOIN
        query = joined_ref[0, :, base : base + HD]
        keys = joined_ref[0, :, base + HD : base + 2 * HD]
        values = joined_ref[0, :, base + 2 * HD : base + 3 * HD]
        mixed_grad = mixed_grad_ref[0, :, head * HD : (head + 1) * HD]
        scores = (dot_nt(keys, query) + dot_nt(spots_ref[...], table_ref[head])) * SCALE
        exact = jnp.exp(scores - total_ref[0, head : head + 1, :])
        value_grad = dot_nn(exact.astype(jnp.bfloat16), mixed_grad)
        prob_grad = dot_nt(values, mixed_grad)
        shared = jnp.sum(exact * prob_grad, 0, keepdims=True)
        score_grad = (exact * (prob_grad - shared)).astype(jnp.bfloat16)
        key_grad = dot_nn(score_grad, query) * SCALE
        wide = jnp.concatenate([keys, spots_ref[:, : 2 * GRID]], 1)
        query_wide = dot_tn(score_grad, wide)
        shift_ref[head] += query_wide
        grad_ref[0, :, base : base + HD] = (query_wide[:, :HD] * SCALE).astype(jnp.bfloat16)
        grad_ref[0, :, base + HD : base + 2 * HD] = key_grad.astype(jnp.bfloat16)
        grad_ref[0, :, base + 2 * HD : base + 3 * HD] = value_grad.astype(jnp.bfloat16)
    column_ref[0] = dot_nn(jnp.ones((8, TOKS), jnp.bfloat16), grad_ref[0])


def attention_backward(joined_rows, total, mixed_grad, table, spots):
    images = joined_rows.shape[0]
    wide = HD + 2 * GRID
    return pl.pallas_call(
        attention_backward_kernel,
        grid=(images,),
        in_specs=[
            pl.BlockSpec((1, TOKS, H * JOIN), lambda i: (i, 0, 0)),
            pl.BlockSpec((1, H, TOKS), lambda i: (i, 0, 0)),
            pl.BlockSpec((1, TOKS, D), lambda i: (i, 0, 0)),
            pl.BlockSpec(table.shape, lambda i: (0, 0, 0)),
            pl.BlockSpec(spots.shape, lambda i: (0, 0)),
        ],
        out_specs=[
            pl.BlockSpec((1, TOKS, H * JOIN), lambda i: (i, 0, 0)),
            pl.BlockSpec((1, 8, H * JOIN), lambda i: (i, 0, 0)),
            pl.BlockSpec((H, TOKS, wide), lambda i: (0, 0, 0)),
        ],
        out_shape=[
            jax.ShapeDtypeStruct((images, TOKS, H * JOIN), jnp.bfloat16),
            jax.ShapeDtypeStruct((images, 8, H * JOIN), jnp.float32),
            jax.ShapeDtypeStruct((H, TOKS, wide), jnp.float32),
        ],
        cost_estimate=pl.CostEstimate(
            flops=images * H * 10 * TOKS * TOKS * 128,
            transcendentals=images * H * TOKS * TOKS,
            bytes_accessed=images * TOKS * D * 16,
        ),
        compiler_params=pltpu.CompilerParams(vmem_limit_bytes=48 * 1024 * 1024),
        name="attention_backward",
    )(joined_rows, total, mixed_grad, table, spots)


def relative_tables(rel_table):
    rows = offset_table()
    span = 2 * GRID - 1
    along_rows = jnp.dot(rel_table[:, :span], rows, precision=highest).reshape(H, GRID, 1, GRID)
    along_cols = jnp.dot(rel_table[:, span:], rows, precision=highest).reshape(H, 1, GRID, GRID)
    full = (H, GRID, GRID, GRID)
    table = jnp.concatenate(
        [jnp.broadcast_to(along_rows, full), jnp.broadcast_to(along_cols, full)], 3
    ).reshape(H, TOKS, 2 * GRID) * math.sqrt(HD)
    upper = table.astype(jnp.bfloat16)
    lower = (table - upper.astype(jnp.float32)).astype(jnp.bfloat16)
    return jnp.concatenate([upper, lower], 2)


def spot_table():
    places = jnp.arange(TOKS)
    rows = (places[:, None] // GRID == jnp.arange(GRID)[None, :]).astype(jnp.bfloat16)
    cols = (places[:, None] % GRID == jnp.arange(GRID)[None, :]).astype(jnp.bfloat16)
    return jnp.concatenate([rows, cols, rows, cols], 1)


def relative_gradient(shifts):
    rows = offset_table()
    row_part = jnp.sum(shifts[:, :, :GRID].reshape(H, GRID, GRID, GRID), 2)
    col_part = jnp.sum(shifts[:, :, GRID:].reshape(H, GRID, GRID, GRID), 1)
    return jnp.concatenate(
        [
            jnp.dot(row_part.reshape(H, TOKS), rows.T, precision=highest),
            jnp.dot(col_part.reshape(H, TOKS), rows.T, precision=highest),
        ],
        1,
    ).reshape(H * REL)


def small_gather(values, axes, count):
    spread = jnp.broadcast_to(values[None], (count,) + values.shape)
    return lax.all_to_all(spread, axes, 0, 0, tiled=True)


def pick(values, index, dim):
    return lax.dynamic_index_in_dim(values, index, dim, keepdims=False)


def reduce_step(values, dim, axis, size, index):
    if size == 2:
        received = lax.ppermute(pick(values, 1 - index, dim), axis, [(0, 1), (1, 0)])
        return pick(values, index, dim).astype(jnp.float32) + received.astype(jnp.float32)
    moved = jnp.moveaxis(values, dim, 0)
    received = lax.all_to_all(moved, axis, 0, 0, tiled=True)
    return jnp.sum(received.astype(jnp.float32), 0)


def reduce_weight(gradient, sizes, places):
    da, db, ny = (sizes[key] for key in ("da", "db", "y"))
    rows = gradient.shape[0] // (da * db)
    width = gradient.shape[1] // (ny * 2)
    blocks = gradient.reshape(da, db, rows, ny, 2, width)
    kept = reduce_step(blocks, 4, "c", 2, places["c"]).astype(jnp.bfloat16)
    half = da // 2
    first = reduce_step(kept[:half], 3, "y", ny, places["y"]).astype(jnp.bfloat16)
    second = reduce_step(kept[half:], 1, "db", db, places["db"]).astype(jnp.bfloat16)
    first = reduce_step(first, 1, "db", db, places["db"]).astype(jnp.bfloat16)
    second = reduce_step(second, 2, "y", ny, places["y"]).astype(jnp.bfloat16)
    received = lax.all_to_all(jnp.concatenate([first, second], 0), "da", 0, 0, tiled=True)
    return jnp.sum(received.astype(jnp.float32), 0)


def whole_weight(gathered, groups, parts, begin, width):
    block = gathered.reshape(groups, parts, gathered.shape[1], gathered.shape[2])
    block = block[:, :, :, begin : begin + width].transpose(0, 2, 1, 3)
    return block.reshape(groups * gathered.shape[1], parts * width)


def adamw_update(master, moment, second, gradient):
    first_new = beta_one * moment + (1.0 - beta_one) * gradient
    square_new = beta_two * second + (1.0 - beta_two) * gradient * gradient
    first_hat = first_new / (1.0 - beta_one**STEP)
    square_hat = square_new / (1.0 - beta_two**STEP)
    master_new = master - learn_rate * (
        first_hat / (jnp.sqrt(square_hat) + adam_eps) + weight_decay * master
    )
    return (first_new, square_new, master_new)


TOKEN_SMALLS = (
    "embed_bias",
    "query_bias",
    "value_bias",
    "out_bias",
    "fc1_bias",
    "fc2_bias",
    "final_bias",
    "embed_weight",
    "final_weight",
    "rel_bias",
)


def per_device(
    sizes,
    latents,
    noises,
    timesteps,
    labels,
    dropped,
    buckets,
    counts,
    *state,
):
    masters, moments, seconds = (state[0::3], state[1::3], state[2::3])
    (
        joined_weight,
        mixback_weight,
        expand_weight,
        narrow_weight,
        timeone_weight,
        timetwo_weight,
        modulator_weight,
        classes_weight,
        smalls_weight,
    ) = masters
    da, db, ny, nc = (sizes[key] for key in ("da", "db", "y", "c"))
    dp, mp = (da * db, ny * nc)
    dp_axes, mp_axes = (("da", "db"), ("y", "c"))
    all_axes = dp_axes + mp_axes
    places_now = {key: lax.axis_index(key) for key in ("da", "db", "y", "c")}
    dp_index = places_now["da"] * db + places_now["db"]
    mp_index = places_now["y"] * nc + places_now["c"]
    places = layout()
    zero_index = jnp.zeros((), jnp.int32)

    def small_piece(key_name):
        begin_at, length = places[key_name]
        return smalls_weight[begin_at : begin_at + length]

    own_images = latents.shape[0]
    group_size = timesteps.shape[0]
    images_all = dp * group_size
    row_width = timetwo_weight.shape[0]
    width_mp = timetwo_weight.shape[1]
    mod_width = modulator_weight.shape[1]

    gathered_one = lax.all_gather(
        jnp.concatenate([joined_weight, mixback_weight], 1).astype(jnp.bfloat16), all_axes
    )
    gathered_two = lax.all_gather(
        jnp.concatenate([expand_weight, narrow_weight], 1).astype(jnp.bfloat16), all_axes
    )
    joined = whole_weight(gathered_one, dp, mp, 0, joined_weight.shape[1])
    mixback = whole_weight(gathered_one, dp, mp, joined_weight.shape[1], mixback_weight.shape[1])
    expand = whole_weight(gathered_two, dp, mp, 0, expand_weight.shape[1])
    narrow = whole_weight(gathered_two, dp, mp, expand_weight.shape[1], narrow_weight.shape[1])

    facts = small_gather(
        jnp.concatenate([timesteps, labels, dropped, buckets, counts]).astype(jnp.float32),
        dp_axes,
        dp,
    )
    times_all = facts[:, :group_size].reshape(images_all)
    labels_all = facts[:, group_size : 2 * group_size].reshape(images_all)
    dropped_all = facts[:, 2 * group_size : 3 * group_size].reshape(images_all)
    buckets_all = facts[:, 3 * group_size]
    token_count = jnp.sum(facts[:, 3 * group_size + 1]) * TOKS
    time_first = small_gather(timeone_weight.astype(jnp.bfloat16), dp_axes, dp).reshape(
        FREQ, width_mp
    )
    time_second_all = small_gather(timetwo_weight.astype(jnp.bfloat16), dp_axes, dp).reshape(
        D, width_mp
    )
    bucket_width = float(1000 // NB)
    rows_in = frequencies(
        jnp.concatenate([times_all, buckets_all * bucket_width + 0.5 * bucket_width])
    ).astype(jnp.bfloat16)
    hidden_time = jnp.dot(
        rows_in, time_first, preferred_element_type=jnp.float32
    ) + lax.dynamic_slice_in_dim(small_piece("time_bias_one"), mp_index * width_mp, width_mp)
    hidden_act = jax.nn.silu(hidden_time).astype(jnp.bfloat16)
    embed_part = dot_nt(hidden_act, timetwo_weight.astype(jnp.bfloat16))
    class_index = jnp.where(dropped_all > 0, float(NCLS), labels_all)
    onehot = (class_index[:, None] == jnp.arange(NCLS + 1, dtype=jnp.float32)[None, :]).astype(
        jnp.bfloat16
    )
    label_cols = jnp.dot(
        onehot, classes_weight.astype(jnp.bfloat16), preferred_element_type=jnp.float32
    )
    column_at = dp_index * row_width
    owner = column_at // width_mp
    label_part = lax.dynamic_slice_in_dim(label_cols, column_at - owner * width_mp, row_width, 1)
    label_part = jnp.where(mp_index == owner, label_part, 0.0)
    condition = jnp.sum(
        small_gather(
            jnp.concatenate([embed_part[:images_all] + label_part, embed_part[images_all:]], 0),
            mp_axes,
            mp,
        ),
        0,
    ) + lax.dynamic_slice_in_dim(small_piece("time_bias_two"), column_at, row_width)
    cond_act = jax.nn.silu(condition).astype(jnp.bfloat16)
    modulator = modulator_weight.astype(jnp.bfloat16)
    global_cols = mp_index * mod_width + jnp.arange(mod_width)
    mods_part = jnp.dot(cond_act, modulator, preferred_element_type=jnp.float32)
    outgoing = jnp.where(
        global_cols < 8 * D,
        mods_part[:images_all].reshape(dp, group_size, mod_width),
        mods_part[images_all:].reshape(dp, 1, mod_width),
    ).astype(jnp.bfloat16)
    incoming = lax.all_to_all(
        outgoing.reshape(dp * mp, own_images, mod_width), all_axes, 0, 0, tiled=True
    ).reshape(dp, mp, own_images, mod_width)
    modulation = jnp.sum(incoming.astype(jnp.float32), 0).transpose(1, 0, 2).reshape(
        own_images, 10 * D
    ) + small_piece("cond_bias")

    own_times = lax.dynamic_slice_in_dim(timesteps, mp_index * own_images, own_images)
    slot_index = mp_index * own_images + jnp.arange(own_images)
    valid_flags = (slot_index >= group_size - counts[0]).astype(jnp.float32)
    time_frac = (own_times.astype(jnp.float32) + 1.0) / 1000.0
    alpha_scale = jnp.cos(0.5 * math.pi * time_frac)[:, None, None]
    sigma_scale = jnp.sin(0.5 * math.pi * time_frac)[:, None, None]
    noisy_all = patchify(alpha_scale * latents + sigma_scale * noises)
    target = patchify(jnp.concatenate([alpha_scale * noises - sigma_scale * latents, noises], 1))
    embed_weight = small_piece("embed_weight").reshape(16, D)
    final_weight = small_piece("final_weight").reshape(D, 32)
    table = relative_tables(small_piece("rel_bias").reshape(H, REL))
    spots = spot_table()
    images = own_images
    rows_all = images * TOKS

    embed_in = noisy_all.astype(jnp.bfloat16)
    stream_zero = (
        jnp.einsum(
            "ntc,cd->ntd",
            embed_in,
            embed_weight.astype(jnp.bfloat16),
            preferred_element_type=jnp.float32,
        )
        + small_piece("embed_bias")
        + position_table()
    )
    normed_a, inverse_a = layernorm_parts(stream_zero)
    first_in = (
        (normed_a * (1.0 + column_of(modulation, 1)) + column_of(modulation, 0))
        .astype(jnp.bfloat16)
        .reshape(rows_all, D)
    )
    added = jnp.stack(
        [
            (small_piece("query_bias") + modulation[:, 8 * D : 9 * D]).reshape(images, H, HD),
            jnp.zeros((images, H, HD), jnp.float32),
            (small_piece("value_bias") + modulation[:, 9 * D :]).reshape(images, H, HD),
        ],
        2,
    ).reshape(images, 1, 3 * D)
    joined_rows = (
        dot_nn(first_in, joined).reshape(images, TOKS, 3 * D) + added
    ).astype(jnp.bfloat16)
    mixed_heads, log_total = attention_forward(joined_rows, table, spots)
    mixed_heads = mixed_heads.reshape(rows_all, D)
    branch = (dot_nt(mixed_heads, mixback) + small_piece("out_bias")).reshape(images, TOKS, D)
    stream_one = stream_zero + column_of(modulation, 2) * branch
    normed_b, inverse_b = layernorm_parts(stream_one)
    second_in = (
        (normed_b * (1.0 + column_of(modulation, 4)) + column_of(modulation, 3))
        .astype(jnp.bfloat16)
        .reshape(rows_all, D)
    )
    hidden = dot_nn(second_in, expand) + small_piece("fc1_bias")
    active = jax.nn.gelu(hidden, approximate=True).astype(jnp.bfloat16)
    branch_two = (dot_nt(active, narrow) + small_piece("fc2_bias")).reshape(images, TOKS, D)
    stream_two = stream_one + column_of(modulation, 5) * branch_two
    normed_c, inverse_c = layernorm_parts(stream_two)
    final_in = (
        (normed_c * (1.0 + column_of(modulation, 7)) + column_of(modulation, 6))
        .astype(jnp.bfloat16)
        .reshape(rows_all, D)
    )
    output = dot_nn(final_in, final_weight.astype(jnp.bfloat16)) + small_piece("final_bias")

    residual_error = output - target.reshape(rows_all, 32)
    valid_rows = jnp.repeat(valid_flags, TOKS)[:, None]
    loss_part = jnp.sum(valid_rows * jnp.mean(residual_error * residual_error, -1, keepdims=True))
    grad_out = (valid_rows * 2.0 * residual_error / 32.0).astype(jnp.bfloat16)
    grad_small = {}
    grad_small["final_bias"] = jnp.sum(grad_out.astype(jnp.float32), 0)
    grad_small["final_weight"] = dot_tn(final_in, grad_out).reshape(32 * D)
    grad_final = dot_nt(grad_out, final_weight.astype(jnp.bfloat16)).reshape(images, TOKS, D)

    def modulate_back(gradient, normed, inverse, scale_col):
        scaled = gradient * (1.0 + column_of(modulation, scale_col))
        return (
            layernorm_back(normed, inverse, scaled),
            jnp.sum(gradient, 1),
            jnp.sum(gradient * normed, 1),
        )

    grad_two, shift_c, scale_c = modulate_back(grad_final, normed_c, inverse_c, 7)
    grad_branch_two = (
        (column_of(modulation, 5) * grad_two).astype(jnp.bfloat16).reshape(rows_all, D)
    )
    gate_two = jnp.sum(grad_two * branch_two, 1)
    grad_small["fc2_bias"] = jnp.sum(grad_branch_two.astype(jnp.float32), 0)
    narrow_grad = reduce_weight(
        dot_tn(grad_branch_two, active).astype(jnp.bfloat16), sizes, places_now
    )
    grad_active = dot_nn(grad_branch_two, narrow)
    _, pullback = jax.vjp(partial(jax.nn.gelu, approximate=True), hidden)
    grad_hidden = pullback(grad_active)[0].astype(jnp.bfloat16)
    grad_small["fc1_bias"] = jnp.sum(grad_hidden.astype(jnp.float32), 0)
    expand_grad = reduce_weight(
        dot_tn(second_in, grad_hidden).astype(jnp.bfloat16), sizes, places_now
    )
    grad_second = dot_nt(grad_hidden, expand).reshape(images, TOKS, D)
    grad_one_part, shift_b, scale_b = modulate_back(grad_second, normed_b, inverse_b, 4)
    grad_one = grad_two + grad_one_part
    grad_branch = (column_of(modulation, 2) * grad_one).astype(jnp.bfloat16).reshape(rows_all, D)
    gate_one = jnp.sum(grad_one * branch, 1)
    grad_small["out_bias"] = jnp.sum(grad_branch.astype(jnp.float32), 0)
    mixback_grad = reduce_weight(
        dot_tn(grad_branch, mixed_heads).astype(jnp.bfloat16), sizes, places_now
    )
    grad_mixed = dot_nn(grad_branch, mixback).astype(jnp.bfloat16).reshape(images, TOKS, D)
    grad_joined, column_sums, shifts = attention_backward(
        joined_rows, log_total, grad_mixed, table, spots
    )
    grad_joined = grad_joined.reshape(rows_all, 3 * D)
    grad_small["rel_bias"] = relative_gradient(shifts[:, :, HD:])
    sums = column_sums[:, 0].reshape(images, H, 3, HD)
    time_query = sums[:, :, 0].reshape(images, D)
    time_value = sums[:, :, 2].reshape(images, D)
    grad_small["query_bias"] = jnp.sum(time_query, 0)
    grad_small["value_bias"] = jnp.sum(time_value, 0)
    grad_first = dot_nt(grad_joined, joined).reshape(images, TOKS, D)
    joined_grad = reduce_weight(
        dot_tn(first_in, grad_joined).astype(jnp.bfloat16), sizes, places_now
    )
    grad_zero_part, shift_a, scale_a = modulate_back(grad_first, normed_a, inverse_a, 1)
    grad_zero = grad_one + grad_zero_part
    grad_small["embed_bias"] = jnp.sum(grad_zero, (0, 1))
    grad_small["embed_weight"] = jnp.einsum(
        "ntc,ntd->cd", embed_in.astype(jnp.float32), grad_zero, precision=highest
    ).reshape(16 * D)

    mods_grads = jnp.concatenate(
        [
            shift_a,
            scale_a,
            gate_one,
            shift_b,
            scale_b,
            gate_two,
            shift_c,
            scale_c,
            time_query,
            time_value,
        ],
        1,
    ).astype(jnp.bfloat16)
    to_owners = mods_grads.reshape(own_images, mp, mod_width).transpose(1, 0, 2)
    returned = lax.all_to_all(
        jnp.broadcast_to(to_owners[None], (dp,) + to_owners.shape).reshape(
            dp * mp, own_images, mod_width
        ),
        all_axes,
        0,
        0,
        tiled=True,
    ).reshape(images_all, mod_width)
    is_image = (global_cols < 8 * D)[None, :]
    returned_wide = returned.astype(jnp.float32)
    cond_bias_grad = jnp.sum(returned_wide, 0)
    bucket_sums = jnp.where(
        is_image, 0.0, jnp.sum(returned_wide.reshape(dp, group_size, mod_width), 1)
    )

    def split_rows(image_rows, bucket_rows):
        upper = bucket_rows.astype(jnp.bfloat16)
        lower = (bucket_rows - upper.astype(jnp.float32)).astype(jnp.bfloat16)
        return jnp.concatenate([image_rows.astype(jnp.bfloat16), upper, lower], 0)

    def double_rows(rows):
        return jnp.concatenate([rows, rows[images_all:]], 0)

    grad_mod = split_rows(jnp.where(is_image, returned, jnp.zeros_like(returned)), bucket_sums)
    modulator_grad = dot_tn(double_rows(cond_act), grad_mod)
    cond_part = dot_nt(grad_mod, modulator)
    cond_part = jnp.concatenate(
        [cond_part[:images_all], cond_part[images_all : images_all + dp] + cond_part[images_all + dp :]],
        0,
    )
    grad_act = jnp.sum(small_gather(cond_part, mp_axes, mp), 0)
    _, pullback = jax.vjp(jax.nn.silu, condition)
    grad_cond_own = pullback(grad_act)[0]
    grad_embed_own = split_rows(grad_cond_own[:images_all], grad_cond_own[images_all:])
    timetwo_grad = dot_tn(grad_embed_own, double_rows(hidden_act))
    grad_cond = (
        small_gather(grad_cond_own, dp_axes, dp)
        .transpose(1, 0, 2)
        .reshape(images_all + dp, D)
    )
    grad_embed = split_rows(grad_cond[:images_all], grad_cond[images_all:])
    bias_two_grad = jnp.sum(grad_embed.astype(jnp.float32), 0)
    grad_hidden_act = dot_nn(grad_embed, time_second_all)
    grad_hidden_act = jnp.concatenate(
        [
            grad_hidden_act[:images_all],
            grad_hidden_act[images_all : images_all + dp] + grad_hidden_act[images_all + dp :],
        ],
        0,
    )
    _, pullback = jax.vjp(jax.nn.silu, hidden_time)
    grad_hidden_time = pullback(grad_hidden_act)[0]
    grad_hidden_time = split_rows(grad_hidden_time[:images_all], grad_hidden_time[images_all:])
    bias_one_grad = jnp.sum(grad_hidden_time.astype(jnp.float32), 0)
    rows_own = lax.dynamic_slice_in_dim(
        rows_in, dp_index * timeone_weight.shape[0], timeone_weight.shape[0], 1
    )
    timeone_grad = dot_tn(double_rows(rows_own), grad_hidden_time)
    label_rows = lax.dynamic_slice_in_dim(grad_cond[:images_all], mp_index * width_mp, width_mp, 1)
    label_upper = label_rows.astype(jnp.bfloat16)
    label_lower = (label_rows - label_upper.astype(jnp.float32)).astype(jnp.bfloat16)
    class_raw = dot_tn(
        jnp.concatenate([onehot, onehot], 0), jnp.concatenate([label_upper, label_lower], 0)
    )

    vector = jnp.concatenate([grad_small[key_name] for key_name in TOKEN_SMALLS])
    slice_length = -(-vector.shape[0] // (dp * mp))
    padded = jnp.pad(vector, (0, slice_length * dp * mp - vector.shape[0]))
    slice_sum = jnp.sum(
        lax.all_to_all(padded.reshape(dp * mp, slice_length), all_axes, 0, 0, tiled=True), 0
    )
    mod_slice = -(-mod_width // dp)
    one_slice = -(-width_mp // dp)
    own_cond = lax.dynamic_slice_in_dim(
        jnp.pad(cond_bias_grad, (0, mod_slice * dp - mod_width)), dp_index * mod_slice, mod_slice
    )
    own_one = lax.dynamic_slice_in_dim(
        jnp.pad(bias_one_grad, (0, one_slice * dp - width_mp)), dp_index * one_slice, one_slice
    )
    own_two = lax.dynamic_slice_in_dim(bias_two_grad, column_at, row_width)

    owned = [
        member / token_count
        for member in (
            joined_grad,
            mixback_grad,
            expand_grad,
            narrow_grad,
            timeone_grad,
            timetwo_grad,
            modulator_grad,
        )
    ]
    class_grad = class_raw / token_count
    own_slices = jnp.concatenate([slice_sum, own_cond, own_one]) / token_count
    squares = sum((jnp.sum(member * member) for member in owned)) + jnp.sum(own_slices * own_slices)
    squares = squares + jnp.where(dp_index == 0, jnp.sum(class_grad * class_grad), 0.0)
    own_two = own_two / token_count
    squares = squares + jnp.where(mp_index == 0, jnp.sum(own_two * own_two), 0.0)
    final = small_gather(
        jnp.concatenate([own_slices, squares[None], loss_part[None]]), all_axes, dp * mp
    )
    ends = slice_length + mod_slice + one_slice
    grad_norm = jnp.sqrt(jnp.sum(final[:, ends]))
    loss_sum = jnp.sum(final[:, ends + 1])
    factor = jnp.minimum(1.0, clip_level / grad_norm)
    token_smalls = final[:, :slice_length].reshape(dp * mp * slice_length)
    pieces = {"time_bias_two": bias_two_grad / token_count}
    pieces["cond_bias"] = (
        final[:, slice_length : slice_length + mod_slice]
        .reshape(dp, mp, mod_slice)
        .transpose(1, 0, 2)
        .reshape(mp, dp * mod_slice)[:, :mod_width]
        .reshape(10 * D)
    )
    pieces["time_bias_one"] = (
        final[:, slice_length + mod_slice : ends]
        .reshape(dp, mp, one_slice)
        .transpose(1, 0, 2)
        .reshape(mp, dp * one_slice)[:, :width_mp]
        .reshape(D)
    )
    offset = 0
    for key_name in TOKEN_SMALLS:
        length = places[key_name][1]
        pieces[key_name] = token_smalls[offset : offset + length]
        offset = offset + length
    small_grad = jnp.concatenate([pieces[key_name] for key_name in places])
    gradients = owned + [class_grad, small_grad]
    results = [loss_sum, token_count, grad_norm]
    for master, moment, second, gradient in zip(masters, moments, seconds, gradients):
        results.extend(adamw_update(master, moment, second, gradient * factor))
    return tuple(results)


def solution(mesh):
    dp, mp = (mesh.shape["dp"], mesh.shape["mp"])
    sizes = {"da": dp // 2, "db": 2, "y": mp // 2, "c": 2}
    inner = Mesh(
        mesh.devices.reshape(sizes["da"], sizes["db"], sizes["y"], sizes["c"]),
        ("da", "db", "y", "c"),
    )
    groups, parts = (("da", "db"), ("y", "c"))
    weight_specs = (P(groups, parts),) * 21 + (P(None, parts),) * 3 + (P(),) * 3
    in_specs = (P(groups + parts, None, None),) * 2 + (P(groups),) * 5 + weight_specs
    out_specs = (P(),) * 3 + weight_specs
    return jax.shard_map(
        partial(per_device, sizes),
        mesh=inner,
        in_specs=in_specs,
        out_specs=out_specs,
        check_vma=False,
    )
```

```python
from functools import partial
import math

import jax
import jax.numpy as jnp
from jax import lax
from jax.experimental import pallas as pl
from jax.experimental.pallas import tpu as pltpu
from jax.sharding import Mesh
from jax.sharding import PartitionSpec as P

D = 1152
H = 16
HD = 72
FF = 4608
FREQ = 256
NCLS = 1000
GRID = 16
NB = 20
STEP = 10
TOKS = 256
REL = 62


norm_eps = 1e-06
beta_one = 0.9
beta_two = 0.999
learn_rate = 0.04
weight_decay = 0.01
adam_eps = 1e-12
clip_level = 0.001
highest = lax.Precision.HIGHEST


def layout():
    entries = [
        ("embed_bias", D),
        ("time_bias_one", D),
        ("time_bias_two", D),
        ("cond_bias", 10 * D),
        ("query_bias", D),
        ("value_bias", D),
        ("out_bias", D),
        ("fc1_bias", FF),
        ("fc2_bias", D),
        ("final_bias", 32),
        ("embed_weight", 16 * D),
        ("final_weight", 32 * D),
        ("rel_bias", H * REL),
    ]
    places = {}
    offset = 0
    for entry_name, length in entries:
        places[entry_name] = (offset, length)
        offset = offset + length
    return places


def patchify(field):
    images, channels = (field.shape[0], field.shape[1])
    shaped = field.reshape(images, channels, GRID, 2, GRID, 2)
    return shaped.transpose(0, 2, 4, 1, 3, 5).reshape(images, GRID * GRID, channels * 4)


def frequencies(moments_in):
    half_freq = FREQ // 2
    omegas = jnp.exp(-math.log(10000.0) * jnp.arange(half_freq, dtype=jnp.float32) / half_freq)
    angles = moments_in[:, None] * omegas[None, :]
    return jnp.concatenate([jnp.cos(angles), jnp.sin(angles)], 1)


def position_table():
    quarter = D // 4
    omegas = 1.0 / 10000.0 ** (jnp.arange(quarter, dtype=jnp.float32) / quarter)
    coords = jnp.arange(GRID, dtype=jnp.float32)
    row_angle = jnp.repeat(coords, GRID)[:, None] * omegas[None, :]
    col_angle = jnp.tile(coords, GRID)[:, None] * omegas[None, :]
    return jnp.concatenate(
        [jnp.sin(row_angle), jnp.cos(row_angle), jnp.sin(col_angle), jnp.cos(col_angle)], 1
    )


def offset_table():
    coords = jnp.arange(GRID)
    shifts = coords[:, None] - coords[None, :] + GRID - 1
    return (
        (shifts[None, :, :] == jnp.arange(2 * GRID - 1)[:, None, None])
        .astype(jnp.float32)
        .reshape(2 * GRID - 1, GRID * GRID)
    )


def layernorm_parts(values):
    center = values - jnp.mean(values, -1, keepdims=True)
    inverse = lax.rsqrt(jnp.mean(center * center, -1, keepdims=True) + norm_eps)
    return (center * inverse, inverse)


def column_of(modulation, index_col):
    return modulation[:, None, index_col * D : (index_col + 1) * D]


BIG = 58 * 1024 * 1024
SCALE = 1.0 / math.sqrt(HD)
JOIN = 3 * HD
ROOT = math.sqrt(2.0 / math.pi)


def dot_nn(left, right):
    return jnp.dot(left, right, preferred_element_type=jnp.float32)


def dot_nt(left, right):
    return lax.dot_general(
        left, right, (((1,), (1,)), ((), ())), preferred_element_type=jnp.float32
    )


def dot_tn(left, right):
    return lax.dot_general(
        left, right, (((0,), (0,)), ((), ())), preferred_element_type=jnp.float32
    )


def params(*order):
    return pltpu.CompilerParams(
        dimension_semantics=order, vmem_limit_bytes=BIG
    )


def cost(flops, moved, exps=0):
    return pl.CostEstimate(flops=int(flops), bytes_accessed=int(moved), transcendentals=int(exps))


def block_of(weight_ref, width):
    block = weight_ref[:, 0, :, :width]
    return block.reshape(block.shape[0] * block.shape[1], width)


def weight_spec(weights, width, place):
    groups, _, rows, _ = weights.shape
    return pl.BlockSpec((groups, 1, rows, width), lambda m, i: (0, m, 0, place))


def norm_of(values):
    center = values - jnp.mean(values, -1, keepdims=True)
    inverse = lax.rsqrt(jnp.mean(center * center, -1, keepdims=True) + norm_eps)
    return center * inverse, inverse


def norm_back(normed, inverse, gradient):
    return (
        gradient
        - jnp.mean(gradient, -1, keepdims=True)
        - normed * jnp.mean(gradient * normed, -1, keepdims=True)
    ) * inverse


def total_rows(values):
    return jnp.sum(values, 0, keepdims=True)


def ordered(kernel, count, extra):
    def run(*refs):
        return kernel(*refs[:count], *refs[count + extra :])

    return run


def unread(others):
    return [pl.BlockSpec(memory_space=pl.ANY) for _ in others]


def hold(m, last, i):
    return jnp.where(m == last, i, 0)


def attention_forward_kernel(
    width, first_ref, weight_ref, added_ref, table_ref, spots_ref, joined_ref, mixed_ref, total_ref
):
    heads = width // JOIN
    rows = dot_nn(first_ref[0], block_of(weight_ref, width)) + added_ref[0, 0]
    joined_ref[0, 0] = rows.astype(jnp.bfloat16)
    for head in range(heads):
        base = head * JOIN
        query = joined_ref[0, 0, :, base : base + HD]
        keys = joined_ref[0, 0, :, base + HD : base + 2 * HD]
        values = joined_ref[0, 0, :, base + 2 * HD : base + 3 * HD]
        scores = (dot_nt(keys, query) + dot_nt(spots_ref[...], table_ref[head])) * SCALE
        largest = jnp.max(scores, 0, keepdims=True)
        grown = jnp.exp(scores - largest)
        total = jnp.sum(grown, 0, keepdims=True)
        prob = (grown * (1.0 / total)).astype(jnp.bfloat16)
        mixed_ref[0, 0, :, head * HD : (head + 1) * HD] = dot_tn(prob, values).astype(jnp.bfloat16)
        total_ref[0, 0, head : head + 1, :] = largest + jnp.log(total)


def attention_forward(first_in, weights, lanes, width, added, table, spots):
    images = first_in.shape[0]
    parts = weights.shape[1]
    heads = width // JOIN
    return pl.pallas_call(
        partial(attention_forward_kernel, width),
        grid=(parts, images),
        in_specs=[
            pl.BlockSpec((1, TOKS, D), lambda m, i: (i, 0, 0)),
            weight_spec(weights, lanes, 0),
            pl.BlockSpec((1, 1, 1, width), lambda m, i: (m, i, 0, 0)),
            pl.BlockSpec((heads, TOKS, 4 * GRID), lambda m, i: (m, 0, 0)),
            pl.BlockSpec((TOKS, 4 * GRID), lambda m, i: (0, 0)),
        ],
        out_specs=[
            pl.BlockSpec((1, 1, TOKS, width), lambda m, i: (m, i, 0, 0)),
            pl.BlockSpec((1, 1, TOKS, heads * HD), lambda m, i: (m, i, 0, 0)),
            pl.BlockSpec((1, 1, heads, TOKS), lambda m, i: (m, i, 0, 0)),
        ],
        out_shape=[
            jax.ShapeDtypeStruct((parts, images, TOKS, width), jnp.bfloat16),
            jax.ShapeDtypeStruct((parts, images, TOKS, heads * HD), jnp.bfloat16),
            jax.ShapeDtypeStruct((parts, images, heads, TOKS), jnp.float32),
        ],
        cost_estimate=cost(images * (2 * TOKS * D * 3 * D + H * 4 * TOKS * TOKS * 128), 3e7),
        compiler_params=params("arbitrary", "arbitrary"),
        name="attention_forward",
    )(first_in, weights, added, table, spots)


def attention_backward_kernel(
    branch_grad_ref,
    weight_ref,
    joined_ref,
    total_ref,
    table_ref,
    spots_ref,
    grad_ref,
    column_ref,
    shift_ref,
    mixed_grad_ref,
):
    heads = shift_ref.shape[0]

    @pl.when(pl.program_id(1) == 0)
    def start():
        shift_ref[...] = jnp.zeros_like(shift_ref)

    mixed_grad_ref[...] = dot_nn(
        branch_grad_ref[0], block_of(weight_ref, heads * HD)
    ).astype(jnp.bfloat16)
    for head in range(heads):
        base = head * JOIN
        query = joined_ref[0, 0, :, base : base + HD]
        keys = joined_ref[0, 0, :, base + HD : base + 2 * HD]
        values = joined_ref[0, 0, :, base + 2 * HD : base + 3 * HD]
        mixed_grad = mixed_grad_ref[:, head * HD : (head + 1) * HD]
        scores = (dot_nt(keys, query) + dot_nt(spots_ref[...], table_ref[head])) * SCALE
        exact = jnp.exp(scores - total_ref[0, 0, head : head + 1, :])
        value_grad = dot_nn(exact.astype(jnp.bfloat16), mixed_grad)
        prob_grad = dot_nt(values, mixed_grad)
        shared = jnp.sum(exact * prob_grad, 0, keepdims=True)
        score_grad = (exact * (prob_grad - shared)).astype(jnp.bfloat16)
        key_grad = dot_nn(score_grad, query) * SCALE
        wide = jnp.concatenate([keys, spots_ref[:, : 2 * GRID]], 1)
        query_wide = dot_tn(score_grad, wide)
        shift_ref[head] += query_wide
        grad_ref[0, 0, :, base : base + HD] = (query_wide[:, :HD] * SCALE).astype(jnp.bfloat16)
        grad_ref[0, 0, :, base + HD : base + 2 * HD] = key_grad.astype(jnp.bfloat16)
        grad_ref[0, 0, :, base + 2 * HD : base + 3 * HD] = value_grad.astype(jnp.bfloat16)
    column_ref[0, 0] = dot_nn(jnp.ones((8, TOKS), jnp.bfloat16), grad_ref[0, 0])


def attention_backward(branch_grad, weights, joined_rows, total, table, spots, others):
    parts, images, _, width = joined_rows.shape
    heads = width // JOIN
    wide = HD + 2 * GRID
    return pl.pallas_call(
        ordered(attention_backward_kernel, 6, len(others)),
        grid=(parts, images),
        in_specs=[
            pl.BlockSpec((1, TOKS, D), lambda m, i: (i, 0, 0)),
            weight_spec(weights, weights.shape[3], 0),
            pl.BlockSpec((1, 1, TOKS, width), lambda m, i: (m, i, 0, 0)),
            pl.BlockSpec((1, 1, heads, TOKS), lambda m, i: (m, i, 0, 0)),
            pl.BlockSpec((heads, TOKS, 4 * GRID), lambda m, i: (m, 0, 0)),
            pl.BlockSpec((TOKS, 4 * GRID), lambda m, i: (0, 0)),
            *unread(others),
        ],
        out_specs=[
            pl.BlockSpec((1, 1, TOKS, width), lambda m, i: (m, i, 0, 0)),
            pl.BlockSpec((1, 1, 8, width), lambda m, i: (m, i, 0, 0)),
            pl.BlockSpec((heads, TOKS, wide), lambda m, i: (m, 0, 0)),
        ],
        out_shape=[
            jax.ShapeDtypeStruct((parts, images, TOKS, width), jnp.bfloat16),
            jax.ShapeDtypeStruct((parts, images, 8, width), jnp.float32),
            jax.ShapeDtypeStruct((parts * heads, TOKS, wide), jnp.float32),
        ],
        scratch_shapes=[pltpu.VMEM((TOKS, heads * HD), jnp.bfloat16)],
        cost_estimate=cost(images * (2 * TOKS * D * D + H * 10 * TOKS * TOKS * 128), 5e7),
        compiler_params=params("arbitrary", "arbitrary"),
        name="attention_backward",
    )(branch_grad, weights, joined_rows, total, table, spots, *others)


def mixback_kernel(mixed_ref, weight_ref, stream_ref, mods_ref, bias_ref, branch_ref, one_ref, second_ref):
    parts, width = mixed_ref.shape[0], mixed_ref.shape[3]
    total = bias_ref[...]
    for part in range(parts):
        block = weight_ref[:, part]
        total = total + dot_nt(
            mixed_ref[part, 0], block.reshape(block.shape[0] * block.shape[1], width)
        )
    branch_ref[0] = total.astype(jnp.bfloat16)
    stream = stream_ref[0] + mods_ref[0, 2:3] * total
    one_ref[0] = stream
    normed, _ = norm_of(stream)
    second_ref[0] = (normed * (1.0 + mods_ref[0, 4:5]) + mods_ref[0, 3:4]).astype(jnp.bfloat16)


def mixback_forward(mixed, weights, stream, mods, bias):
    parts, images, _, width = mixed.shape
    tile = pl.BlockSpec((1, TOKS, D), lambda i: (i, 0, 0))
    return pl.pallas_call(
        mixback_kernel,
        grid=(images,),
        in_specs=[
            pl.BlockSpec((parts, 1, TOKS, width), lambda i: (0, i, 0, 0)),
            pl.BlockSpec(weights.shape, lambda i: (0, 0, 0, 0)),
            tile,
            pl.BlockSpec((1, 8, D), lambda i: (i, 0, 0)),
            pl.BlockSpec((1, D), lambda i: (0, 0)),
        ],
        out_specs=[tile, tile, tile],
        out_shape=[
            jax.ShapeDtypeStruct((images, TOKS, D), jnp.bfloat16),
            jax.ShapeDtypeStruct((images, TOKS, D), jnp.float32),
            jax.ShapeDtypeStruct((images, TOKS, D), jnp.bfloat16),
        ],
        cost_estimate=cost(images * 2 * TOKS * D * D, images * TOKS * D * 14),
        compiler_params=params("arbitrary"),
        name="mixback_forward",
    )(mixed, weights, stream, mods, bias)


def feed_forward_kernel(
    width,
    second_ref,
    expand_ref,
    narrow_ref,
    bias_ref,
    stream_ref,
    mods_ref,
    biases_ref,
    final_ref,
    final_bias_ref,
    target_ref,
    valid_ref,
    active_ref,
    slope_ref,
    two_ref,
    branch_grad_ref,
    sums_ref,
    final_grad_ref,
    output_ref,
    total_ref,
):
    m, i = pl.program_id(0), pl.program_id(1)
    last = pl.num_programs(0) - 1
    chunk = width // 3 if width % 384 == 0 else width
    second = second_ref[0]
    total = None
    for begin in range(0, width, chunk):
        columns = expand_ref[:, 0, :, begin : begin + chunk]
        columns = columns.reshape(columns.shape[0] * columns.shape[1], chunk)
        hidden = dot_nn(second, columns) + bias_ref[0, :, begin : begin + chunk]
        square = hidden * hidden
        curve = jnp.tanh(ROOT * hidden * (1.0 + 0.044715 * square))
        half = 0.5 * (1.0 + curve)
        active = (hidden * half).astype(jnp.bfloat16)
        slope = half + 0.5 * hidden * (1.0 - curve * curve) * (
            ROOT * (1.0 + 3.0 * 0.044715 * square)
        )
        active_ref[0, 0, :, begin : begin + chunk] = active
        slope_ref[0, 0, :, begin : begin + chunk] = slope.astype(jnp.bfloat16)
        columns = narrow_ref[:, 0, :, begin : begin + chunk]
        columns = columns.reshape(columns.shape[0] * columns.shape[1], chunk)
        product = dot_nt(active, columns)
        total = product if total is None else total + product

    @pl.when(m == 0)
    def begin_total():
        total_ref[i] = total

    @pl.when((m > 0) & (m < last))
    def add_total():
        total_ref[i] += total

    @pl.when(m == last)
    def finish():
        branch = total_ref[i] + total + biases_ref[0:1]
        gate = mods_ref[0, 5:6]
        scale = 1.0 + mods_ref[0, 7:8]
        normed, inverse = norm_of(stream_ref[0] + gate * branch)
        final_in = (normed * scale + mods_ref[0, 6:7]).astype(jnp.bfloat16)
        error = dot_nn(final_in, final_ref[...]) + final_bias_ref[...] - target_ref[0]
        valid = valid_ref[0, :, 0:1]
        loss = valid * (total_rows(jnp.mean(error * error, -1, keepdims=True)))
        output_grad = (valid * 2.0 * error / 32.0).astype(jnp.bfloat16)
        gradient = dot_nt(output_grad, final_ref[...])
        two = norm_back(normed, inverse, gradient * scale)
        two_ref[0] = two
        branch_grad = (gate * two).astype(jnp.bfloat16)
        branch_grad_ref[0] = branch_grad
        sums_ref[0, 0:1] = total_rows(gradient)
        sums_ref[0, 1:2] = total_rows(gradient * normed)
        sums_ref[0, 2:3] = total_rows(two * branch)
        sums_ref[0, 3:4] = total_rows(branch_grad.astype(jnp.float32))
        final_grad_ref[0] = dot_tn(output_grad, final_in)
        output_ref[0, 0:1] = total_rows(output_grad.astype(jnp.float32))
        output_ref[0, 1:2] = jnp.broadcast_to(loss, (1, 32))


def feed_forward(second_in, weights, lanes, width, bias, stream, mods, biases, final, final_bias, target, valid):
    images = second_in.shape[0]
    parts = weights.shape[1]
    last = parts - 1
    tile = pl.BlockSpec((1, TOKS, D), lambda m, i: (i, 0, 0))
    late = pl.BlockSpec((1, TOKS, D), lambda m, i: (hold(m, last, i), 0, 0))
    wide = pl.BlockSpec((1, 1, TOKS, width), lambda m, i: (m, i, 0, 0))
    fixed = lambda shape: pl.BlockSpec(shape, lambda m, i: (0,) * len(shape))
    lately = lambda shape: pl.BlockSpec((1,) + shape, lambda m, i: (hold(m, last, i), 0, 0))
    return pl.pallas_call(
        partial(feed_forward_kernel, width),
        grid=(parts, images),
        in_specs=[
            tile,
            weight_spec(weights, lanes, 0),
            weight_spec(weights, lanes, 1),
            pl.BlockSpec((1, 1, width), lambda m, i: (m, 0, 0)),
            late,
            pl.BlockSpec((1, 8, D), lambda m, i: (i, 0, 0)),
            fixed(biases.shape),
            fixed(final.shape),
            fixed(final_bias.shape),
            lately((TOKS, 32)),
            pl.BlockSpec((1, 1, 128), lambda m, i: (i, 0, 0)),
        ],
        out_specs=[wide, wide, late, late, lately((4, D)), lately((32, D)), lately((2, 32))],
        out_shape=[
            jax.ShapeDtypeStruct((parts, images, TOKS, width), jnp.bfloat16),
            jax.ShapeDtypeStruct((parts, images, TOKS, width), jnp.bfloat16),
            jax.ShapeDtypeStruct((images, TOKS, D), jnp.float32),
            jax.ShapeDtypeStruct((images, TOKS, D), jnp.bfloat16),
            jax.ShapeDtypeStruct((images, 4, D), jnp.float32),
            jax.ShapeDtypeStruct((images, 32, D), jnp.float32),
            jax.ShapeDtypeStruct((images, 2, 32), jnp.float32),
        ],
        scratch_shapes=[pltpu.VMEM((images, TOKS, D), jnp.float32)],
        cost_estimate=cost(images * 4 * TOKS * D * FF, 6e7, images * TOKS * FF),
        compiler_params=params("arbitrary", "arbitrary"),
        name="feed_forward",
    )(second_in, weights, weights, bias, stream, mods, biases, final, final_bias, target, valid)


def feed_backward_kernel(
    width,
    branch_grad_ref,
    expand_ref,
    narrow_ref,
    slope_ref,
    two_ref,
    stream_ref,
    branch_ref,
    mods_ref,
    hidden_grad_ref,
    hidden_sum_ref,
    one_ref,
    first_grad_ref,
    sums_ref,
    total_ref,
):
    m, i = pl.program_id(0), pl.program_id(1)
    last = pl.num_programs(0) - 1
    chunk = width // 3 if width % 384 == 0 else width
    branch_grad = branch_grad_ref[0]

    @pl.when(i == 0)
    def start():
        hidden_sum_ref[...] = jnp.zeros_like(hidden_sum_ref)

    total = None
    for begin in range(0, width, chunk):
        columns = narrow_ref[:, 0, :, begin : begin + chunk]
        columns = columns.reshape(columns.shape[0] * columns.shape[1], chunk)
        active_grad = dot_nn(branch_grad, columns)
        hidden_grad = (
            active_grad * slope_ref[0, 0, :, begin : begin + chunk].astype(jnp.float32)
        ).astype(jnp.bfloat16)
        hidden_grad_ref[0, 0, :, begin : begin + chunk] = hidden_grad
        hidden_sum_ref[0, :, begin : begin + chunk] += total_rows(hidden_grad.astype(jnp.float32))
        columns = expand_ref[:, 0, :, begin : begin + chunk]
        columns = columns.reshape(columns.shape[0] * columns.shape[1], chunk)
        product = dot_nt(hidden_grad, columns)
        total = product if total is None else total + product

    @pl.when(m == 0)
    def begin_total():
        total_ref[i] = total

    @pl.when((m > 0) & (m < last))
    def add_total():
        total_ref[i] += total

    @pl.when(m == last)
    def finish():
        gradient = total_ref[i] + total
        normed, inverse = norm_of(stream_ref[0])
        one = two_ref[0] + norm_back(normed, inverse, gradient * (1.0 + mods_ref[0, 4:5]))
        one_ref[0] = one
        first_grad = (mods_ref[0, 2:3] * one).astype(jnp.bfloat16)
        first_grad_ref[0] = first_grad
        sums_ref[0, 0:1] = total_rows(gradient)
        sums_ref[0, 1:2] = total_rows(gradient * normed)
        sums_ref[0, 2:3] = total_rows(one * branch_ref[0].astype(jnp.float32))
        sums_ref[0, 3:4] = total_rows(first_grad.astype(jnp.float32))


def feed_backward(branch_grad, weights, lanes, width, slope, two, stream, branch, mods, others):
    images = branch_grad.shape[0]
    parts = weights.shape[1]
    last = parts - 1
    tile = pl.BlockSpec((1, TOKS, D), lambda m, i: (i, 0, 0))
    late = pl.BlockSpec((1, TOKS, D), lambda m, i: (hold(m, last, i), 0, 0))
    wide = pl.BlockSpec((1, 1, TOKS, width), lambda m, i: (m, i, 0, 0))
    return pl.pallas_call(
        ordered(partial(feed_backward_kernel, width), 8, len(others)),
        grid=(parts, images),
        in_specs=[
            tile,
            weight_spec(weights, lanes, 0),
            weight_spec(weights, lanes, 1),
            wide,
            late,
            late,
            late,
            pl.BlockSpec((1, 8, D), lambda m, i: (i, 0, 0)),
            *unread(others),
        ],
        out_specs=[
            wide,
            pl.BlockSpec((1, 1, width), lambda m, i: (m, 0, 0)),
            late,
            late,
            pl.BlockSpec((1, 4, D), lambda m, i: (hold(m, last, i), 0, 0)),
        ],
        out_shape=[
            jax.ShapeDtypeStruct((parts, images, TOKS, width), jnp.bfloat16),
            jax.ShapeDtypeStruct((parts, 1, width), jnp.float32),
            jax.ShapeDtypeStruct((images, TOKS, D), jnp.float32),
            jax.ShapeDtypeStruct((images, TOKS, D), jnp.bfloat16),
            jax.ShapeDtypeStruct((images, 4, D), jnp.float32),
        ],
        scratch_shapes=[pltpu.VMEM((images, TOKS, D), jnp.float32)],
        cost_estimate=cost(images * 4 * TOKS * D * FF, 6e7),
        compiler_params=params("arbitrary", "arbitrary"),
        name="feed_backward",
    )(branch_grad, weights, weights, slope, two, stream, branch, mods, *others)


def joined_backward_kernel(
    width,
    grad_ref,
    weight_ref,
    one_ref,
    zero_ref,
    mods_ref,
    embed_ref,
    sums_ref,
    embed_grad_ref,
    total_ref,
):
    m, i = pl.program_id(0), pl.program_id(1)
    last = pl.num_programs(0) - 1
    total = dot_nt(grad_ref[0, 0], block_of(weight_ref, width))

    @pl.when(m == 0)
    def begin_total():
        total_ref[i] = total

    @pl.when((m > 0) & (m < last))
    def add_total():
        total_ref[i] += total

    @pl.when(m == last)
    def finish():
        gradient = total_ref[i] + total
        normed, inverse = norm_of(zero_ref[0])
        zero = one_ref[0] + norm_back(normed, inverse, gradient * (1.0 + mods_ref[0, 1:2]))
        sums_ref[0, 0:1] = total_rows(gradient)
        sums_ref[0, 1:2] = total_rows(gradient * normed)
        sums_ref[0, 2:3] = total_rows(zero)
        sums_ref[0, 3:4] = jnp.zeros((1, D), jnp.float32)
        upper = zero.astype(jnp.bfloat16)
        lower = (zero - upper.astype(jnp.float32)).astype(jnp.bfloat16)
        embed_grad_ref[0] = dot_tn(embed_ref[0], upper) + dot_tn(embed_ref[0], lower)


def joined_backward(grad_joined, weights, lanes, one, zero, mods, embed_in, others):
    parts, images, _, width = grad_joined.shape
    last = parts - 1
    late = pl.BlockSpec((1, TOKS, D), lambda m, i: (hold(m, last, i), 0, 0))
    return pl.pallas_call(
        ordered(partial(joined_backward_kernel, width), 6, len(others)),
        grid=(parts, images),
        in_specs=[
            pl.BlockSpec((1, 1, TOKS, width), lambda m, i: (m, i, 0, 0)),
            weight_spec(weights, lanes, 0),
            late,
            late,
            pl.BlockSpec((1, 8, D), lambda m, i: (i, 0, 0)),
            pl.BlockSpec((1, TOKS, 16), lambda m, i: (i, 0, 0)),
            *unread(others),
        ],
        out_specs=[
            pl.BlockSpec((1, 4, D), lambda m, i: (hold(m, last, i), 0, 0)),
            pl.BlockSpec((1, 16, D), lambda m, i: (hold(m, last, i), 0, 0)),
        ],
        out_shape=[
            jax.ShapeDtypeStruct((images, 4, D), jnp.float32),
            jax.ShapeDtypeStruct((images, 16, D), jnp.float32),
        ],
        scratch_shapes=[pltpu.VMEM((images, TOKS, D), jnp.float32)],
        cost_estimate=cost(images * 2 * TOKS * D * 3 * D, 3e7),
        compiler_params=params("arbitrary", "arbitrary"),
        name="joined_backward",
    )(grad_joined, weights, one, zero, mods, embed_in, *others)


def weight_gradient_kernel(widths, *refs):
    pairs = len(widths)
    inputs, gradients = refs[:pairs], refs[pairs : 2 * pairs]
    received_ref = refs[2 * pairs] if len(refs) == 3 * pairs + 2 else None
    grad_ref, turned = refs[-pairs - 1], refs[-pairs:]

    @pl.when((pl.program_id(0) == 0) & (pl.program_id(1) == 0))
    def turn():
        for turned_ref, inputs_ref in zip(turned, inputs):
            turned_ref[...] = inputs_ref[...].T

    begin = 0
    for width, turned_ref, gradient_ref in zip(widths, turned, gradients):
        product = dot_nn(turned_ref[...], gradient_ref[0])
        if received_ref is not None:
            product = product + received_ref[0, :, begin : begin + width].astype(jnp.float32)
        grad_ref[0, :, begin : begin + width] = product.astype(jnp.bfloat16)
        begin = begin + width


def weight_gradient(pairs, chosen, cores, received=None, others=()):
    rows = pairs[0][0].shape[0]
    parts = pairs[0][1].shape[0]
    widths = [gradient.shape[2] for _, gradient in pairs]
    width = sum(widths)
    chunks = 3 if len(pairs) == 1 and width % 384 == 0 else 1
    pieces = [member // chunks for member in widths]
    count = parts // cores
    taken = 2 * len(pairs) + (received is not None)
    kernel = ordered(partial(weight_gradient_kernel, pieces), taken, len(others))
    out_spec = pl.BlockSpec((1, D, width // chunks), lambda y, k, chosen: (y, 0, k))
    in_specs = [pl.BlockSpec((rows, D), lambda y, k, chosen: (0, 0)) for _ in pairs] + [
        pl.BlockSpec((1, rows, piece), lambda y, k, chosen: (y * cores + chosen[0], 0, k))
        for piece in pieces
    ]
    operands = [member for member, _ in pairs] + [member for _, member in pairs]
    if received is not None:
        in_specs.append(out_spec)
        operands.append(received)
    return pl.pallas_call(
        lambda chosen_ref, *refs: kernel(*refs),
        grid_spec=pltpu.PrefetchScalarGridSpec(
            num_scalar_prefetch=1,
            grid=(count, chunks),
            in_specs=in_specs + unread(others),
            out_specs=out_spec,
            scratch_shapes=[pltpu.VMEM((D, rows), jnp.bfloat16) for _ in pairs],
        ),
        out_shape=jax.ShapeDtypeStruct((count, D, width), jnp.bfloat16),
        cost_estimate=cost(2 * rows * D * width * count, rows * (D + width * count) * 2),
        compiler_params=params("arbitrary", "arbitrary"),
        name="weight_gradient",
    )(chosen, *operands, *others)


def whole_gradient_kernel(inputs_ref, gradient_ref, grad_ref, turned_ref):
    @pl.when((pl.program_id(0) == 0) & (pl.program_id(1) == 0))
    def turn():
        turned_ref[...] = inputs_ref[...].T

    product = dot_nn(turned_ref[...], gradient_ref[0]).astype(jnp.bfloat16)
    groups, _, rows, width = grad_ref.shape
    grad_ref[:, 0] = product.reshape(groups, rows, width)


def whole_gradient(inputs, gradient, groups):
    rows = inputs.shape[0]
    parts, _, width = gradient.shape
    chunks = 3 if width % 384 == 0 else 1
    piece = width // chunks
    split = groups if (D // groups) % 16 == 0 else 1
    result = pl.pallas_call(
        whole_gradient_kernel,
        grid=(parts, chunks),
        in_specs=[
            pl.BlockSpec((rows, D), lambda m, k: (0, 0)),
            pl.BlockSpec((1, rows, piece), lambda m, k: (m, 0, k)),
        ],
        out_specs=pl.BlockSpec((split, 1, D // split, piece), lambda m, k: (0, m, 0, k)),
        out_shape=jax.ShapeDtypeStruct((split, parts, D // split, width), jnp.bfloat16),
        scratch_shapes=[pltpu.VMEM((D, rows), jnp.bfloat16)],
        cost_estimate=cost(2 * rows * D * width * parts, rows * (D + width * parts) * 2),
        compiler_params=params("arbitrary", "arbitrary"),
        name="whole_gradient",
    )(inputs, gradient)
    if split == 1:
        result = result.reshape(parts, groups, D // groups, width).transpose(1, 0, 2, 3)
    return result.reshape(groups * parts, D // groups, width)


def relative_tables(rel_table):
    rows = offset_table()
    span = 2 * GRID - 1
    along_rows = jnp.dot(rel_table[:, :span], rows, precision=highest).reshape(H, GRID, 1, GRID)
    along_cols = jnp.dot(rel_table[:, span:], rows, precision=highest).reshape(H, 1, GRID, GRID)
    full = (H, GRID, GRID, GRID)
    table = jnp.concatenate(
        [jnp.broadcast_to(along_rows, full), jnp.broadcast_to(along_cols, full)], 3
    ).reshape(H, TOKS, 2 * GRID) * math.sqrt(HD)
    upper = table.astype(jnp.bfloat16)
    lower = (table - upper.astype(jnp.float32)).astype(jnp.bfloat16)
    return jnp.concatenate([upper, lower], 2)


def spot_table():
    places = jnp.arange(TOKS)
    rows = (places[:, None] // GRID == jnp.arange(GRID)[None, :]).astype(jnp.bfloat16)
    cols = (places[:, None] % GRID == jnp.arange(GRID)[None, :]).astype(jnp.bfloat16)
    return jnp.concatenate([rows, cols, rows, cols], 1)


def relative_gradient(shifts):
    rows = offset_table()
    row_part = jnp.sum(shifts[:, :, :GRID].reshape(H, GRID, GRID, GRID), 2)
    col_part = jnp.sum(shifts[:, :, GRID:].reshape(H, GRID, GRID, GRID), 1)
    return jnp.concatenate(
        [
            jnp.dot(row_part.reshape(H, TOKS), rows.T, precision=highest),
            jnp.dot(col_part.reshape(H, TOKS), rows.T, precision=highest),
        ],
        1,
    ).reshape(H * REL)


def small_gather(values, axes, count):
    spread = jnp.broadcast_to(values[None], (count,) + values.shape)
    return lax.all_to_all(spread, axes, 0, 0, tiled=True)


def pick(values, index, dim):
    return lax.dynamic_index_in_dim(values, index, dim, keepdims=False)


def tie(*values):
    return lax.optimization_barrier(values)


def swap(values, axis):
    return lax.ppermute(values, axis, [(0, 1), (1, 0)])


class Exchange:
    def __init__(self, sizes, places):
        self.sizes, self.places = sizes, places
        self.chosen = places["c"].astype(jnp.int32).reshape(1)

    def gradient(self, pairs, others=()):
        self.sent = weight_gradient(pairs, 1 - self.chosen, self.sizes["c"], None, others)
        self.received = swap(self.sent, "c")

    def kept_gradient(self, pairs, others=()):
        return weight_gradient(pairs, self.chosen, self.sizes["c"], self.received, others)

    def prepare(self, values, dim, axis):
        size, index = self.sizes[axis], self.places[axis]
        if size == 2:
            return pick(values, 1 - index, dim), pick(values, index, dim)
        return jnp.moveaxis(values, dim, 0), None

    def launch_one(self, sent, axis):
        if self.sizes[axis] == 2:
            return swap(sent, axis)
        return lax.all_to_all(sent, axis, 0, 0, tiled=True)

    def open_first(self, kept):
        da, db, ny = (self.sizes[key] for key in ("da", "db", "y"))
        kept = kept.reshape(ny, da, db, D // (da * db), kept.shape[2])
        half = da // 2
        sent_a, own_a = self.prepare(kept[:, :half], 0, "y")
        sent_b, own_b = self.prepare(kept[:, half:], 2, "db")
        self.own, self.axes = (own_a, own_b), ("y", "db")
        self.sent = (sent_a, sent_b)

    def launch(self):
        self.arrived = tuple(map(self.launch_one, self.sent, self.axes))

    def close(self):
        def add(own, arrived):
            if own is None:
                return jnp.sum(arrived.astype(jnp.float32), 0).astype(jnp.bfloat16)
            return (own.astype(jnp.float32) + arrived.astype(jnp.float32)).astype(jnp.bfloat16)

        return tuple(map(add, self.own, self.arrived))

    def open_second(self):
        part_a, part_b = self.close()
        sent_a, own_a = self.prepare(part_a, 1, "db")
        sent_b, own_b = self.prepare(part_b, 0, "y")
        self.own, self.axes = (own_a, own_b), ("db", "y")
        self.sent = (sent_a, sent_b)

    def open_last(self):
        joint = jnp.concatenate(self.close(), 0)
        size, index = self.sizes["da"], self.places["da"]
        if size > 4:
            self.own, self.sent = None, (joint,)
            return
        self.own = pick(joint, index, 0)
        self.sent = tuple(pick(joint, (index + shift) % size, 0) for shift in range(1, size))

    def launch_last(self):
        size = self.sizes["da"]
        if self.own is None:
            self.arrived = (lax.all_to_all(self.sent[0], "da", 0, 0, tiled=True),)
            return
        self.arrived = tuple(
            lax.ppermute(sent, "da", [(place, (place + shift + 1) % size) for place in range(size)])
            for shift, sent in enumerate(self.sent)
        )

    def result(self):
        if self.own is None:
            return jnp.sum(self.arrived[0].astype(jnp.float32), 0)
        return sum((member.astype(jnp.float32) for member in self.arrived), self.own.astype(jnp.float32))


def lane_padded(values):
    width = values.shape[1]
    return jnp.pad(values, ((0, 0), (0, -width % 128)))


def in_parts(gathered, groups, parts):
    rows, width = gathered.shape[1:]
    blocks = gathered.reshape(groups, parts, rows, width)
    if rows % 16 == 0:
        return blocks
    return blocks.transpose(1, 0, 2, 3).reshape(1, parts, groups * rows, width)


def adamw_update(master, moment, second, gradient):
    first_new = beta_one * moment + (1.0 - beta_one) * gradient
    square_new = beta_two * second + (1.0 - beta_two) * gradient * gradient
    first_hat = first_new / (1.0 - beta_one**STEP)
    square_hat = square_new / (1.0 - beta_two**STEP)
    master_new = master - learn_rate * (
        first_hat / (jnp.sqrt(square_hat) + adam_eps) + weight_decay * master
    )
    return (first_new, square_new, master_new)


TOKEN_SMALLS = (
    "embed_bias",
    "query_bias",
    "value_bias",
    "out_bias",
    "fc1_bias",
    "fc2_bias",
    "final_bias",
    "embed_weight",
    "final_weight",
    "rel_bias",
)


def per_device(
    sizes,
    latents,
    noises,
    timesteps,
    labels,
    dropped,
    buckets,
    counts,
    *state,
):
    masters, moments, seconds = (state[0::3], state[1::3], state[2::3])
    (
        joined_weight,
        mixback_weight,
        expand_weight,
        narrow_weight,
        timeone_weight,
        timetwo_weight,
        modulator_weight,
        classes_weight,
        smalls_weight,
    ) = masters
    da, db, ny, nc = (sizes[key] for key in ("da", "db", "y", "c"))
    dp, mp = (da * db, ny * nc)
    dp_axes, mp_axes = (("da", "db"), ("y", "c"))
    all_axes = dp_axes + mp_axes
    places_now = {key: lax.axis_index(key) for key in ("da", "db", "y", "c")}
    dp_index = places_now["da"] * db + places_now["db"]
    mp_index = places_now["y"] * nc + places_now["c"]
    places = layout()
    zero_index = jnp.zeros((), jnp.int32)

    def small_piece(key_name):
        begin_at, length = places[key_name]
        return smalls_weight[begin_at : begin_at + length]

    own_images = latents.shape[0]
    group_size = timesteps.shape[0]
    images_all = dp * group_size
    row_width = timetwo_weight.shape[0]
    width_mp = timetwo_weight.shape[1]
    mod_width = modulator_weight.shape[1]

    joined_width, mixback_width = (joined_weight.shape[1], mixback_weight.shape[1])
    hidden_width = expand_weight.shape[1]
    shard_one = jnp.concatenate([lane_padded(joined_weight), mixback_weight], 1)
    shard_two = jnp.concatenate([lane_padded(expand_weight), lane_padded(narrow_weight)], 1)
    gathered_one = in_parts(
        lax.all_gather(shard_one.astype(jnp.bfloat16), all_axes), dp, mp
    )
    feed = in_parts(lax.all_gather(shard_two.astype(jnp.bfloat16), all_axes), dp, mp)
    joined_lanes = gathered_one.shape[3] - mixback_width
    hidden_lanes = feed.shape[3] // 2
    mixback = gathered_one[:, :, :, joined_lanes:]

    facts = small_gather(
        jnp.concatenate([timesteps, labels, dropped, buckets, counts]).astype(jnp.float32),
        dp_axes,
        dp,
    )
    times_all = facts[:, :group_size].reshape(images_all)
    labels_all = facts[:, group_size : 2 * group_size].reshape(images_all)
    dropped_all = facts[:, 2 * group_size : 3 * group_size].reshape(images_all)
    buckets_all = facts[:, 3 * group_size]
    token_count = jnp.sum(facts[:, 3 * group_size + 1]) * TOKS
    time_first = small_gather(timeone_weight.astype(jnp.bfloat16), dp_axes, dp).reshape(
        FREQ, width_mp
    )
    bucket_width = float(1000 // NB)
    rows_in = frequencies(
        jnp.concatenate([times_all, buckets_all * bucket_width + 0.5 * bucket_width])
    ).astype(jnp.bfloat16)
    hidden_time = jnp.dot(
        rows_in, time_first, preferred_element_type=jnp.float32
    ) + lax.dynamic_slice_in_dim(small_piece("time_bias_one"), mp_index * width_mp, width_mp)
    hidden_act = jax.nn.silu(hidden_time).astype(jnp.bfloat16)
    embed_part = dot_nt(hidden_act, timetwo_weight.astype(jnp.bfloat16))
    class_index = jnp.where(dropped_all > 0, float(NCLS), labels_all)
    onehot = (class_index[:, None] == jnp.arange(NCLS + 1, dtype=jnp.float32)[None, :]).astype(
        jnp.bfloat16
    )
    label_cols = jnp.dot(
        onehot, classes_weight.astype(jnp.bfloat16), preferred_element_type=jnp.float32
    )
    column_at = dp_index * row_width
    owner = column_at // width_mp
    label_part = lax.dynamic_slice_in_dim(label_cols, column_at - owner * width_mp, row_width, 1)
    label_part = jnp.where(mp_index == owner, label_part, 0.0)
    condition = jnp.sum(
        small_gather(
            jnp.concatenate([embed_part[:images_all] + label_part, embed_part[images_all:]], 0),
            mp_axes,
            mp,
        ),
        0,
    ) + lax.dynamic_slice_in_dim(small_piece("time_bias_two"), column_at, row_width)
    cond_act = jax.nn.silu(condition).astype(jnp.bfloat16)
    modulator = modulator_weight.astype(jnp.bfloat16)
    global_cols = mp_index * mod_width + jnp.arange(mod_width)
    mods_part = jnp.dot(cond_act, modulator, preferred_element_type=jnp.float32)
    outgoing = jnp.where(
        global_cols < 8 * D,
        mods_part[:images_all].reshape(dp, group_size, mod_width),
        mods_part[images_all:].reshape(dp, 1, mod_width),
    ).astype(jnp.bfloat16)
    incoming = lax.all_to_all(
        outgoing.reshape(dp * mp, own_images, mod_width), all_axes, 0, 0, tiled=True
    ).reshape(dp, mp, own_images, mod_width)
    modulation = jnp.sum(incoming.astype(jnp.float32), 0).transpose(1, 0, 2).reshape(
        own_images, 10 * D
    ) + small_piece("cond_bias")

    own_times = lax.dynamic_slice_in_dim(timesteps, mp_index * own_images, own_images)
    slot_index = mp_index * own_images + jnp.arange(own_images)
    valid_flags = (slot_index >= group_size - counts[0]).astype(jnp.float32)
    time_frac = (own_times.astype(jnp.float32) + 1.0) / 1000.0
    alpha_scale = jnp.cos(0.5 * math.pi * time_frac)[:, None, None]
    sigma_scale = jnp.sin(0.5 * math.pi * time_frac)[:, None, None]
    noisy_all = patchify(alpha_scale * latents + sigma_scale * noises)
    target = patchify(jnp.concatenate([alpha_scale * noises - sigma_scale * latents, noises], 1))
    embed_weight = small_piece("embed_weight").reshape(16, D)
    final_weight = small_piece("final_weight").reshape(D, 32)
    table = relative_tables(small_piece("rel_bias").reshape(H, REL))
    spots = spot_table()
    images = own_images
    rows_all = images * TOKS
    mods = modulation[:, : 8 * D].reshape(images, 8, D)

    embed_in = noisy_all.astype(jnp.bfloat16)
    stream_zero = (
        jnp.einsum(
            "ntc,cd->ntd",
            embed_in,
            embed_weight.astype(jnp.bfloat16),
            preferred_element_type=jnp.float32,
        )
        + small_piece("embed_bias")
        + position_table()
    )
    normed_a, _ = layernorm_parts(stream_zero)
    first_in = (
        normed_a * (1.0 + column_of(modulation, 1)) + column_of(modulation, 0)
    ).astype(jnp.bfloat16)
    added = jnp.stack(
        [
            (small_piece("query_bias") + modulation[:, 8 * D : 9 * D]).reshape(images, H, HD),
            jnp.zeros((images, H, HD), jnp.float32),
            (small_piece("value_bias") + modulation[:, 9 * D :]).reshape(images, H, HD),
        ],
        2,
    )
    added = added.reshape(images, mp, joined_width).transpose(1, 0, 2)[:, :, None]
    joined_rows, mixed, log_total = attention_forward(
        first_in, gathered_one, joined_lanes, joined_width, added, table, spots
    )
    branch, stream_one, second_in = mixback_forward(
        mixed, mixback, stream_zero, mods, small_piece("out_bias")[None]
    )
    timetwo_narrow, second_in = tie(timetwo_weight.astype(jnp.bfloat16), second_in)
    time_second_all = small_gather(timetwo_narrow, dp_axes, dp)
    active, slope, grad_two, grad_branch_two, sums_c, final_grads, output_sums = feed_forward(
        second_in,
        feed,
        hidden_lanes,
        hidden_width,
        small_piece("fc1_bias").reshape(mp, 1, hidden_width),
        stream_one,
        mods,
        small_piece("fc2_bias")[None],
        final_weight.astype(jnp.bfloat16),
        small_piece("final_bias")[None],
        target,
        jnp.broadcast_to(valid_flags[:, None, None], (images, 1, 128)),
    )
    loss_part = jnp.sum(output_sums[:, 1, 0])
    time_second_all, grad_branch_two = tie(time_second_all, grad_branch_two)
    time_second_all = time_second_all.reshape(D, width_mp)

    def flat(values):
        return values.reshape(rows_all, D)

    def in_rows(values):
        return values.reshape(mp, rows_all, values.shape[3])

    narrow_sum, heads_sum = (Exchange(sizes, places_now) for _ in range(2))
    narrow_pairs = [(flat(grad_branch_two), in_rows(active))]
    narrow_sum.gradient(narrow_pairs)
    grad_hidden, hidden_sums, grad_one, grad_branch, sums_b = feed_backward(
        grad_branch_two,
        feed,
        hidden_lanes,
        hidden_width,
        slope,
        grad_two,
        stream_one,
        branch,
        mods,
        [narrow_sum.sent],
    )
    expand_all = whole_gradient(flat(second_in), in_rows(grad_hidden), dp)
    expand_shard = lax.psum_scatter(expand_all, all_axes, scatter_dimension=0, tiled=True)[0]
    narrow_sum.open_first(narrow_sum.kept_gradient(narrow_pairs, [expand_all]))
    narrow_sum.launch()
    grad_joined, column_sums, shifts = attention_backward(
        grad_branch, mixback, joined_rows, log_total, table, spots, list(narrow_sum.sent)
    )
    heads_pairs = [(flat(first_in), in_rows(grad_joined)), (flat(grad_branch), in_rows(mixed))]
    narrow_sum.arrived, heads_first = tie(narrow_sum.arrived, grad_joined)
    narrow_sum.open_second()
    narrow_sum.launch()
    heads_sum.gradient(heads_pairs, list(narrow_sum.sent))
    sums_a, embed_grads = joined_backward(
        heads_first,
        gathered_one,
        joined_lanes,
        grad_one,
        stream_zero,
        mods,
        embed_in,
        [heads_sum.sent],
    )
    sums = (
        column_sums[:, :, 0]
        .reshape(mp, images, H // mp, 3, HD)
        .transpose(3, 1, 0, 2, 4)
        .reshape(3, images, D)
    )
    mods_grads = jnp.concatenate(
        [
            sums_a[:, 0],
            sums_a[:, 1],
            sums_b[:, 2],
            sums_b[:, 0],
            sums_b[:, 1],
            sums_c[:, 2],
            sums_c[:, 0],
            sums_c[:, 1],
            sums[0],
            sums[2],
        ],
        1,
    ).astype(jnp.bfloat16)
    to_owners = mods_grads.reshape(own_images, mp, mod_width).transpose(1, 0, 2)
    returned = lax.all_to_all(
        jnp.broadcast_to(to_owners[None], (dp,) + to_owners.shape).reshape(
            dp * mp, own_images, mod_width
        ),
        all_axes,
        0,
        0,
        tiled=True,
    ).reshape(images_all, mod_width)
    heads_kept = heads_sum.kept_gradient(heads_pairs, [to_owners])
    narrow_sum.open_last()
    narrow_sum.sent, heads_kept = tie(narrow_sum.sent, heads_kept)
    narrow_sum.launch_last()
    returned, heads_kept, expand_shard = tie(returned, heads_kept, expand_shard)
    heads_sum.open_first(heads_kept)
    heads_sum.sent, returned = tie(heads_sum.sent, returned)
    heads_sum.launch()
    grad_small = {
        "embed_bias": jnp.sum(sums_a[:, 2], 0),
        "query_bias": jnp.sum(sums[0], 0),
        "value_bias": jnp.sum(sums[2], 0),
        "out_bias": jnp.sum(sums_b[:, 3], 0),
        "fc1_bias": hidden_sums.reshape(FF),
        "fc2_bias": jnp.sum(sums_c[:, 3], 0),
        "final_bias": jnp.sum(output_sums[:, 0], 0),
        "embed_weight": jnp.sum(embed_grads, 0).reshape(16 * D),
        "final_weight": jnp.sum(final_grads, 0).T.reshape(32 * D),
        "rel_bias": relative_gradient(shifts[:, :, HD:]),
    }

    is_image = (global_cols < 8 * D)[None, :]
    returned_wide = returned.astype(jnp.float32)
    cond_bias_grad = jnp.sum(returned_wide, 0)
    bucket_sums = jnp.where(
        is_image, 0.0, jnp.sum(returned_wide.reshape(dp, group_size, mod_width), 1)
    )

    def split_rows(image_rows, bucket_rows):
        upper = bucket_rows.astype(jnp.bfloat16)
        lower = (bucket_rows - upper.astype(jnp.float32)).astype(jnp.bfloat16)
        return jnp.concatenate([image_rows.astype(jnp.bfloat16), upper, lower], 0)

    def double_rows(rows):
        return jnp.concatenate([rows, rows[images_all:]], 0)

    grad_mod = split_rows(jnp.where(is_image, returned, jnp.zeros_like(returned)), bucket_sums)
    modulator_grad = dot_tn(double_rows(cond_act), grad_mod)
    cond_part = dot_nt(grad_mod, modulator)
    cond_part = jnp.concatenate(
        [cond_part[:images_all], cond_part[images_all : images_all + dp] + cond_part[images_all + dp :]],
        0,
    )
    grad_act = small_gather(cond_part, mp_axes, mp)
    grad_act, narrow_sum.arrived = tie(grad_act, narrow_sum.arrived)
    grad_act = jnp.sum(grad_act, 0)
    _, pullback = jax.vjp(jax.nn.silu, condition)
    grad_cond_own = pullback(grad_act)[0]
    grad_embed_own = split_rows(grad_cond_own[:images_all], grad_cond_own[images_all:])
    timetwo_grad = dot_tn(grad_embed_own, double_rows(hidden_act))
    grad_cond = small_gather(grad_cond_own, dp_axes, dp)
    heads_sum.open_second()
    heads_sum.sent, grad_cond = tie(heads_sum.sent, grad_cond)
    heads_sum.launch()
    grad_cond = (
        grad_cond
        .transpose(1, 0, 2)
        .reshape(images_all + dp, D)
    )
    vector = jnp.concatenate([grad_small[key_name] for key_name in TOKEN_SMALLS])
    slice_length = -(-vector.shape[0] // (dp * mp))
    padded = jnp.pad(vector, (0, slice_length * dp * mp - vector.shape[0]))
    padded, grad_cond = tie(padded.reshape(dp * mp, slice_length), grad_cond)
    slice_sum = jnp.sum(lax.all_to_all(padded, all_axes, 0, 0, tiled=True), 0)
    grad_embed = split_rows(grad_cond[:images_all], grad_cond[images_all:])
    bias_two_grad = jnp.sum(grad_embed.astype(jnp.float32), 0)
    grad_hidden_act = dot_nn(grad_embed, time_second_all)
    grad_hidden_act = jnp.concatenate(
        [
            grad_hidden_act[:images_all],
            grad_hidden_act[images_all : images_all + dp] + grad_hidden_act[images_all + dp :],
        ],
        0,
    )
    _, pullback = jax.vjp(jax.nn.silu, hidden_time)
    grad_hidden_time = pullback(grad_hidden_act)[0]
    grad_hidden_time = split_rows(grad_hidden_time[:images_all], grad_hidden_time[images_all:])
    bias_one_grad = jnp.sum(grad_hidden_time.astype(jnp.float32), 0)
    rows_own = lax.dynamic_slice_in_dim(
        rows_in, dp_index * timeone_weight.shape[0], timeone_weight.shape[0], 1
    )
    timeone_grad = dot_tn(double_rows(rows_own), grad_hidden_time)
    label_rows = lax.dynamic_slice_in_dim(grad_cond[:images_all], mp_index * width_mp, width_mp, 1)
    label_upper = label_rows.astype(jnp.bfloat16)
    label_lower = (label_rows - label_upper.astype(jnp.float32)).astype(jnp.bfloat16)
    class_raw = dot_tn(
        jnp.concatenate([onehot, onehot], 0), jnp.concatenate([label_upper, label_lower], 0)
    )

    heads_sum.open_last()
    heads_sum.launch_last()
    heads_grad, narrow_grad = (member.result() for member in (heads_sum, narrow_sum))
    expand_grad = expand_shard.astype(jnp.float32)
    joined_grad, mixback_grad = (heads_grad[:, :joined_width], heads_grad[:, joined_width:])
    mod_slice = -(-mod_width // dp)
    one_slice = -(-width_mp // dp)
    own_cond = lax.dynamic_slice_in_dim(
        jnp.pad(cond_bias_grad, (0, mod_slice * dp - mod_width)), dp_index * mod_slice, mod_slice
    )
    own_one = lax.dynamic_slice_in_dim(
        jnp.pad(bias_one_grad, (0, one_slice * dp - width_mp)), dp_index * one_slice, one_slice
    )
    own_two = lax.dynamic_slice_in_dim(bias_two_grad, column_at, row_width)

    owned = [
        member / token_count
        for member in (
            joined_grad,
            mixback_grad,
            expand_grad,
            narrow_grad,
            timeone_grad,
            timetwo_grad,
            modulator_grad,
        )
    ]
    class_grad = class_raw / token_count
    own_slices = jnp.concatenate([slice_sum, own_cond, own_one]) / token_count
    squares = sum((jnp.sum(member * member) for member in owned)) + jnp.sum(own_slices * own_slices)
    squares = squares + jnp.where(dp_index == 0, jnp.sum(class_grad * class_grad), 0.0)
    own_two = own_two / token_count
    squares = squares + jnp.where(mp_index == 0, jnp.sum(own_two * own_two), 0.0)
    final = small_gather(
        jnp.concatenate([own_slices, squares[None], loss_part[None]]), all_axes, dp * mp
    )
    ends = slice_length + mod_slice + one_slice
    grad_norm = jnp.sqrt(jnp.sum(final[:, ends]))
    loss_sum = jnp.sum(final[:, ends + 1])
    factor = jnp.minimum(1.0, clip_level / grad_norm)
    token_smalls = final[:, :slice_length].reshape(dp * mp * slice_length)
    pieces = {"time_bias_two": bias_two_grad / token_count}
    pieces["cond_bias"] = (
        final[:, slice_length : slice_length + mod_slice]
        .reshape(dp, mp, mod_slice)
        .transpose(1, 0, 2)
        .reshape(mp, dp * mod_slice)[:, :mod_width]
        .reshape(10 * D)
    )
    pieces["time_bias_one"] = (
        final[:, slice_length + mod_slice : ends]
        .reshape(dp, mp, one_slice)
        .transpose(1, 0, 2)
        .reshape(mp, dp * one_slice)[:, :width_mp]
        .reshape(D)
    )
    offset = 0
    for key_name in TOKEN_SMALLS:
        length = places[key_name][1]
        pieces[key_name] = token_smalls[offset : offset + length]
        offset = offset + length
    small_grad = jnp.concatenate([pieces[key_name] for key_name in places])
    gradients = owned + [class_grad, small_grad]
    results = [loss_sum, token_count, grad_norm]
    for master, moment, second, gradient in zip(masters, moments, seconds, gradients):
        results.extend(adamw_update(master, moment, second, gradient * factor))
    return tuple(results)


def solution(mesh):
    dp, mp = (mesh.shape["dp"], mesh.shape["mp"])
    sizes = {"da": dp // 2, "db": 2, "y": mp // 2, "c": 2}
    inner = Mesh(
        mesh.devices.reshape(sizes["da"], sizes["db"], sizes["y"], sizes["c"]),
        ("da", "db", "y", "c"),
    )
    groups, parts = (("da", "db"), ("y", "c"))
    weight_specs = (P(groups, parts),) * 21 + (P(None, parts),) * 3 + (P(),) * 3
    in_specs = (P(groups + parts, None, None),) * 2 + (P(groups),) * 5 + weight_specs
    out_specs = (P(),) * 3 + weight_specs
    return jax.shard_map(
        partial(per_device, sizes),
        mesh=inner,
        in_specs=in_specs,
        out_specs=out_specs,
        check_vma=False,
    )
```

```python
from functools import partial
import math

import jax
import jax.numpy as jnp
from jax import lax
from jax.experimental import pallas as pl
from jax.experimental.pallas import tpu as pltpu
from jax.sharding import Mesh
from jax.sharding import PartitionSpec as P

D = 1152
H = 16
HD = 72
FF = 4608
FREQ = 256
NCLS = 1000
GRID = 16
NB = 20
STEP = 10
TOKS = 256
REL = 62


norm_eps = 1e-06
beta_one = 0.9
beta_two = 0.999
learn_rate = 0.04
weight_decay = 0.01
adam_eps = 1e-12
clip_level = 0.001
highest = lax.Precision.HIGHEST


def layout():
    entries = [
        ("embed_bias", D),
        ("time_bias_one", D),
        ("time_bias_two", D),
        ("cond_bias", 10 * D),
        ("query_bias", D),
        ("value_bias", D),
        ("out_bias", D),
        ("fc1_bias", FF),
        ("fc2_bias", D),
        ("final_bias", 32),
        ("embed_weight", 16 * D),
        ("final_weight", 32 * D),
        ("rel_bias", H * REL),
    ]
    places = {}
    offset = 0
    for entry_name, length in entries:
        places[entry_name] = (offset, length)
        offset = offset + length
    return places


def patchify(field):
    images, channels = (field.shape[0], field.shape[1])
    shaped = field.reshape(images, channels, GRID, 2, GRID, 2)
    return shaped.transpose(0, 2, 4, 1, 3, 5).reshape(images, GRID * GRID, channels * 4)


def frequencies(moments_in):
    half_freq = FREQ // 2
    omegas = jnp.exp(-math.log(10000.0) * jnp.arange(half_freq, dtype=jnp.float32) / half_freq)
    angles = moments_in[:, None] * omegas[None, :]
    return jnp.concatenate([jnp.cos(angles), jnp.sin(angles)], 1)


def position_table():
    quarter = D // 4
    omegas = 1.0 / 10000.0 ** (jnp.arange(quarter, dtype=jnp.float32) / quarter)
    coords = jnp.arange(GRID, dtype=jnp.float32)
    row_angle = jnp.repeat(coords, GRID)[:, None] * omegas[None, :]
    col_angle = jnp.tile(coords, GRID)[:, None] * omegas[None, :]
    return jnp.concatenate(
        [jnp.sin(row_angle), jnp.cos(row_angle), jnp.sin(col_angle), jnp.cos(col_angle)], 1
    )


def offset_table():
    coords = jnp.arange(GRID)
    shifts = coords[:, None] - coords[None, :] + GRID - 1
    return (
        (shifts[None, :, :] == jnp.arange(2 * GRID - 1)[:, None, None])
        .astype(jnp.float32)
        .reshape(2 * GRID - 1, GRID * GRID)
    )


def layernorm_parts(values):
    center = values - jnp.mean(values, -1, keepdims=True)
    inverse = lax.rsqrt(jnp.mean(center * center, -1, keepdims=True) + norm_eps)
    return (center * inverse, inverse)


def column_of(modulation, index_col):
    return modulation[:, None, index_col * D : (index_col + 1) * D]


BIG = 58 * 1024 * 1024
SCALE = 1.0 / math.sqrt(HD)
JOIN = 3 * HD
ROOT = math.sqrt(2.0 / math.pi)
CUBE = 0.044715
SCALE_TWO = SCALE / math.log(2.0)


def dot_nn(left, right):
    return jnp.dot(left, right, preferred_element_type=jnp.float32)


def dot_nt(left, right):
    return lax.dot_general(
        left, right, (((1,), (1,)), ((), ())), preferred_element_type=jnp.float32
    )


def dot_tn(left, right):
    return lax.dot_general(
        left, right, (((0,), (0,)), ((), ())), preferred_element_type=jnp.float32
    )


def params(*order):
    return pltpu.CompilerParams(
        dimension_semantics=order, vmem_limit_bytes=BIG
    )


def cost(flops, moved, exps=0):
    return pl.CostEstimate(flops=int(flops), bytes_accessed=int(moved), transcendentals=int(exps))


def block_of(weight_ref, width):
    block = weight_ref[:, 0, :, :width]
    return block.reshape(block.shape[0] * block.shape[1], width)


def weight_spec(weights, width, place):
    groups, _, rows, _ = weights.shape
    return pl.BlockSpec((groups, 1, rows, width), lambda m, i: (0, m, 0, place))


def norm_of(values):
    center = values - jnp.mean(values, -1, keepdims=True)
    inverse = lax.rsqrt(jnp.mean(center * center, -1, keepdims=True) + norm_eps)
    return center * inverse, inverse


def norm_back(normed, inverse, gradient):
    return (
        gradient
        - jnp.mean(gradient, -1, keepdims=True)
        - normed * jnp.mean(gradient * normed, -1, keepdims=True)
    ) * inverse


def total_rows(values):
    return jnp.sum(values, 0, keepdims=True)


def ordered(kernel, count, extra):
    def run(*refs):
        return kernel(*refs[:count], *refs[count + extra :])

    return run


def unread(others):
    return [pl.BlockSpec(memory_space=pl.ANY) for _ in others]


def hold(m, last, i):
    return jnp.where(m == last, i, 0)


def attention_forward_kernel(
    width, first_ref, weight_ref, added_ref, table_ref, spots_ref, joined_ref, mixed_ref, total_ref
):
    heads = width // JOIN
    rows = dot_nn(first_ref[0], block_of(weight_ref, width)) + added_ref[0, 0]
    joined_ref[0, 0] = rows.astype(jnp.bfloat16)
    for head in range(heads):
        base = head * JOIN
        query = joined_ref[0, 0, :, base : base + HD]
        keys = joined_ref[0, 0, :, base + HD : base + 2 * HD]
        values = joined_ref[0, 0, :, base + 2 * HD : base + 3 * HD]
        scores = SCALE_TWO * dot_nt(
            jnp.concatenate([keys, spots_ref[...]], 1), jnp.concatenate([query, table_ref[head]], 1)
        )
        largest = jnp.max(scores, 0, keepdims=True)
        grown = jnp.exp2(scores - largest)
        total = jnp.sum(grown, 0, keepdims=True)
        prob = (grown * (1.0 / total)).astype(jnp.bfloat16)
        mixed_ref[0, 0, :, head * HD : (head + 1) * HD] = dot_tn(prob, values).astype(jnp.bfloat16)
        total_ref[0, 0, head : head + 1, :] = largest + jnp.log2(total)


def attention_forward(first_in, weights, lanes, width, added, table, spots):
    images = first_in.shape[0]
    parts = weights.shape[1]
    heads = width // JOIN
    return pl.pallas_call(
        partial(attention_forward_kernel, width),
        grid=(parts, images),
        in_specs=[
            pl.BlockSpec((1, TOKS, D), lambda m, i: (i, 0, 0)),
            weight_spec(weights, lanes, 1),
            pl.BlockSpec((1, 1, 1, width), lambda m, i: (m, i, 0, 0)),
            pl.BlockSpec((heads, TOKS, 4 * GRID), lambda m, i: (m, 0, 0)),
            pl.BlockSpec((TOKS, 4 * GRID), lambda m, i: (0, 0)),
        ],
        out_specs=[
            pl.BlockSpec((1, 1, TOKS, width), lambda m, i: (m, i, 0, 0)),
            pl.BlockSpec((1, 1, TOKS, heads * HD), lambda m, i: (m, i, 0, 0)),
            pl.BlockSpec((1, 1, heads, TOKS), lambda m, i: (m, i, 0, 0)),
        ],
        out_shape=[
            jax.ShapeDtypeStruct((parts, images, TOKS, width), jnp.bfloat16),
            jax.ShapeDtypeStruct((parts, images, TOKS, heads * HD), jnp.bfloat16),
            jax.ShapeDtypeStruct((parts, images, heads, TOKS), jnp.float32),
        ],
        cost_estimate=cost(images * (2 * TOKS * D * 3 * D + H * 4 * TOKS * TOKS * 128), 3e7),
        compiler_params=params("arbitrary", "arbitrary"),
        name="attention_forward",
    )(first_in, weights, added, table, spots)


def attention_backward_kernel(
    branch_grad_ref,
    weight_ref,
    joined_ref,
    total_ref,
    table_ref,
    spots_ref,
    grad_ref,
    column_ref,
    shift_ref,
    mixed_grad_ref,
):
    heads = shift_ref.shape[0]

    @pl.when(pl.program_id(1) == 0)
    def start():
        shift_ref[...] = jnp.zeros_like(shift_ref)

    mixed_grad_ref[...] = dot_nn(
        branch_grad_ref[0], block_of(weight_ref, heads * HD)
    ).astype(jnp.bfloat16)
    for head in range(heads):
        base = head * JOIN
        query = joined_ref[0, 0, :, base : base + HD]
        keys = joined_ref[0, 0, :, base + HD : base + 2 * HD]
        values = joined_ref[0, 0, :, base + 2 * HD : base + 3 * HD]
        mixed_grad = mixed_grad_ref[:, head * HD : (head + 1) * HD]
        wide = jnp.concatenate([keys, spots_ref[...]], 1)
        scores = SCALE_TWO * dot_nt(wide, jnp.concatenate([query, table_ref[head]], 1))
        exact = jnp.exp2(scores - total_ref[0, 0, head : head + 1, :])
        value_grad = dot_nn(exact.astype(jnp.bfloat16), mixed_grad)
        prob_grad = dot_nt(values, mixed_grad)
        shared = jnp.sum(exact * prob_grad, 0, keepdims=True)
        score_grad = (exact * (prob_grad - shared)).astype(jnp.bfloat16)
        key_grad = dot_nn(score_grad, query) * SCALE
        query_wide = dot_tn(score_grad, wide[:, : HD + 2 * GRID])
        shift_ref[head] += query_wide
        grad_ref[0, 0, :, base : base + HD] = (query_wide[:, :HD] * SCALE).astype(jnp.bfloat16)
        grad_ref[0, 0, :, base + HD : base + 2 * HD] = key_grad.astype(jnp.bfloat16)
        grad_ref[0, 0, :, base + 2 * HD : base + 3 * HD] = value_grad.astype(jnp.bfloat16)
    column_ref[0, 0] = dot_nn(jnp.ones((8, TOKS), jnp.bfloat16), grad_ref[0, 0])


def attention_backward(branch_grad, weights, joined_rows, total, table, spots, others):
    parts, images, _, width = joined_rows.shape
    heads = width // JOIN
    wide = HD + 2 * GRID
    return pl.pallas_call(
        ordered(attention_backward_kernel, 6, len(others)),
        grid=(parts, images),
        in_specs=[
            pl.BlockSpec((1, TOKS, D), lambda m, i: (i, 0, 0)),
            weight_spec(weights, weights.shape[3], 0),
            pl.BlockSpec((1, 1, TOKS, width), lambda m, i: (m, i, 0, 0)),
            pl.BlockSpec((1, 1, heads, TOKS), lambda m, i: (m, i, 0, 0)),
            pl.BlockSpec((heads, TOKS, 4 * GRID), lambda m, i: (m, 0, 0)),
            pl.BlockSpec((TOKS, 4 * GRID), lambda m, i: (0, 0)),
            *unread(others),
        ],
        out_specs=[
            pl.BlockSpec((1, 1, TOKS, width), lambda m, i: (m, i, 0, 0)),
            pl.BlockSpec((1, 1, 8, width), lambda m, i: (m, i, 0, 0)),
            pl.BlockSpec((heads, TOKS, wide), lambda m, i: (m, 0, 0)),
        ],
        out_shape=[
            jax.ShapeDtypeStruct((parts, images, TOKS, width), jnp.bfloat16),
            jax.ShapeDtypeStruct((parts, images, 8, width), jnp.float32),
            jax.ShapeDtypeStruct((parts * heads, TOKS, wide), jnp.float32),
        ],
        scratch_shapes=[pltpu.VMEM((TOKS, heads * HD), jnp.bfloat16)],
        cost_estimate=cost(images * (2 * TOKS * D * D + H * 10 * TOKS * TOKS * 128), 5e7),
        compiler_params=params("arbitrary", "arbitrary"),
        name="attention_backward",
    )(branch_grad, weights, joined_rows, total, table, spots, *others)


def mixback_kernel(mixed_ref, weight_ref, stream_ref, mods_ref, bias_ref, branch_ref, one_ref, second_ref):
    parts, width = mixed_ref.shape[0], mixed_ref.shape[3]
    total = bias_ref[...]
    for part in range(parts):
        block = weight_ref[:, part]
        total = total + dot_nt(
            mixed_ref[part, 0], block.reshape(block.shape[0] * block.shape[1], width)
        )
    branch_ref[0] = total.astype(jnp.bfloat16)
    stream = stream_ref[0] + mods_ref[0, 2:3] * total
    one_ref[0] = stream
    normed, _ = norm_of(stream)
    second_ref[0] = (normed * (1.0 + mods_ref[0, 4:5]) + mods_ref[0, 3:4]).astype(jnp.bfloat16)


def mixback_forward(mixed, weights, stream, mods, bias):
    parts, images, _, width = mixed.shape
    tile = pl.BlockSpec((1, TOKS, D), lambda i: (i, 0, 0))
    return pl.pallas_call(
        mixback_kernel,
        grid=(images,),
        in_specs=[
            pl.BlockSpec((parts, 1, TOKS, width), lambda i: (0, i, 0, 0)),
            pl.BlockSpec(weights.shape, lambda i: (0, 0, 0, 0)),
            tile,
            pl.BlockSpec((1, 8, D), lambda i: (i, 0, 0)),
            pl.BlockSpec((1, D), lambda i: (0, 0)),
        ],
        out_specs=[tile, tile, tile],
        out_shape=[
            jax.ShapeDtypeStruct((images, TOKS, D), jnp.bfloat16),
            jax.ShapeDtypeStruct((images, TOKS, D), jnp.float32),
            jax.ShapeDtypeStruct((images, TOKS, D), jnp.bfloat16),
        ],
        cost_estimate=cost(images * 2 * TOKS * D * D, images * TOKS * D * 14),
        compiler_params=params("arbitrary"),
        name="mixback_forward",
    )(mixed, weights, stream, mods, bias)


def expand_kernel(width, second_ref, expand_ref, bias_ref, active_ref, slope_ref):
    hidden = dot_nn(second_ref[0], block_of(expand_ref, width)) + bias_ref[0]
    square = hidden * hidden
    curve = jnp.tanh(hidden * (ROOT + ROOT * CUBE * square))
    half = 0.5 + 0.5 * curve
    active = hidden * half
    slope = half + active * (0.5 - 0.5 * curve) * (2.0 * ROOT + 6.0 * ROOT * CUBE * square)
    active_ref[0, 0] = active.astype(jnp.bfloat16)
    slope_ref[0, 0] = slope.astype(jnp.bfloat16)


def expand_forward(second_in, weights, lanes, width, bias):
    images = second_in.shape[0]
    parts = weights.shape[1]
    wide = pl.BlockSpec((1, 1, TOKS, width), lambda m, i: (m, i, 0, 0))
    return pl.pallas_call(
        partial(expand_kernel, width),
        grid=(parts, images),
        in_specs=[
            pl.BlockSpec((1, TOKS, D), lambda m, i: (i, 0, 0)),
            weight_spec(weights, lanes, 0),
            pl.BlockSpec((1, 1, width), lambda m, i: (m, 0, 0)),
        ],
        out_specs=[wide, wide],
        out_shape=[jax.ShapeDtypeStruct((parts, images, TOKS, width), jnp.bfloat16)] * 2,
        cost_estimate=cost(images * 2 * TOKS * D * FF, 3e7, images * TOKS * FF),
        compiler_params=params("arbitrary", "arbitrary"),
        name="expand_forward",
    )(second_in, weights, bias)


def narrow_kernel(
    width,
    active_ref,
    narrow_ref,
    stream_ref,
    mods_ref,
    bias_ref,
    final_ref,
    final_bias_ref,
    target_ref,
    valid_ref,
    two_ref,
    branch_grad_ref,
    sums_ref,
    final_grad_ref,
    output_ref,
    total_ref,
):
    m, i = pl.program_id(0), pl.program_id(1)
    last = pl.num_programs(0) - 1
    total = dot_nt(active_ref[0, 0], block_of(narrow_ref, width))

    @pl.when(m == 0)
    def begin_total():
        total_ref[i] = total

    @pl.when((m > 0) & (m < last))
    def add_total():
        total_ref[i] += total

    @pl.when(m == last)
    def finish():
        branch = total_ref[i] + total + bias_ref[...]
        gate = mods_ref[0, 5:6]
        scale = 1.0 + mods_ref[0, 7:8]
        normed, inverse = norm_of(stream_ref[0] + gate * branch)
        final_in = (normed * scale + mods_ref[0, 6:7]).astype(jnp.bfloat16)
        error = dot_nn(final_in, final_ref[...]) + final_bias_ref[...] - target_ref[0]
        valid = valid_ref[0, :, 0:1]
        loss = valid * (total_rows(jnp.mean(error * error, -1, keepdims=True)))
        output_grad = (valid * 2.0 * error / 32.0).astype(jnp.bfloat16)
        gradient = dot_nt(output_grad, final_ref[...])
        two = norm_back(normed, inverse, gradient * scale)
        two_ref[0] = two
        branch_grad = (gate * two).astype(jnp.bfloat16)
        branch_grad_ref[0] = branch_grad
        sums_ref[0, 0:1] = total_rows(gradient)
        sums_ref[0, 1:2] = total_rows(gradient * normed)
        sums_ref[0, 2:3] = total_rows(two * branch)
        sums_ref[0, 3:4] = total_rows(branch_grad.astype(jnp.float32))
        final_grad_ref[0] = dot_tn(output_grad, final_in)
        output_ref[0, 0:1] = total_rows(output_grad.astype(jnp.float32))
        output_ref[0, 1:2] = jnp.broadcast_to(loss, (1, 32))


def narrow_forward(active, weights, lanes, width, stream, mods, bias, final, final_bias, target, valid):
    parts, images = active.shape[:2]
    last = parts - 1
    late = pl.BlockSpec((1, TOKS, D), lambda m, i: (hold(m, last, i), 0, 0))
    fixed = lambda shape: pl.BlockSpec(shape, lambda m, i: (0,) * len(shape))
    lately = lambda shape: pl.BlockSpec((1,) + shape, lambda m, i: (hold(m, last, i), 0, 0))
    return pl.pallas_call(
        partial(narrow_kernel, width),
        grid=(parts, images),
        in_specs=[
            pl.BlockSpec((1, 1, TOKS, width), lambda m, i: (m, i, 0, 0)),
            weight_spec(weights, lanes, 0),
            late,
            pl.BlockSpec((1, 8, D), lambda m, i: (i, 0, 0)),
            fixed(bias.shape),
            fixed(final.shape),
            fixed(final_bias.shape),
            lately((TOKS, 32)),
            pl.BlockSpec((1, 1, 128), lambda m, i: (i, 0, 0)),
        ],
        out_specs=[late, late, lately((4, D)), lately((32, D)), lately((2, 32))],
        out_shape=[
            jax.ShapeDtypeStruct((images, TOKS, D), jnp.float32),
            jax.ShapeDtypeStruct((images, TOKS, D), jnp.bfloat16),
            jax.ShapeDtypeStruct((images, 4, D), jnp.float32),
            jax.ShapeDtypeStruct((images, 32, D), jnp.float32),
            jax.ShapeDtypeStruct((images, 2, 32), jnp.float32),
        ],
        scratch_shapes=[pltpu.VMEM((images, TOKS, D), jnp.float32)],
        cost_estimate=cost(images * 2 * TOKS * D * FF, 4e7),
        compiler_params=params("arbitrary", "arbitrary"),
        name="narrow_forward",
    )(active, weights, stream, mods, bias, final, final_bias, target, valid)


def feed_backward_kernel(
    width,
    branch_grad_ref,
    expand_ref,
    narrow_ref,
    slope_ref,
    two_ref,
    stream_ref,
    branch_ref,
    mods_ref,
    hidden_grad_ref,
    hidden_sum_ref,
    one_ref,
    first_grad_ref,
    sums_ref,
    total_ref,
):
    m, i = pl.program_id(0), pl.program_id(1)
    last = pl.num_programs(0) - 1
    chunk = width
    branch_grad = branch_grad_ref[0]

    @pl.when(i == 0)
    def start():
        hidden_sum_ref[...] = jnp.zeros_like(hidden_sum_ref)

    total = None
    for begin in range(0, width, chunk):
        columns = narrow_ref[:, 0, :, begin : begin + chunk]
        columns = columns.reshape(columns.shape[0] * columns.shape[1], chunk)
        active_grad = dot_nn(branch_grad, columns)
        hidden_grad = (
            active_grad * slope_ref[0, 0, :, begin : begin + chunk].astype(jnp.float32)
        ).astype(jnp.bfloat16)
        hidden_grad_ref[0, 0, :, begin : begin + chunk] = hidden_grad
        hidden_sum_ref[0, :, begin : begin + chunk] += total_rows(hidden_grad.astype(jnp.float32))
        columns = expand_ref[:, 0, :, begin : begin + chunk]
        columns = columns.reshape(columns.shape[0] * columns.shape[1], chunk)
        product = dot_nt(hidden_grad, columns)
        total = product if total is None else total + product

    @pl.when(m == 0)
    def begin_total():
        total_ref[i] = total

    @pl.when((m > 0) & (m < last))
    def add_total():
        total_ref[i] += total

    @pl.when(m == last)
    def finish():
        gradient = total_ref[i] + total
        normed, inverse = norm_of(stream_ref[0])
        one = two_ref[0] + norm_back(normed, inverse, gradient * (1.0 + mods_ref[0, 4:5]))
        one_ref[0] = one
        first_grad = (mods_ref[0, 2:3] * one).astype(jnp.bfloat16)
        first_grad_ref[0] = first_grad
        sums_ref[0, 0:1] = total_rows(gradient)
        sums_ref[0, 1:2] = total_rows(gradient * normed)
        sums_ref[0, 2:3] = total_rows(one * branch_ref[0].astype(jnp.float32))
        sums_ref[0, 3:4] = total_rows(first_grad.astype(jnp.float32))


def feed_backward(
    branch_grad, expand, narrow, lanes, width, slope, two, stream, branch, mods, others
):
    images = branch_grad.shape[0]
    parts = expand.shape[1]
    last = parts - 1
    tile = pl.BlockSpec((1, TOKS, D), lambda m, i: (i, 0, 0))
    late = pl.BlockSpec((1, TOKS, D), lambda m, i: (hold(m, last, i), 0, 0))
    wide = pl.BlockSpec((1, 1, TOKS, width), lambda m, i: (m, i, 0, 0))
    return pl.pallas_call(
        ordered(partial(feed_backward_kernel, width), 8, len(others)),
        grid=(parts, images),
        in_specs=[
            tile,
            weight_spec(expand, lanes, 0),
            weight_spec(narrow, lanes, 0),
            wide,
            late,
            late,
            late,
            pl.BlockSpec((1, 8, D), lambda m, i: (i, 0, 0)),
            *unread(others),
        ],
        out_specs=[
            wide,
            pl.BlockSpec((1, 1, width), lambda m, i: (m, 0, 0)),
            late,
            late,
            pl.BlockSpec((1, 4, D), lambda m, i: (hold(m, last, i), 0, 0)),
        ],
        out_shape=[
            jax.ShapeDtypeStruct((parts, images, TOKS, width), jnp.bfloat16),
            jax.ShapeDtypeStruct((parts, 1, width), jnp.float32),
            jax.ShapeDtypeStruct((images, TOKS, D), jnp.float32),
            jax.ShapeDtypeStruct((images, TOKS, D), jnp.bfloat16),
            jax.ShapeDtypeStruct((images, 4, D), jnp.float32),
        ],
        scratch_shapes=[pltpu.VMEM((images, TOKS, D), jnp.float32)],
        cost_estimate=cost(images * 4 * TOKS * D * FF, 6e7),
        compiler_params=params("arbitrary", "arbitrary"),
        name="feed_backward",
    )(branch_grad, expand, narrow, slope, two, stream, branch, mods, *others)


def joined_backward_kernel(
    width,
    grad_ref,
    weight_ref,
    one_ref,
    zero_ref,
    mods_ref,
    embed_ref,
    sums_ref,
    embed_grad_ref,
    total_ref,
):
    m, i = pl.program_id(0), pl.program_id(1)
    last = pl.num_programs(0) - 1
    total = dot_nt(grad_ref[0, 0], block_of(weight_ref, width))

    @pl.when(m == 0)
    def begin_total():
        total_ref[i] = total

    @pl.when((m > 0) & (m < last))
    def add_total():
        total_ref[i] += total

    @pl.when(m == last)
    def finish():
        gradient = total_ref[i] + total
        normed, inverse = norm_of(zero_ref[0])
        zero = one_ref[0] + norm_back(normed, inverse, gradient * (1.0 + mods_ref[0, 1:2]))
        sums_ref[0, 0:1] = total_rows(gradient)
        sums_ref[0, 1:2] = total_rows(gradient * normed)
        sums_ref[0, 2:3] = total_rows(zero)
        sums_ref[0, 3:4] = jnp.zeros((1, D), jnp.float32)
        upper = zero.astype(jnp.bfloat16)
        lower = (zero - upper.astype(jnp.float32)).astype(jnp.bfloat16)
        embed_grad_ref[0] = dot_tn(embed_ref[0], upper) + dot_tn(embed_ref[0], lower)


def joined_backward(grad_joined, weights, lanes, one, zero, mods, embed_in, others):
    parts, images, _, width = grad_joined.shape
    last = parts - 1
    late = pl.BlockSpec((1, TOKS, D), lambda m, i: (hold(m, last, i), 0, 0))
    return pl.pallas_call(
        ordered(partial(joined_backward_kernel, width), 6, len(others)),
        grid=(parts, images),
        in_specs=[
            pl.BlockSpec((1, 1, TOKS, width), lambda m, i: (m, i, 0, 0)),
            weight_spec(weights, lanes, 1),
            late,
            late,
            pl.BlockSpec((1, 8, D), lambda m, i: (i, 0, 0)),
            pl.BlockSpec((1, TOKS, 16), lambda m, i: (i, 0, 0)),
            *unread(others),
        ],
        out_specs=[
            pl.BlockSpec((1, 4, D), lambda m, i: (hold(m, last, i), 0, 0)),
            pl.BlockSpec((1, 16, D), lambda m, i: (hold(m, last, i), 0, 0)),
        ],
        out_shape=[
            jax.ShapeDtypeStruct((images, 4, D), jnp.float32),
            jax.ShapeDtypeStruct((images, 16, D), jnp.float32),
        ],
        scratch_shapes=[pltpu.VMEM((images, TOKS, D), jnp.float32)],
        cost_estimate=cost(images * 2 * TOKS * D * 3 * D, 3e7),
        compiler_params=params("arbitrary", "arbitrary"),
        name="joined_backward",
    )(grad_joined, weights, one, zero, mods, embed_in, *others)


def weight_gradient_kernel(widths, *refs):
    pairs = len(widths)
    inputs, gradients = refs[:pairs], refs[pairs : 2 * pairs]
    received_ref = refs[2 * pairs] if len(refs) == 3 * pairs + 2 else None
    grad_ref, turned = refs[-pairs - 1], refs[-pairs:]

    @pl.when((pl.program_id(0) == 0) & (pl.program_id(1) == 0))
    def turn():
        for turned_ref, inputs_ref in zip(turned, inputs):
            turned_ref[...] = inputs_ref[...].T

    begin = 0
    for width, turned_ref, gradient_ref in zip(widths, turned, gradients):
        product = dot_nn(turned_ref[...], gradient_ref[0])
        if received_ref is not None:
            product = product + received_ref[0, :, begin : begin + width].astype(jnp.float32)
        grad_ref[0, :, begin : begin + width] = product.astype(jnp.bfloat16)
        begin = begin + width


def weight_gradient(pairs, chosen, cores, received=None, others=()):
    rows = pairs[0][0].shape[0]
    parts = pairs[0][1].shape[0]
    widths = [gradient.shape[2] for _, gradient in pairs]
    width = sum(widths)
    chunks = 1
    pieces = [member // chunks for member in widths]
    count = parts // cores
    taken = 2 * len(pairs) + (received is not None)
    kernel = ordered(partial(weight_gradient_kernel, pieces), taken, len(others))
    out_spec = pl.BlockSpec((1, D, width // chunks), lambda y, k, chosen: (y, 0, k))
    in_specs = [pl.BlockSpec((rows, D), lambda y, k, chosen: (0, 0)) for _ in pairs] + [
        pl.BlockSpec((1, rows, piece), lambda y, k, chosen: (y * cores + chosen[0], 0, k))
        for piece in pieces
    ]
    operands = [member for member, _ in pairs] + [member for _, member in pairs]
    if received is not None:
        in_specs.append(out_spec)
        operands.append(received)
    return pl.pallas_call(
        lambda chosen_ref, *refs: kernel(*refs),
        grid_spec=pltpu.PrefetchScalarGridSpec(
            num_scalar_prefetch=1,
            grid=(count, chunks),
            in_specs=in_specs + unread(others),
            out_specs=out_spec,
            scratch_shapes=[pltpu.VMEM((D, rows), jnp.bfloat16) for _ in pairs],
        ),
        out_shape=jax.ShapeDtypeStruct((count, D, width), jnp.bfloat16),
        cost_estimate=cost(2 * rows * D * width * count, rows * (D + width * count) * 2),
        compiler_params=params("arbitrary", "arbitrary"),
        name="weight_gradient",
    )(chosen, *operands, *others)


def whole_gradient_kernel(inputs_ref, gradient_ref, grad_ref, turned_ref):
    @pl.when((pl.program_id(0) == 0) & (pl.program_id(1) == 0))
    def turn():
        turned_ref[...] = inputs_ref[...].T

    product = dot_nn(turned_ref[...], gradient_ref[0]).astype(jnp.bfloat16)
    groups, _, rows, width = grad_ref.shape
    grad_ref[:, 0] = product.reshape(groups, rows, width)


def whole_gradient(inputs, gradient, groups):
    rows = inputs.shape[0]
    parts, _, width = gradient.shape
    chunks = 3 if width % 384 == 0 else 1
    piece = width // chunks
    split = groups if (D // groups) % 16 == 0 else 1
    result = pl.pallas_call(
        whole_gradient_kernel,
        grid=(parts, chunks),
        in_specs=[
            pl.BlockSpec((rows, D), lambda m, k: (0, 0)),
            pl.BlockSpec((1, rows, piece), lambda m, k: (m, 0, k)),
        ],
        out_specs=pl.BlockSpec((split, 1, D // split, piece), lambda m, k: (0, m, 0, k)),
        out_shape=jax.ShapeDtypeStruct((split, parts, D // split, width), jnp.bfloat16),
        scratch_shapes=[pltpu.VMEM((D, rows), jnp.bfloat16)],
        cost_estimate=cost(2 * rows * D * width * parts, rows * (D + width * parts) * 2),
        compiler_params=params("arbitrary", "arbitrary"),
        name="whole_gradient",
    )(inputs, gradient)
    if split == 1:
        result = result.reshape(parts, groups, D // groups, width).transpose(1, 0, 2, 3)
    return result.reshape(groups * parts, D // groups, width)


def two_terms(values):
    upper = lax.reduce_precision(values, 8, 7)
    return upper.astype(jnp.bfloat16), (values - upper).astype(jnp.bfloat16)


def relative_tables(rel_table):
    rows = offset_table()
    span = 2 * GRID - 1
    along_rows = jnp.dot(rel_table[:, :span], rows, precision=highest).reshape(H, GRID, 1, GRID)
    along_cols = jnp.dot(rel_table[:, span:], rows, precision=highest).reshape(H, 1, GRID, GRID)
    full = (H, GRID, GRID, GRID)
    table = jnp.concatenate(
        [jnp.broadcast_to(along_rows, full), jnp.broadcast_to(along_cols, full)], 3
    ).reshape(H, TOKS, 2 * GRID) * math.sqrt(HD)
    return jnp.concatenate(two_terms(table), 2)


def spot_table():
    places = jnp.arange(TOKS)
    rows = (places[:, None] // GRID == jnp.arange(GRID)[None, :]).astype(jnp.bfloat16)
    cols = (places[:, None] % GRID == jnp.arange(GRID)[None, :]).astype(jnp.bfloat16)
    return jnp.concatenate([rows, cols, rows, cols], 1)


def relative_gradient(shifts):
    rows = offset_table()
    row_part = jnp.sum(shifts[:, :, :GRID].reshape(H, GRID, GRID, GRID), 2)
    col_part = jnp.sum(shifts[:, :, GRID:].reshape(H, GRID, GRID, GRID), 1)
    return jnp.concatenate(
        [
            jnp.dot(row_part.reshape(H, TOKS), rows.T, precision=highest),
            jnp.dot(col_part.reshape(H, TOKS), rows.T, precision=highest),
        ],
        1,
    ).reshape(H * REL)


def small_gather(values, axes, count):
    spread = jnp.broadcast_to(values[None], (count,) + values.shape)
    return lax.all_to_all(spread, axes, 0, 0, tiled=True)


def pick(values, index, dim):
    return lax.dynamic_index_in_dim(values, index, dim, keepdims=False)


def tie(*values):
    return lax.optimization_barrier(values)


def swap(values, axis):
    return lax.ppermute(values, axis, [(0, 1), (1, 0)])


class Exchange:
    def __init__(self, sizes, places):
        self.sizes, self.places = sizes, places
        self.chosen = places["c"].astype(jnp.int32).reshape(1)

    def gradient(self, pairs, others=()):
        self.sent = weight_gradient(pairs, 1 - self.chosen, self.sizes["c"], None, others)
        self.received = swap(self.sent, "c")

    def kept_gradient(self, pairs, others=()):
        return weight_gradient(pairs, self.chosen, self.sizes["c"], self.received, others)

    def prepare(self, values, dim, axis):
        size, index = self.sizes[axis], self.places[axis]
        if size == 2:
            return pick(values, 1 - index, dim), pick(values, index, dim)
        return jnp.moveaxis(values, dim, 0), None

    def launch_one(self, sent, axis):
        if self.sizes[axis] == 2:
            return swap(sent, axis)
        return lax.all_to_all(sent, axis, 0, 0, tiled=True)

    def open_first(self, kept):
        da, db, ny = (self.sizes[key] for key in ("da", "db", "y"))
        kept = kept.reshape(ny, da, db, D // (da * db), kept.shape[2])
        half = da // 2
        sent_a, own_a = self.prepare(kept[:, :half], 0, "y")
        sent_b, own_b = self.prepare(kept[:, half:], 2, "db")
        self.own, self.axes = (own_a, own_b), ("y", "db")
        self.sent = (sent_a, sent_b)

    def launch(self):
        self.arrived = tuple(map(self.launch_one, self.sent, self.axes))

    def close(self):
        def add(own, arrived):
            if own is None:
                return jnp.sum(arrived.astype(jnp.float32), 0).astype(jnp.bfloat16)
            return (own.astype(jnp.float32) + arrived.astype(jnp.float32)).astype(jnp.bfloat16)

        return tuple(map(add, self.own, self.arrived))

    def open_second(self):
        part_a, part_b = self.close()
        sent_a, own_a = self.prepare(part_a, 1, "db")
        sent_b, own_b = self.prepare(part_b, 0, "y")
        self.own, self.axes = (own_a, own_b), ("db", "y")
        self.sent = (sent_a, sent_b)

    def open_last(self):
        joint = jnp.concatenate(self.close(), 0)
        size, index = self.sizes["da"], self.places["da"]
        if size > 4:
            self.own, self.sent = None, (joint,)
            return
        self.own = pick(joint, index, 0)
        self.sent = tuple(pick(joint, (index + shift) % size, 0) for shift in range(1, size))

    def launch_last(self):
        size = self.sizes["da"]
        if self.own is None:
            self.arrived = (lax.all_to_all(self.sent[0], "da", 0, 0, tiled=True),)
            return
        self.arrived = tuple(
            lax.ppermute(sent, "da", [(place, (place + shift + 1) % size) for place in range(size)])
            for shift, sent in enumerate(self.sent)
        )

    def result(self):
        if self.own is None:
            return jnp.sum(self.arrived[0].astype(jnp.float32), 0)
        return sum((member.astype(jnp.float32) for member in self.arrived), self.own.astype(jnp.float32))


def lane_padded(values):
    width = values.shape[1]
    return jnp.pad(values, ((0, 0), (0, -width % 128)))


def in_parts(gathered, groups, parts):
    rows, width = gathered.shape[1:]
    blocks = gathered.reshape(groups, parts, rows, width)
    if rows % 16 == 0:
        return blocks
    return blocks.transpose(1, 0, 2, 3).reshape(1, parts, groups * rows, width)


def adamw_update(master, moment, second, gradient):
    first_new = beta_one * moment + (1.0 - beta_one) * gradient
    square_new = beta_two * second + (1.0 - beta_two) * gradient * gradient
    first_hat = first_new / (1.0 - beta_one**STEP)
    square_hat = square_new / (1.0 - beta_two**STEP)
    master_new = master - learn_rate * (
        first_hat / (jnp.sqrt(square_hat) + adam_eps) + weight_decay * master
    )
    return (first_new, square_new, master_new)


TOKEN_SMALLS = (
    "embed_bias",
    "query_bias",
    "value_bias",
    "out_bias",
    "fc1_bias",
    "fc2_bias",
    "final_bias",
    "embed_weight",
    "final_weight",
    "rel_bias",
)


def per_device(
    sizes,
    latents,
    noises,
    timesteps,
    labels,
    dropped,
    buckets,
    counts,
    *state,
):
    masters, moments, seconds = (state[0::3], state[1::3], state[2::3])
    (
        joined_weight,
        mixback_weight,
        expand_weight,
        narrow_weight,
        timeone_weight,
        timetwo_weight,
        modulator_weight,
        classes_weight,
        smalls_weight,
    ) = masters
    da, db, ny, nc = (sizes[key] for key in ("da", "db", "y", "c"))
    dp, mp = (da * db, ny * nc)
    dp_axes, mp_axes = (("da", "db"), ("y", "c"))
    all_axes = dp_axes + mp_axes
    places_now = {key: lax.axis_index(key) for key in ("da", "db", "y", "c")}
    dp_index = places_now["da"] * db + places_now["db"]
    mp_index = places_now["y"] * nc + places_now["c"]
    places = layout()
    zero_index = jnp.zeros((), jnp.int32)

    def small_piece(key_name):
        begin_at, length = places[key_name]
        return smalls_weight[begin_at : begin_at + length]

    own_images = latents.shape[0]
    group_size = timesteps.shape[0]
    images_all = dp * group_size
    row_width = timetwo_weight.shape[0]
    width_mp = timetwo_weight.shape[1]
    mod_width = modulator_weight.shape[1]

    joined_width, mixback_width = (joined_weight.shape[1], mixback_weight.shape[1])
    hidden_width = expand_weight.shape[1]
    shard_one = jnp.concatenate(
        [
            lane_padded(expand_weight),
            lane_padded(jnp.concatenate([joined_weight, mixback_weight], 1)),
        ],
        1,
    )
    first = in_parts(lax.all_gather(shard_one.astype(jnp.bfloat16), all_axes), dp, mp)
    narrow = in_parts(
        lax.all_gather(lane_padded(narrow_weight).astype(jnp.bfloat16), all_axes), dp, mp
    )
    lanes = narrow.shape[3]
    mixback = first[:, :, :, lanes + joined_width : lanes + joined_width + mixback_width]

    facts_own = jnp.concatenate([timesteps, labels, dropped, buckets, counts])
    first_words = timeone_weight.size
    packed = small_gather(
        jnp.concatenate(
            [
                timeone_weight.astype(jnp.bfloat16).reshape(first_words),
                (facts_own // 8).astype(jnp.bfloat16),
                (facts_own % 8).astype(jnp.bfloat16),
            ]
        ),
        dp_axes,
        dp,
    )
    facts = packed[:, first_words:].astype(jnp.float32).reshape(dp, 2, facts_own.shape[0])
    facts = 8.0 * facts[:, 0] + facts[:, 1]
    times_all = facts[:, :group_size].reshape(images_all)
    labels_all = facts[:, group_size : 2 * group_size].reshape(images_all)
    dropped_all = facts[:, 2 * group_size : 3 * group_size].reshape(images_all)
    buckets_all = facts[:, 3 * group_size]
    token_count = jnp.sum(facts[:, 3 * group_size + 1]) * TOKS
    time_first = packed[:, :first_words].reshape(FREQ, width_mp)
    bucket_width = float(1000 // NB)
    rows_in = frequencies(
        jnp.concatenate([times_all, buckets_all * bucket_width + 0.5 * bucket_width])
    ).astype(jnp.bfloat16)
    hidden_time = jnp.dot(
        rows_in, time_first, preferred_element_type=jnp.float32
    ) + lax.dynamic_slice_in_dim(small_piece("time_bias_one"), mp_index * width_mp, width_mp)
    hidden_act = jax.nn.silu(hidden_time).astype(jnp.bfloat16)
    embed_part = dot_nt(hidden_act, timetwo_weight.astype(jnp.bfloat16))
    class_index = jnp.where(dropped_all > 0, float(NCLS), labels_all)
    onehot = (class_index[:, None] == jnp.arange(NCLS + 1, dtype=jnp.float32)[None, :]).astype(
        jnp.bfloat16
    )
    label_cols = jnp.dot(
        onehot, classes_weight.astype(jnp.bfloat16), preferred_element_type=jnp.float32
    )
    column_at = dp_index * row_width
    owner = column_at // width_mp
    label_part = lax.dynamic_slice_in_dim(label_cols, column_at - owner * width_mp, row_width, 1)
    label_part = jnp.where(mp_index == owner, label_part, 0.0)
    condition = jnp.sum(
        small_gather(
            jnp.concatenate([embed_part[:images_all] + label_part, embed_part[images_all:]], 0),
            mp_axes,
            mp,
        ),
        0,
    ) + lax.dynamic_slice_in_dim(small_piece("time_bias_two"), column_at, row_width)
    cond_act = jax.nn.silu(condition).astype(jnp.bfloat16)
    modulator = modulator_weight.astype(jnp.bfloat16)
    global_cols = mp_index * mod_width + jnp.arange(mod_width)
    mods_part = jnp.dot(cond_act, modulator, preferred_element_type=jnp.float32)
    outgoing = jnp.where(
        global_cols < 8 * D,
        mods_part[:images_all].reshape(dp, group_size, mod_width),
        mods_part[images_all:].reshape(dp, 1, mod_width),
    ).astype(jnp.bfloat16)
    incoming = lax.all_to_all(
        outgoing.reshape(dp * mp, own_images, mod_width), all_axes, 0, 0, tiled=True
    ).reshape(dp, mp, own_images, mod_width)
    modulation = jnp.sum(incoming.astype(jnp.float32), 0).transpose(1, 0, 2).reshape(
        own_images, 10 * D
    ) + small_piece("cond_bias")

    own_times = lax.dynamic_slice_in_dim(timesteps, mp_index * own_images, own_images)
    slot_index = mp_index * own_images + jnp.arange(own_images)
    valid_flags = (slot_index >= group_size - counts[0]).astype(jnp.float32)
    time_frac = (own_times.astype(jnp.float32) + 1.0) / 1000.0
    alpha_scale = jnp.cos(0.5 * math.pi * time_frac)[:, None, None]
    sigma_scale = jnp.sin(0.5 * math.pi * time_frac)[:, None, None]
    noisy_all = patchify(alpha_scale * latents + sigma_scale * noises)
    target = patchify(jnp.concatenate([alpha_scale * noises - sigma_scale * latents, noises], 1))
    embed_weight = small_piece("embed_weight").reshape(16, D)
    final_weight = small_piece("final_weight").reshape(D, 32)
    table = relative_tables(small_piece("rel_bias").reshape(H, REL))
    spots = spot_table()
    images = own_images
    rows_all = images * TOKS
    mods = modulation[:, : 8 * D].reshape(images, 8, D)

    embed_in = noisy_all.astype(jnp.bfloat16)
    stream_zero = (
        jnp.einsum(
            "ntc,cd->ntd",
            embed_in,
            embed_weight.astype(jnp.bfloat16),
            preferred_element_type=jnp.float32,
        )
        + small_piece("embed_bias")
        + position_table()
    )
    normed_a, _ = layernorm_parts(stream_zero)
    first_in = (
        normed_a * (1.0 + column_of(modulation, 1)) + column_of(modulation, 0)
    ).astype(jnp.bfloat16)
    added = jnp.stack(
        [
            (small_piece("query_bias") + modulation[:, 8 * D : 9 * D]).reshape(images, H, HD),
            jnp.zeros((images, H, HD), jnp.float32),
            (small_piece("value_bias") + modulation[:, 9 * D :]).reshape(images, H, HD),
        ],
        2,
    )
    added = added.reshape(images, mp, joined_width).transpose(1, 0, 2)[:, :, None]
    joined_rows, mixed, log_total = attention_forward(
        first_in, first, lanes, joined_width, added, table, spots
    )
    branch, stream_one, second_in = mixback_forward(
        mixed, mixback, stream_zero, mods, small_piece("out_bias")[None]
    )
    timetwo_narrow, second_in = tie(timetwo_weight.astype(jnp.bfloat16), second_in)
    time_second_all = small_gather(timetwo_narrow, dp_axes, dp)
    active, slope = expand_forward(
        second_in, first, lanes, hidden_width, small_piece("fc1_bias").reshape(mp, 1, hidden_width)
    )
    grad_two, grad_branch_two, sums_c, final_grads, output_sums = narrow_forward(
        active,
        narrow,
        lanes,
        hidden_width,
        stream_one,
        mods,
        small_piece("fc2_bias")[None],
        final_weight.astype(jnp.bfloat16),
        small_piece("final_bias")[None],
        target,
        jnp.broadcast_to(valid_flags[:, None, None], (images, 1, 128)),
    )
    loss_part = jnp.sum(output_sums[:, 1, 0])
    time_second_all, grad_branch_two = tie(time_second_all, grad_branch_two)
    time_second_all = time_second_all.reshape(D, width_mp)

    def flat(values):
        return values.reshape(rows_all, D)

    def in_rows(values):
        return values.reshape(mp, rows_all, values.shape[3])

    narrow_sum, heads_sum = (Exchange(sizes, places_now) for _ in range(2))
    narrow_pairs = [(flat(grad_branch_two), in_rows(active))]
    narrow_sum.gradient(narrow_pairs)
    grad_hidden, hidden_sums, grad_one, grad_branch, sums_b = feed_backward(
        grad_branch_two,
        first,
        narrow,
        lanes,
        hidden_width,
        slope,
        grad_two,
        stream_one,
        branch,
        mods,
        [narrow_sum.sent],
    )
    expand_all = whole_gradient(flat(second_in), in_rows(grad_hidden), dp)
    expand_shard = lax.psum_scatter(expand_all, all_axes, scatter_dimension=0, tiled=True)[0]
    narrow_sum.open_first(narrow_sum.kept_gradient(narrow_pairs, [expand_all]))
    narrow_sum.launch()
    grad_joined, column_sums, shifts = attention_backward(
        grad_branch, mixback, joined_rows, log_total, table, spots, list(narrow_sum.sent)
    )
    heads_pairs = [(flat(first_in), in_rows(grad_joined)), (flat(grad_branch), in_rows(mixed))]
    narrow_sum.arrived, heads_first = tie(narrow_sum.arrived, grad_joined)
    narrow_sum.open_second()
    narrow_sum.launch()
    heads_sum.gradient(heads_pairs, list(narrow_sum.sent))
    sums_a, embed_grads = joined_backward(
        heads_first,
        first,
        lanes,
        grad_one,
        stream_zero,
        mods,
        embed_in,
        [heads_sum.sent],
    )
    sums = (
        column_sums[:, :, 0]
        .reshape(mp, images, H // mp, 3, HD)
        .transpose(3, 1, 0, 2, 4)
        .reshape(3, images, D)
    )
    mods_grads = jnp.concatenate(
        [
            sums_a[:, 0],
            sums_a[:, 1],
            sums_b[:, 2],
            sums_b[:, 0],
            sums_b[:, 1],
            sums_c[:, 2],
            sums_c[:, 0],
            sums_c[:, 1],
            sums[0],
            sums[2],
        ],
        1,
    ).astype(jnp.bfloat16)
    to_owners = mods_grads.reshape(own_images, mp, mod_width).transpose(1, 0, 2)
    returned = lax.all_to_all(
        jnp.broadcast_to(to_owners[None], (dp,) + to_owners.shape).reshape(
            dp * mp, own_images, mod_width
        ),
        all_axes,
        0,
        0,
        tiled=True,
    ).reshape(images_all, mod_width)
    heads_kept = heads_sum.kept_gradient(heads_pairs, [to_owners])
    narrow_sum.open_last()
    narrow_sum.sent, heads_kept = tie(narrow_sum.sent, heads_kept)
    narrow_sum.launch_last()
    returned, heads_kept, expand_shard = tie(returned, heads_kept, expand_shard)
    heads_sum.open_first(heads_kept)
    heads_sum.sent, returned = tie(heads_sum.sent, returned)
    heads_sum.launch()
    grad_small = {
        "embed_bias": jnp.sum(sums_a[:, 2], 0),
        "query_bias": jnp.sum(sums[0], 0),
        "value_bias": jnp.sum(sums[2], 0),
        "out_bias": jnp.sum(sums_b[:, 3], 0),
        "fc1_bias": hidden_sums.reshape(FF),
        "fc2_bias": jnp.sum(sums_c[:, 3], 0),
        "final_bias": jnp.sum(output_sums[:, 0], 0),
        "embed_weight": jnp.sum(embed_grads, 0).reshape(16 * D),
        "final_weight": jnp.sum(final_grads, 0).T.reshape(32 * D),
        "rel_bias": relative_gradient(shifts[:, :, HD:]),
    }

    is_image = (global_cols < 8 * D)[None, :]
    returned_wide = returned.astype(jnp.float32)
    cond_bias_grad = jnp.sum(returned_wide, 0)
    bucket_sums = jnp.where(
        is_image, 0.0, jnp.sum(returned_wide.reshape(dp, group_size, mod_width), 1)
    )

    def split_rows(image_rows, bucket_rows):
        upper, lower = two_terms(bucket_rows)
        return jnp.concatenate([image_rows.astype(jnp.bfloat16), upper, lower], 0)

    def double_rows(rows):
        return jnp.concatenate([rows, rows[images_all:]], 0)

    grad_mod = split_rows(jnp.where(is_image, returned, jnp.zeros_like(returned)), bucket_sums)
    modulator_grad = dot_tn(double_rows(cond_act), grad_mod)
    cond_part = dot_nt(grad_mod, modulator)
    cond_part = jnp.concatenate(
        [cond_part[:images_all], cond_part[images_all : images_all + dp] + cond_part[images_all + dp :]],
        0,
    )
    grad_act = small_gather(cond_part, mp_axes, mp)
    grad_act, narrow_sum.arrived = tie(grad_act, narrow_sum.arrived)
    grad_act = jnp.sum(grad_act, 0)
    _, pullback = jax.vjp(jax.nn.silu, condition)
    grad_cond_own = pullback(grad_act)[0]
    grad_embed_own = split_rows(grad_cond_own[:images_all], grad_cond_own[images_all:])
    timetwo_grad = dot_tn(grad_embed_own, double_rows(hidden_act))
    grad_cond = small_gather(grad_cond_own, dp_axes, dp)
    heads_sum.open_second()
    heads_sum.sent, grad_cond = tie(heads_sum.sent, grad_cond)
    heads_sum.launch()
    grad_cond = (
        grad_cond
        .transpose(1, 0, 2)
        .reshape(images_all + dp, D)
    )
    vector = jnp.concatenate([grad_small[key_name] for key_name in TOKEN_SMALLS])
    slice_length = -(-vector.shape[0] // (dp * mp))
    padded = jnp.pad(vector, (0, slice_length * dp * mp - vector.shape[0]))
    padded, grad_cond = tie(padded.reshape(dp * mp, slice_length), grad_cond)
    slice_sum = jnp.sum(lax.all_to_all(padded, all_axes, 0, 0, tiled=True), 0)
    grad_embed = split_rows(grad_cond[:images_all], grad_cond[images_all:])
    bias_two_grad = jnp.sum(grad_embed.astype(jnp.float32), 0)
    grad_hidden_act = dot_nn(grad_embed, time_second_all)
    grad_hidden_act = jnp.concatenate(
        [
            grad_hidden_act[:images_all],
            grad_hidden_act[images_all : images_all + dp] + grad_hidden_act[images_all + dp :],
        ],
        0,
    )
    _, pullback = jax.vjp(jax.nn.silu, hidden_time)
    grad_hidden_time = pullback(grad_hidden_act)[0]
    grad_hidden_time = split_rows(grad_hidden_time[:images_all], grad_hidden_time[images_all:])
    bias_one_grad = jnp.sum(grad_hidden_time.astype(jnp.float32), 0)
    rows_own = lax.dynamic_slice_in_dim(
        rows_in, dp_index * timeone_weight.shape[0], timeone_weight.shape[0], 1
    )
    timeone_grad = dot_tn(double_rows(rows_own), grad_hidden_time)
    label_rows = lax.dynamic_slice_in_dim(grad_cond[:images_all], mp_index * width_mp, width_mp, 1)
    label_upper, label_lower = two_terms(label_rows)
    class_raw = dot_tn(
        jnp.concatenate([onehot, onehot], 0), jnp.concatenate([label_upper, label_lower], 0)
    )

    heads_sum.open_last()
    heads_sum.launch_last()
    heads_grad, narrow_grad = (member.result() for member in (heads_sum, narrow_sum))
    expand_grad = expand_shard.astype(jnp.float32)
    joined_grad, mixback_grad = (heads_grad[:, :joined_width], heads_grad[:, joined_width:])
    mod_slice = -(-mod_width // dp)
    one_slice = -(-width_mp // dp)
    own_cond = lax.dynamic_slice_in_dim(
        jnp.pad(cond_bias_grad, (0, mod_slice * dp - mod_width)), dp_index * mod_slice, mod_slice
    )
    own_one = lax.dynamic_slice_in_dim(
        jnp.pad(bias_one_grad, (0, one_slice * dp - width_mp)), dp_index * one_slice, one_slice
    )
    own_two = lax.dynamic_slice_in_dim(bias_two_grad, column_at, row_width)

    owned = [
        member / token_count
        for member in (
            joined_grad,
            mixback_grad,
            expand_grad,
            narrow_grad,
            timeone_grad,
            timetwo_grad,
            modulator_grad,
        )
    ]
    class_grad = class_raw / token_count
    own_slices = jnp.concatenate([slice_sum, own_cond, own_one]) / token_count
    squares = sum((jnp.sum(member * member) for member in owned)) + jnp.sum(own_slices * own_slices)
    squares = squares + jnp.where(dp_index == 0, jnp.sum(class_grad * class_grad), 0.0)
    own_two = own_two / token_count
    squares = squares + jnp.where(mp_index == 0, jnp.sum(own_two * own_two), 0.0)
    final = small_gather(
        jnp.concatenate([own_slices, squares[None], loss_part[None]]), all_axes, dp * mp
    )
    ends = slice_length + mod_slice + one_slice
    grad_norm = jnp.sqrt(jnp.sum(final[:, ends]))
    loss_sum = jnp.sum(final[:, ends + 1])
    factor = jnp.minimum(1.0, clip_level / grad_norm)
    token_smalls = final[:, :slice_length].reshape(dp * mp * slice_length)
    pieces = {"time_bias_two": bias_two_grad / token_count}
    pieces["cond_bias"] = (
        final[:, slice_length : slice_length + mod_slice]
        .reshape(dp, mp, mod_slice)
        .transpose(1, 0, 2)
        .reshape(mp, dp * mod_slice)[:, :mod_width]
        .reshape(10 * D)
    )
    pieces["time_bias_one"] = (
        final[:, slice_length + mod_slice : ends]
        .reshape(dp, mp, one_slice)
        .transpose(1, 0, 2)
        .reshape(mp, dp * one_slice)[:, :width_mp]
        .reshape(D)
    )
    offset = 0
    for key_name in TOKEN_SMALLS:
        length = places[key_name][1]
        pieces[key_name] = token_smalls[offset : offset + length]
        offset = offset + length
    small_grad = jnp.concatenate([pieces[key_name] for key_name in places])
    gradients = owned + [class_grad, small_grad]
    results = [loss_sum, token_count, grad_norm]
    for master, moment, second, gradient in zip(masters, moments, seconds, gradients):
        results.extend(adamw_update(master, moment, second, gradient * factor))
    return tuple(results)


def solution(mesh):
    dp, mp = (mesh.shape["dp"], mesh.shape["mp"])
    sizes = {"da": dp // 2, "db": 2, "y": mp // 2, "c": 2}
    inner = Mesh(
        mesh.devices.reshape(sizes["da"], sizes["db"], sizes["y"], sizes["c"]),
        ("da", "db", "y", "c"),
    )
    groups, parts = (("da", "db"), ("y", "c"))
    weight_specs = (P(groups, parts),) * 21 + (P(None, parts),) * 3 + (P(),) * 3
    in_specs = (P(groups + parts, None, None),) * 2 + (P(groups),) * 5 + weight_specs
    out_specs = (P(),) * 3 + weight_specs
    return jax.shard_map(
        partial(per_device, sizes),
        mesh=inner,
        in_specs=in_specs,
        out_specs=out_specs,
        check_vma=False,
    )
```

```python
from functools import partial
import math

import jax
import jax.numpy as jnp
from jax import lax
from jax.experimental import pallas as pl
from jax.experimental.pallas import tpu as pltpu
from jax.sharding import Mesh
from jax.sharding import PartitionSpec as P

D = 1152
H = 16
HD = 72
FF = 4608
FREQ = 256
NCLS = 1000
GRID = 16
NB = 20
STEP = 10
TOKS = 256
REL = 62


norm_eps = 1e-06
beta_one = 0.9
beta_two = 0.999
learn_rate = 0.04
weight_decay = 0.01
adam_eps = 1e-12
clip_level = 0.001
highest = lax.Precision.HIGHEST


def layout():
    entries = [
        ("embed_bias", D),
        ("time_bias_one", D),
        ("time_bias_two", D),
        ("cond_bias", 10 * D),
        ("query_bias", D),
        ("value_bias", D),
        ("out_bias", D),
        ("fc1_bias", FF),
        ("fc2_bias", D),
        ("final_bias", 32),
        ("embed_weight", 16 * D),
        ("final_weight", 32 * D),
        ("rel_bias", H * REL),
    ]
    places = {}
    offset = 0
    for entry_name, length in entries:
        places[entry_name] = (offset, length)
        offset = offset + length
    return places


def patchify(field):
    images, channels = (field.shape[0], field.shape[1])
    shaped = field.reshape(images, channels, GRID, 2, GRID, 2)
    return shaped.transpose(0, 2, 4, 1, 3, 5).reshape(images, GRID * GRID, channels * 4)


def frequencies(moments_in):
    half_freq = FREQ // 2
    omegas = jnp.exp(-math.log(10000.0) * jnp.arange(half_freq, dtype=jnp.float32) / half_freq)
    angles = moments_in[:, None] * omegas[None, :]
    return jnp.concatenate([jnp.cos(angles), jnp.sin(angles)], 1)


def position_table():
    quarter = D // 4
    omegas = 1.0 / 10000.0 ** (jnp.arange(quarter, dtype=jnp.float32) / quarter)
    coords = jnp.arange(GRID, dtype=jnp.float32)
    row_angle = jnp.repeat(coords, GRID)[:, None] * omegas[None, :]
    col_angle = jnp.tile(coords, GRID)[:, None] * omegas[None, :]
    return jnp.concatenate(
        [jnp.sin(row_angle), jnp.cos(row_angle), jnp.sin(col_angle), jnp.cos(col_angle)], 1
    )


def offset_table():
    coords = jnp.arange(GRID)
    shifts = coords[:, None] - coords[None, :] + GRID - 1
    return (
        (shifts[None, :, :] == jnp.arange(2 * GRID - 1)[:, None, None])
        .astype(jnp.float32)
        .reshape(2 * GRID - 1, GRID * GRID)
    )


def layernorm_parts(values):
    center = values - jnp.mean(values, -1, keepdims=True)
    inverse = lax.rsqrt(jnp.mean(center * center, -1, keepdims=True) + norm_eps)
    return (center * inverse, inverse)


def column_of(modulation, index_col):
    return modulation[:, None, index_col * D : (index_col + 1) * D]


BIG = 58 * 1024 * 1024
SCALE = 1.0 / math.sqrt(HD)
JOIN = 3 * HD
ROOT = math.sqrt(2.0 / math.pi)
CUBE = 0.044715
SCALE_TWO = SCALE / math.log(2.0)


def dot_nn(left, right):
    return jnp.dot(left, right, preferred_element_type=jnp.float32)


def dot_nt(left, right):
    return lax.dot_general(
        left, right, (((1,), (1,)), ((), ())), preferred_element_type=jnp.float32
    )


def dot_tn(left, right):
    return lax.dot_general(
        left, right, (((0,), (0,)), ((), ())), preferred_element_type=jnp.float32
    )


def params(*order):
    return pltpu.CompilerParams(
        dimension_semantics=order, vmem_limit_bytes=BIG
    )


def cost(flops, moved, exps=0):
    return pl.CostEstimate(flops=int(flops), bytes_accessed=int(moved), transcendentals=int(exps))


def block_of(weight_ref, width):
    block = weight_ref[:, 0, :, :width]
    return block.reshape(block.shape[0] * block.shape[1], width)


def weight_spec(weights, width, place):
    groups, _, rows, _ = weights.shape
    return pl.BlockSpec((groups, 1, rows, width), lambda m, i: (0, m, 0, place))


def norm_of(values):
    center = values - jnp.mean(values, -1, keepdims=True)
    inverse = lax.rsqrt(jnp.mean(center * center, -1, keepdims=True) + norm_eps)
    return center * inverse, inverse


def norm_back(normed, inverse, gradient):
    return (
        gradient
        - jnp.mean(gradient, -1, keepdims=True)
        - normed * jnp.mean(gradient * normed, -1, keepdims=True)
    ) * inverse


def total_rows(values):
    return jnp.sum(values, 0, keepdims=True)


def ordered(kernel, count, extra):
    def run(*refs):
        return kernel(*refs[:count], *refs[count + extra :])

    return run


def unread(others):
    return [pl.BlockSpec(memory_space=pl.ANY) for _ in others]


def hold(m, last, i):
    return jnp.where(m == last, i, 0)


def attention_forward_kernel(
    width, first_ref, weight_ref, added_ref, table_ref, spots_ref, joined_ref, mixed_ref, total_ref
):
    heads = width // JOIN
    rows = dot_nn(first_ref[0], block_of(weight_ref, width)) + added_ref[0, 0]
    joined_ref[0, 0] = rows.astype(jnp.bfloat16)
    for head in range(heads):
        base = head * JOIN
        query = joined_ref[0, 0, :, base : base + HD]
        keys = joined_ref[0, 0, :, base + HD : base + 2 * HD]
        values = joined_ref[0, 0, :, base + 2 * HD : base + 3 * HD]
        scores = SCALE_TWO * dot_nt(
            jnp.concatenate([keys, spots_ref[...]], 1), jnp.concatenate([query, table_ref[head]], 1)
        )
        largest = jnp.max(scores, 0, keepdims=True)
        grown = jnp.exp2(scores - largest)
        total = jnp.sum(grown, 0, keepdims=True)
        prob = (grown * (1.0 / total)).astype(jnp.bfloat16)
        mixed_ref[0, 0, :, head * HD : (head + 1) * HD] = dot_tn(prob, values).astype(jnp.bfloat16)
        total_ref[0, 0, head : head + 1, :] = largest + jnp.log2(total)


def attention_forward(first_in, weights, lanes, width, added, table, spots):
    images = first_in.shape[0]
    parts = weights.shape[1]
    heads = width // JOIN
    return pl.pallas_call(
        partial(attention_forward_kernel, width),
        grid=(parts, images),
        in_specs=[
            pl.BlockSpec((1, TOKS, D), lambda m, i: (i, 0, 0)),
            weight_spec(weights, lanes, 1),
            pl.BlockSpec((1, 1, 1, width), lambda m, i: (m, i, 0, 0)),
            pl.BlockSpec((heads, TOKS, 4 * GRID), lambda m, i: (m, 0, 0)),
            pl.BlockSpec((TOKS, 4 * GRID), lambda m, i: (0, 0)),
        ],
        out_specs=[
            pl.BlockSpec((1, 1, TOKS, width), lambda m, i: (m, i, 0, 0)),
            pl.BlockSpec((1, 1, TOKS, heads * HD), lambda m, i: (m, i, 0, 0)),
            pl.BlockSpec((1, 1, heads, TOKS), lambda m, i: (m, i, 0, 0)),
        ],
        out_shape=[
            jax.ShapeDtypeStruct((parts, images, TOKS, width), jnp.bfloat16),
            jax.ShapeDtypeStruct((parts, images, TOKS, heads * HD), jnp.bfloat16),
            jax.ShapeDtypeStruct((parts, images, heads, TOKS), jnp.float32),
        ],
        cost_estimate=cost(images * (2 * TOKS * D * 3 * D + H * 4 * TOKS * TOKS * 128), 3e7),
        compiler_params=params("arbitrary", "arbitrary"),
        name="attention_forward",
    )(first_in, weights, added, table, spots)


def attention_backward_kernel(
    branch_grad_ref,
    weight_ref,
    joined_ref,
    total_ref,
    table_ref,
    spots_ref,
    grad_ref,
    column_ref,
    shift_ref,
    mixed_grad_ref,
):
    heads = shift_ref.shape[0]

    @pl.when(pl.program_id(1) == 0)
    def start():
        shift_ref[...] = jnp.zeros_like(shift_ref)

    mixed_grad_ref[...] = dot_nn(
        branch_grad_ref[0], block_of(weight_ref, heads * HD)
    ).astype(jnp.bfloat16)
    for head in range(heads):
        base = head * JOIN
        query = joined_ref[0, 0, :, base : base + HD]
        keys = joined_ref[0, 0, :, base + HD : base + 2 * HD]
        values = joined_ref[0, 0, :, base + 2 * HD : base + 3 * HD]
        mixed_grad = mixed_grad_ref[:, head * HD : (head + 1) * HD]
        wide = jnp.concatenate([keys, spots_ref[...]], 1)
        scores = SCALE_TWO * dot_nt(wide, jnp.concatenate([query, table_ref[head]], 1))
        exact = jnp.exp2(scores - total_ref[0, 0, head : head + 1, :])
        value_grad = dot_nn(exact.astype(jnp.bfloat16), mixed_grad)
        prob_grad = dot_nt(values, mixed_grad)
        shared = jnp.sum(exact * prob_grad, 0, keepdims=True)
        score_grad = (exact * (prob_grad - shared)).astype(jnp.bfloat16)
        key_grad = dot_nn(score_grad, query) * SCALE
        query_wide = dot_tn(score_grad, wide[:, : HD + 2 * GRID])
        shift_ref[head] += query_wide
        grad_ref[0, 0, :, base : base + HD] = (query_wide[:, :HD] * SCALE).astype(jnp.bfloat16)
        grad_ref[0, 0, :, base + HD : base + 2 * HD] = key_grad.astype(jnp.bfloat16)
        grad_ref[0, 0, :, base + 2 * HD : base + 3 * HD] = value_grad.astype(jnp.bfloat16)
    column_ref[0, 0] = dot_nn(jnp.ones((8, TOKS), jnp.bfloat16), grad_ref[0, 0])


def attention_backward(branch_grad, weights, joined_rows, total, table, spots, others):
    parts, images, _, width = joined_rows.shape
    heads = width // JOIN
    wide = HD + 2 * GRID
    return pl.pallas_call(
        ordered(attention_backward_kernel, 6, len(others)),
        grid=(parts, images),
        in_specs=[
            pl.BlockSpec((1, TOKS, D), lambda m, i: (i, 0, 0)),
            weight_spec(weights, weights.shape[3], 0),
            pl.BlockSpec((1, 1, TOKS, width), lambda m, i: (m, i, 0, 0)),
            pl.BlockSpec((1, 1, heads, TOKS), lambda m, i: (m, i, 0, 0)),
            pl.BlockSpec((heads, TOKS, 4 * GRID), lambda m, i: (m, 0, 0)),
            pl.BlockSpec((TOKS, 4 * GRID), lambda m, i: (0, 0)),
            *unread(others),
        ],
        out_specs=[
            pl.BlockSpec((1, 1, TOKS, width), lambda m, i: (m, i, 0, 0)),
            pl.BlockSpec((1, 1, 8, width), lambda m, i: (m, i, 0, 0)),
            pl.BlockSpec((heads, TOKS, wide), lambda m, i: (m, 0, 0)),
        ],
        out_shape=[
            jax.ShapeDtypeStruct((parts, images, TOKS, width), jnp.bfloat16),
            jax.ShapeDtypeStruct((parts, images, 8, width), jnp.float32),
            jax.ShapeDtypeStruct((parts * heads, TOKS, wide), jnp.float32),
        ],
        scratch_shapes=[pltpu.VMEM((TOKS, heads * HD), jnp.bfloat16)],
        cost_estimate=cost(images * (2 * TOKS * D * D + H * 10 * TOKS * TOKS * 128), 5e7),
        compiler_params=params("arbitrary", "arbitrary"),
        name="attention_backward",
    )(branch_grad, weights, joined_rows, total, table, spots, *others)


def mixback_kernel(mixed_ref, weight_ref, stream_ref, mods_ref, bias_ref, branch_ref, one_ref, second_ref):
    parts, width = mixed_ref.shape[0], mixed_ref.shape[3]
    total = bias_ref[...]
    for part in range(parts):
        block = weight_ref[:, part]
        total = total + dot_nt(
            mixed_ref[part, 0], block.reshape(block.shape[0] * block.shape[1], width)
        )
    branch_ref[0] = total.astype(jnp.bfloat16)
    stream = stream_ref[0] + mods_ref[0, 2:3] * total
    one_ref[0] = stream
    normed, _ = norm_of(stream)
    second_ref[0] = (normed * (1.0 + mods_ref[0, 4:5]) + mods_ref[0, 3:4]).astype(jnp.bfloat16)


def mixback_forward(mixed, weights, stream, mods, bias):
    parts, images, _, width = mixed.shape
    tile = pl.BlockSpec((1, TOKS, D), lambda i: (i, 0, 0))
    return pl.pallas_call(
        mixback_kernel,
        grid=(images,),
        in_specs=[
            pl.BlockSpec((parts, 1, TOKS, width), lambda i: (0, i, 0, 0)),
            pl.BlockSpec(weights.shape, lambda i: (0, 0, 0, 0)),
            tile,
            pl.BlockSpec((1, 8, D), lambda i: (i, 0, 0)),
            pl.BlockSpec((1, D), lambda i: (0, 0)),
        ],
        out_specs=[tile, tile, tile],
        out_shape=[
            jax.ShapeDtypeStruct((images, TOKS, D), jnp.bfloat16),
            jax.ShapeDtypeStruct((images, TOKS, D), jnp.float32),
            jax.ShapeDtypeStruct((images, TOKS, D), jnp.bfloat16),
        ],
        cost_estimate=cost(images * 2 * TOKS * D * D, images * TOKS * D * 14),
        compiler_params=params("arbitrary"),
        name="mixback_forward",
    )(mixed, weights, stream, mods, bias)


def expand_kernel(width, second_ref, expand_ref, bias_ref, active_ref, slope_ref):
    hidden = dot_nn(second_ref[0], block_of(expand_ref, width)) + bias_ref[0]
    square = hidden * hidden
    curve = jnp.tanh(hidden * (ROOT + ROOT * CUBE * square))
    half = 0.5 + 0.5 * curve
    active = hidden * half
    slope = half + active * (0.5 - 0.5 * curve) * (2.0 * ROOT + 6.0 * ROOT * CUBE * square)
    active_ref[0, 0] = active.astype(jnp.bfloat16)
    slope_ref[0, 0] = slope.astype(jnp.bfloat16)


def expand_forward(second_in, weights, lanes, width, bias):
    images = second_in.shape[0]
    parts = weights.shape[1]
    wide = pl.BlockSpec((1, 1, TOKS, width), lambda m, i: (m, i, 0, 0))
    return pl.pallas_call(
        partial(expand_kernel, width),
        grid=(parts, images),
        in_specs=[
            pl.BlockSpec((1, TOKS, D), lambda m, i: (i, 0, 0)),
            weight_spec(weights, lanes, 0),
            pl.BlockSpec((1, 1, width), lambda m, i: (m, 0, 0)),
        ],
        out_specs=[wide, wide],
        out_shape=[jax.ShapeDtypeStruct((parts, images, TOKS, width), jnp.bfloat16)] * 2,
        cost_estimate=cost(images * 2 * TOKS * D * FF, 3e7, images * TOKS * FF),
        compiler_params=params("arbitrary", "arbitrary"),
        name="expand_forward",
    )(second_in, weights, bias)


def narrow_kernel(
    width,
    active_ref,
    narrow_ref,
    stream_ref,
    mods_ref,
    bias_ref,
    final_ref,
    final_bias_ref,
    target_ref,
    valid_ref,
    two_ref,
    branch_grad_ref,
    sums_ref,
    final_grad_ref,
    output_ref,
):
    total = None
    for part in range(active_ref.shape[0]):
        block = narrow_ref[:, part, :, :width]
        block = block.reshape(block.shape[0] * block.shape[1], width)
        product = dot_nt(active_ref[part, 0], block)
        total = product if total is None else total + product
    branch = total + bias_ref[...]
    gate = mods_ref[0, 5:6]
    scale = 1.0 + mods_ref[0, 7:8]
    normed, inverse = norm_of(stream_ref[0] + gate * branch)
    final_in = (normed * scale + mods_ref[0, 6:7]).astype(jnp.bfloat16)
    error = dot_nn(final_in, final_ref[...]) + final_bias_ref[...] - target_ref[0]
    valid = valid_ref[0, :, 0:1]
    loss = valid * (total_rows(jnp.mean(error * error, -1, keepdims=True)))
    output_grad = (valid * 2.0 * error / 32.0).astype(jnp.bfloat16)
    gradient = dot_nt(output_grad, final_ref[...])
    two = norm_back(normed, inverse, gradient * scale)
    two_ref[0] = two
    branch_grad = (gate * two).astype(jnp.bfloat16)
    branch_grad_ref[0] = branch_grad
    sums_ref[0, 0:1] = total_rows(gradient)
    sums_ref[0, 1:2] = total_rows(gradient * normed)
    sums_ref[0, 2:3] = total_rows(two * branch)
    sums_ref[0, 3:4] = total_rows(branch_grad.astype(jnp.float32))
    final_grad_ref[0] = dot_tn(output_grad, final_in)
    output_ref[0, 0:1] = total_rows(output_grad.astype(jnp.float32))
    output_ref[0, 1:2] = jnp.broadcast_to(loss, (1, 32))


def narrow_forward(active, weights, lanes, width, stream, mods, bias, final, final_bias, target, valid):
    parts, images = active.shape[:2]
    groups, _, rows, _ = weights.shape
    tile = pl.BlockSpec((1, TOKS, D), lambda i: (i, 0, 0))
    fixed = lambda shape: pl.BlockSpec(shape, lambda i: (0,) * len(shape))
    each = lambda shape: pl.BlockSpec((1,) + shape, lambda i: (i, 0, 0))
    return pl.pallas_call(
        partial(narrow_kernel, width),
        grid=(images,),
        in_specs=[
            pl.BlockSpec((parts, 1, TOKS, width), lambda i: (0, i, 0, 0)),
            pl.BlockSpec(
                (groups, parts, rows, lanes),
                lambda i: (0, 0, 0, 0),
                pipeline_mode=pl.Buffered(1),
            ),
            tile,
            each((8, D)),
            fixed(bias.shape),
            fixed(final.shape),
            fixed(final_bias.shape),
            each((TOKS, 32)),
            each((1, 128)),
        ],
        out_specs=[tile, tile, each((4, D)), each((32, D)), each((2, 32))],
        out_shape=[
            jax.ShapeDtypeStruct((images, TOKS, D), jnp.float32),
            jax.ShapeDtypeStruct((images, TOKS, D), jnp.bfloat16),
            jax.ShapeDtypeStruct((images, 4, D), jnp.float32),
            jax.ShapeDtypeStruct((images, 32, D), jnp.float32),
            jax.ShapeDtypeStruct((images, 2, 32), jnp.float32),
        ],
        cost_estimate=cost(images * 2 * TOKS * D * FF, 4e7),
        compiler_params=params("arbitrary"),
        name="narrow_forward",
    )(active, weights, stream, mods, bias, final, final_bias, target, valid)


def feed_backward_kernel(
    width,
    branch_grad_ref,
    expand_ref,
    narrow_ref,
    slope_ref,
    two_ref,
    stream_ref,
    branch_ref,
    mods_ref,
    hidden_grad_ref,
    hidden_sum_ref,
    one_ref,
    first_grad_ref,
    sums_ref,
    total_ref,
):
    m, i = pl.program_id(0), pl.program_id(1)
    last = pl.num_programs(0) - 1
    chunk = width
    branch_grad = branch_grad_ref[0]

    @pl.when(i == 0)
    def start():
        hidden_sum_ref[...] = jnp.zeros_like(hidden_sum_ref)

    total = None
    for begin in range(0, width, chunk):
        columns = narrow_ref[:, 0, :, begin : begin + chunk]
        columns = columns.reshape(columns.shape[0] * columns.shape[1], chunk)
        active_grad = dot_nn(branch_grad, columns)
        hidden_grad = (
            active_grad * slope_ref[0, 0, :, begin : begin + chunk].astype(jnp.float32)
        ).astype(jnp.bfloat16)
        hidden_grad_ref[0, 0, :, begin : begin + chunk] = hidden_grad
        hidden_sum_ref[0, :, begin : begin + chunk] += total_rows(hidden_grad.astype(jnp.float32))
        columns = expand_ref[:, 0, :, begin : begin + chunk]
        columns = columns.reshape(columns.shape[0] * columns.shape[1], chunk)
        product = dot_nt(hidden_grad, columns)
        total = product if total is None else total + product

    @pl.when(m == 0)
    def begin_total():
        total_ref[i] = total

    @pl.when((m > 0) & (m < last))
    def add_total():
        total_ref[i] += total

    @pl.when(m == last)
    def finish():
        gradient = total_ref[i] + total
        normed, inverse = norm_of(stream_ref[0])
        one = two_ref[0] + norm_back(normed, inverse, gradient * (1.0 + mods_ref[0, 4:5]))
        one_ref[0] = one
        first_grad = (mods_ref[0, 2:3] * one).astype(jnp.bfloat16)
        first_grad_ref[0] = first_grad
        sums_ref[0, 0:1] = total_rows(gradient)
        sums_ref[0, 1:2] = total_rows(gradient * normed)
        sums_ref[0, 2:3] = total_rows(one * branch_ref[0].astype(jnp.float32))
        sums_ref[0, 3:4] = total_rows(first_grad.astype(jnp.float32))


def feed_backward(
    branch_grad, expand, narrow, lanes, width, slope, two, stream, branch, mods, others
):
    images = branch_grad.shape[0]
    parts = expand.shape[1]
    last = parts - 1
    tile = pl.BlockSpec((1, TOKS, D), lambda m, i: (i, 0, 0))
    late = pl.BlockSpec((1, TOKS, D), lambda m, i: (hold(m, last, i), 0, 0))
    wide = pl.BlockSpec((1, 1, TOKS, width), lambda m, i: (m, i, 0, 0))
    return pl.pallas_call(
        ordered(partial(feed_backward_kernel, width), 8, len(others)),
        grid=(parts, images),
        in_specs=[
            tile,
            weight_spec(expand, lanes, 0),
            weight_spec(narrow, lanes, 0),
            wide,
            late,
            late,
            late,
            pl.BlockSpec((1, 8, D), lambda m, i: (i, 0, 0)),
            *unread(others),
        ],
        out_specs=[
            wide,
            pl.BlockSpec((1, 1, width), lambda m, i: (m, 0, 0)),
            late,
            late,
            pl.BlockSpec((1, 4, D), lambda m, i: (hold(m, last, i), 0, 0)),
        ],
        out_shape=[
            jax.ShapeDtypeStruct((parts, images, TOKS, width), jnp.bfloat16),
            jax.ShapeDtypeStruct((parts, 1, width), jnp.float32),
            jax.ShapeDtypeStruct((images, TOKS, D), jnp.float32),
            jax.ShapeDtypeStruct((images, TOKS, D), jnp.bfloat16),
            jax.ShapeDtypeStruct((images, 4, D), jnp.float32),
        ],
        scratch_shapes=[pltpu.VMEM((images, TOKS, D), jnp.float32)],
        cost_estimate=cost(images * 4 * TOKS * D * FF, 6e7),
        compiler_params=params("arbitrary", "arbitrary"),
        name="feed_backward",
    )(branch_grad, expand, narrow, slope, two, stream, branch, mods, *others)


def joined_backward_kernel(
    width, grad_ref, weight_ref, one_ref, zero_ref, mods_ref, embed_ref, sums_ref, embed_grad_ref
):
    gradient = None
    for part in range(grad_ref.shape[0]):
        block = weight_ref[:, part, :, :width]
        block = block.reshape(block.shape[0] * block.shape[1], width)
        product = dot_nt(grad_ref[part, 0], block)
        gradient = product if gradient is None else gradient + product
    normed, inverse = norm_of(zero_ref[0])
    zero = one_ref[0] + norm_back(normed, inverse, gradient * (1.0 + mods_ref[0, 1:2]))
    sums_ref[0, 0:1] = total_rows(gradient)
    sums_ref[0, 1:2] = total_rows(gradient * normed)
    sums_ref[0, 2:3] = total_rows(zero)
    sums_ref[0, 3:4] = jnp.zeros((1, D), jnp.float32)
    upper = zero.astype(jnp.bfloat16)
    lower = (zero - upper.astype(jnp.float32)).astype(jnp.bfloat16)
    embed_grad_ref[0] = dot_tn(embed_ref[0], upper) + dot_tn(embed_ref[0], lower)


def joined_backward(grad_joined, weights, lanes, one, zero, mods, embed_in, others):
    parts, images, _, width = grad_joined.shape
    groups, _, rows, _ = weights.shape
    tile = pl.BlockSpec((1, TOKS, D), lambda i: (i, 0, 0))
    return pl.pallas_call(
        ordered(partial(joined_backward_kernel, width), 6, len(others)),
        grid=(images,),
        in_specs=[
            pl.BlockSpec((parts, 1, TOKS, width), lambda i: (0, i, 0, 0)),
            pl.BlockSpec(
                (groups, parts, rows, lanes),
                lambda i: (0, 0, 0, 1),
                pipeline_mode=pl.Buffered(1),
            ),
            tile,
            tile,
            pl.BlockSpec((1, 8, D), lambda i: (i, 0, 0)),
            pl.BlockSpec((1, TOKS, 16), lambda i: (i, 0, 0)),
            *unread(others),
        ],
        out_specs=[
            pl.BlockSpec((1, 4, D), lambda i: (i, 0, 0)),
            pl.BlockSpec((1, 16, D), lambda i: (i, 0, 0)),
        ],
        out_shape=[
            jax.ShapeDtypeStruct((images, 4, D), jnp.float32),
            jax.ShapeDtypeStruct((images, 16, D), jnp.float32),
        ],
        cost_estimate=cost(images * 2 * TOKS * D * 3 * D, 3e7),
        compiler_params=params("arbitrary"),
        name="joined_backward",
    )(grad_joined, weights, one, zero, mods, embed_in, *others)


def weight_gradient_kernel(widths, *refs):
    pairs = len(widths)
    inputs, gradients = refs[:pairs], refs[pairs : 2 * pairs]
    received_ref = refs[2 * pairs] if len(refs) == 3 * pairs + 2 else None
    grad_ref, turned = refs[-pairs - 1], refs[-pairs:]

    @pl.when((pl.program_id(0) == 0) & (pl.program_id(1) == 0))
    def turn():
        for turned_ref, inputs_ref in zip(turned, inputs):
            turned_ref[...] = inputs_ref[...].T

    begin = 0
    for width, turned_ref, gradient_ref in zip(widths, turned, gradients):
        product = dot_nn(turned_ref[...], gradient_ref[0])
        if received_ref is not None:
            product = product + received_ref[0, :, begin : begin + width].astype(jnp.float32)
        grad_ref[0, :, begin : begin + width] = product.astype(jnp.bfloat16)
        begin = begin + width


def weight_gradient(pairs, chosen, cores, received=None, others=()):
    rows = pairs[0][0].shape[0]
    parts = pairs[0][1].shape[0]
    widths = [gradient.shape[2] for _, gradient in pairs]
    width = sum(widths)
    chunks = 1
    pieces = [member // chunks for member in widths]
    count = parts // cores
    taken = 2 * len(pairs) + (received is not None)
    kernel = ordered(partial(weight_gradient_kernel, pieces), taken, len(others))
    out_spec = pl.BlockSpec((1, D, width // chunks), lambda y, k, chosen: (y, 0, k))
    in_specs = [pl.BlockSpec((rows, D), lambda y, k, chosen: (0, 0)) for _ in pairs] + [
        pl.BlockSpec((1, rows, piece), lambda y, k, chosen: (y * cores + chosen[0], 0, k))
        for piece in pieces
    ]
    operands = [member for member, _ in pairs] + [member for _, member in pairs]
    if received is not None:
        in_specs.append(out_spec)
        operands.append(received)
    return pl.pallas_call(
        lambda chosen_ref, *refs: kernel(*refs),
        grid_spec=pltpu.PrefetchScalarGridSpec(
            num_scalar_prefetch=1,
            grid=(count, chunks),
            in_specs=in_specs + unread(others),
            out_specs=out_spec,
            scratch_shapes=[pltpu.VMEM((D, rows), jnp.bfloat16) for _ in pairs],
        ),
        out_shape=jax.ShapeDtypeStruct((count, D, width), jnp.bfloat16),
        cost_estimate=cost(2 * rows * D * width * count, rows * (D + width * count) * 2),
        compiler_params=params("arbitrary", "arbitrary"),
        name="weight_gradient",
    )(chosen, *operands, *others)


def whole_gradient_kernel(inputs_ref, gradient_ref, grad_ref, turned_ref):
    @pl.when((pl.program_id(0) == 0) & (pl.program_id(1) == 0))
    def turn():
        turned_ref[...] = inputs_ref[...].T

    product = dot_nn(turned_ref[...], gradient_ref[0]).astype(jnp.bfloat16)
    groups, _, rows, width = grad_ref.shape
    grad_ref[:, 0] = product.reshape(groups, rows, width)


def whole_gradient(inputs, gradient, groups):
    rows = inputs.shape[0]
    parts, _, width = gradient.shape
    chunks = 1
    piece = width // chunks
    split = groups if (D // groups) % 16 == 0 else 1
    result = pl.pallas_call(
        whole_gradient_kernel,
        grid=(parts, chunks),
        in_specs=[
            pl.BlockSpec((rows, D), lambda m, k: (0, 0)),
            pl.BlockSpec((1, rows, piece), lambda m, k: (m, 0, k)),
        ],
        out_specs=pl.BlockSpec((split, 1, D // split, piece), lambda m, k: (0, m, 0, k)),
        out_shape=jax.ShapeDtypeStruct((split, parts, D // split, width), jnp.bfloat16),
        scratch_shapes=[pltpu.VMEM((D, rows), jnp.bfloat16)],
        cost_estimate=cost(2 * rows * D * width * parts, rows * (D + width * parts) * 2),
        compiler_params=params("arbitrary", "arbitrary"),
        name="whole_gradient",
    )(inputs, gradient)
    if split == 1:
        result = result.reshape(parts, groups, D // groups, width).transpose(1, 0, 2, 3)
    return result.reshape(groups * parts, D // groups, width)


def two_terms(values):
    upper = lax.reduce_precision(values, 8, 7)
    return upper.astype(jnp.bfloat16), (values - upper).astype(jnp.bfloat16)


def relative_tables(rel_table):
    rows = offset_table()
    span = 2 * GRID - 1
    along_rows = jnp.dot(rel_table[:, :span], rows, precision=highest).reshape(H, GRID, 1, GRID)
    along_cols = jnp.dot(rel_table[:, span:], rows, precision=highest).reshape(H, 1, GRID, GRID)
    full = (H, GRID, GRID, GRID)
    table = jnp.concatenate(
        [jnp.broadcast_to(along_rows, full), jnp.broadcast_to(along_cols, full)], 3
    ).reshape(H, TOKS, 2 * GRID) * math.sqrt(HD)
    return jnp.concatenate(two_terms(table), 2)


def spot_table():
    places = jnp.arange(TOKS)
    rows = (places[:, None] // GRID == jnp.arange(GRID)[None, :]).astype(jnp.bfloat16)
    cols = (places[:, None] % GRID == jnp.arange(GRID)[None, :]).astype(jnp.bfloat16)
    return jnp.concatenate([rows, cols, rows, cols], 1)


def relative_gradient(shifts):
    rows = offset_table()
    row_part = jnp.sum(shifts[:, :, :GRID].reshape(H, GRID, GRID, GRID), 2)
    col_part = jnp.sum(shifts[:, :, GRID:].reshape(H, GRID, GRID, GRID), 1)
    return jnp.concatenate(
        [
            jnp.dot(row_part.reshape(H, TOKS), rows.T, precision=highest),
            jnp.dot(col_part.reshape(H, TOKS), rows.T, precision=highest),
        ],
        1,
    ).reshape(H * REL)


def small_gather(values, axes, count):
    spread = jnp.broadcast_to(values[None], (count,) + values.shape)
    return lax.all_to_all(spread, axes, 0, 0, tiled=True)


def pick(values, index, dim):
    return lax.dynamic_index_in_dim(values, index, dim, keepdims=False)


def tie(*values):
    return lax.optimization_barrier(values)


def swap(values, axis):
    return lax.ppermute(values, axis, [(0, 1), (1, 0)])


class Exchange:
    def __init__(self, sizes, places):
        self.sizes, self.places = sizes, places
        self.chosen = places["c"].astype(jnp.int32).reshape(1)

    def gradient(self, pairs, others=()):
        self.sent = weight_gradient(pairs, 1 - self.chosen, self.sizes["c"], None, others)
        self.received = swap(self.sent, "c")

    def kept_gradient(self, pairs, others=()):
        return weight_gradient(pairs, self.chosen, self.sizes["c"], self.received, others)

    def prepare(self, values, dim, axis):
        size, index = self.sizes[axis], self.places[axis]
        if size == 2:
            return pick(values, 1 - index, dim), pick(values, index, dim)
        return jnp.moveaxis(values, dim, 0), None

    def launch_one(self, sent, axis):
        if self.sizes[axis] == 2:
            return swap(sent, axis)
        return lax.all_to_all(sent, axis, 0, 0, tiled=True)

    def open_first(self, kept):
        da, db, ny = (self.sizes[key] for key in ("da", "db", "y"))
        kept = kept.reshape(ny, da, db, D // (da * db), kept.shape[2])
        half = da // 2
        sent_a, own_a = self.prepare(kept[:, :half], 0, "y")
        sent_b, own_b = self.prepare(kept[:, half:], 2, "db")
        self.own, self.axes = (own_a, own_b), ("y", "db")
        self.sent = (sent_a, sent_b)

    def launch(self):
        self.arrived = tuple(map(self.launch_one, self.sent, self.axes))

    def close(self):
        def add(own, arrived):
            if own is None:
                return jnp.sum(arrived.astype(jnp.float32), 0).astype(jnp.bfloat16)
            return (own.astype(jnp.float32) + arrived.astype(jnp.float32)).astype(jnp.bfloat16)

        return tuple(map(add, self.own, self.arrived))

    def open_second(self):
        part_a, part_b = self.close()
        sent_a, own_a = self.prepare(part_a, 1, "db")
        sent_b, own_b = self.prepare(part_b, 0, "y")
        self.own, self.axes = (own_a, own_b), ("db", "y")
        self.sent = (sent_a, sent_b)

    def open_last(self):
        joint = jnp.concatenate(self.close(), 0)
        size, index = self.sizes["da"], self.places["da"]
        if size > 4:
            self.own, self.sent = None, (joint,)
            return
        self.own = pick(joint, index, 0)
        self.sent = tuple(pick(joint, (index + shift) % size, 0) for shift in range(1, size))

    def launch_last(self):
        size = self.sizes["da"]
        if self.own is None:
            self.arrived = (lax.all_to_all(self.sent[0], "da", 0, 0, tiled=True),)
            return
        self.arrived = tuple(
            lax.ppermute(sent, "da", [(place, (place + shift + 1) % size) for place in range(size)])
            for shift, sent in enumerate(self.sent)
        )

    def result(self):
        if self.own is None:
            return jnp.sum(self.arrived[0].astype(jnp.float32), 0)
        return sum((member.astype(jnp.float32) for member in self.arrived), self.own.astype(jnp.float32))


def lane_padded(values):
    width = values.shape[1]
    return jnp.pad(values, ((0, 0), (0, -width % 128)))


def in_parts(gathered, groups, parts):
    rows, width = gathered.shape[1:]
    blocks = gathered.reshape(groups, parts, rows, width)
    if rows % 16 == 0:
        return blocks
    return blocks.transpose(1, 0, 2, 3).reshape(1, parts, groups * rows, width)


def adamw_update(master, moment, second, gradient):
    first_new = beta_one * moment + (1.0 - beta_one) * gradient
    square_new = beta_two * second + (1.0 - beta_two) * gradient * gradient
    first_hat = first_new / (1.0 - beta_one**STEP)
    square_hat = square_new / (1.0 - beta_two**STEP)
    master_new = master - learn_rate * (
        first_hat / (jnp.sqrt(square_hat) + adam_eps) + weight_decay * master
    )
    return (first_new, square_new, master_new)


TOKEN_SMALLS = (
    "embed_bias",
    "query_bias",
    "value_bias",
    "out_bias",
    "fc1_bias",
    "fc2_bias",
    "final_bias",
    "embed_weight",
    "final_weight",
    "rel_bias",
)


def per_device(
    sizes,
    latents,
    noises,
    timesteps,
    labels,
    dropped,
    buckets,
    counts,
    *state,
):
    masters, moments, seconds = (state[0::3], state[1::3], state[2::3])
    (
        joined_weight,
        mixback_weight,
        expand_weight,
        narrow_weight,
        timeone_weight,
        timetwo_weight,
        modulator_weight,
        classes_weight,
        smalls_weight,
    ) = masters
    da, db, ny, nc = (sizes[key] for key in ("da", "db", "y", "c"))
    dp, mp = (da * db, ny * nc)
    dp_axes, mp_axes = (("da", "db"), ("y", "c"))
    all_axes = dp_axes + mp_axes
    places_now = {key: lax.axis_index(key) for key in ("da", "db", "y", "c")}
    dp_index = places_now["da"] * db + places_now["db"]
    mp_index = places_now["y"] * nc + places_now["c"]
    places = layout()
    zero_index = jnp.zeros((), jnp.int32)

    def small_piece(key_name):
        begin_at, length = places[key_name]
        return smalls_weight[begin_at : begin_at + length]

    own_images = latents.shape[0]
    group_size = timesteps.shape[0]
    images_all = dp * group_size
    row_width = timetwo_weight.shape[0]
    width_mp = timetwo_weight.shape[1]
    mod_width = modulator_weight.shape[1]

    joined_width, mixback_width = (joined_weight.shape[1], mixback_weight.shape[1])
    hidden_width = expand_weight.shape[1]
    shard_one = jnp.concatenate(
        [
            lane_padded(expand_weight),
            lane_padded(jnp.concatenate([joined_weight, mixback_weight], 1)),
        ],
        1,
    )
    first = in_parts(lax.all_gather(shard_one.astype(jnp.bfloat16), all_axes), dp, mp)
    narrow = in_parts(
        lax.all_gather(lane_padded(narrow_weight).astype(jnp.bfloat16), all_axes), dp, mp
    )
    lanes = narrow.shape[3]
    mixback = first[:, :, :, lanes + joined_width : lanes + joined_width + mixback_width]

    facts_own = jnp.concatenate([timesteps, labels, dropped, buckets, counts])
    first_words = timeone_weight.size
    packed = small_gather(
        jnp.concatenate(
            [
                timeone_weight.astype(jnp.bfloat16).reshape(first_words),
                (facts_own // 8).astype(jnp.bfloat16),
                (facts_own % 8).astype(jnp.bfloat16),
            ]
        ),
        dp_axes,
        dp,
    )
    facts = packed[:, first_words:].astype(jnp.float32).reshape(dp, 2, facts_own.shape[0])
    facts = 8.0 * facts[:, 0] + facts[:, 1]
    times_all = facts[:, :group_size].reshape(images_all)
    labels_all = facts[:, group_size : 2 * group_size].reshape(images_all)
    dropped_all = facts[:, 2 * group_size : 3 * group_size].reshape(images_all)
    buckets_all = facts[:, 3 * group_size]
    token_count = jnp.sum(facts[:, 3 * group_size + 1]) * TOKS
    time_first = packed[:, :first_words].reshape(FREQ, width_mp)
    bucket_width = float(1000 // NB)
    rows_in = frequencies(
        jnp.concatenate([times_all, buckets_all * bucket_width + 0.5 * bucket_width])
    ).astype(jnp.bfloat16)
    hidden_time = jnp.dot(
        rows_in, time_first, preferred_element_type=jnp.float32
    ) + lax.dynamic_slice_in_dim(small_piece("time_bias_one"), mp_index * width_mp, width_mp)
    hidden_act = jax.nn.silu(hidden_time).astype(jnp.bfloat16)
    embed_part = dot_nt(hidden_act, timetwo_weight.astype(jnp.bfloat16))
    class_index = jnp.where(dropped_all > 0, float(NCLS), labels_all)
    onehot = (class_index[:, None] == jnp.arange(NCLS + 1, dtype=jnp.float32)[None, :]).astype(
        jnp.bfloat16
    )
    label_cols = jnp.dot(
        onehot, classes_weight.astype(jnp.bfloat16), preferred_element_type=jnp.float32
    )
    column_at = dp_index * row_width
    owner = column_at // width_mp
    label_part = lax.dynamic_slice_in_dim(label_cols, column_at - owner * width_mp, row_width, 1)
    label_part = jnp.where(mp_index == owner, label_part, 0.0)
    condition = jnp.sum(
        small_gather(
            jnp.concatenate([embed_part[:images_all] + label_part, embed_part[images_all:]], 0),
            mp_axes,
            mp,
        ),
        0,
    ) + lax.dynamic_slice_in_dim(small_piece("time_bias_two"), column_at, row_width)
    cond_act = jax.nn.silu(condition).astype(jnp.bfloat16)
    modulator = modulator_weight.astype(jnp.bfloat16)
    global_cols = mp_index * mod_width + jnp.arange(mod_width)
    mods_part = jnp.dot(cond_act, modulator, preferred_element_type=jnp.float32)
    outgoing = jnp.where(
        global_cols < 8 * D,
        mods_part[:images_all].reshape(dp, group_size, mod_width),
        mods_part[images_all:].reshape(dp, 1, mod_width),
    ).astype(jnp.bfloat16)
    incoming = lax.all_to_all(
        outgoing.reshape(dp * mp, own_images, mod_width), all_axes, 0, 0, tiled=True
    ).reshape(dp, mp, own_images, mod_width)
    modulation = jnp.sum(incoming.astype(jnp.float32), 0).transpose(1, 0, 2).reshape(
        own_images, 10 * D
    ) + small_piece("cond_bias")

    own_times = lax.dynamic_slice_in_dim(timesteps, mp_index * own_images, own_images)
    slot_index = mp_index * own_images + jnp.arange(own_images)
    valid_flags = (slot_index >= group_size - counts[0]).astype(jnp.float32)
    time_frac = (own_times.astype(jnp.float32) + 1.0) / 1000.0
    alpha_scale = jnp.cos(0.5 * math.pi * time_frac)[:, None, None]
    sigma_scale = jnp.sin(0.5 * math.pi * time_frac)[:, None, None]
    noisy_all = patchify(alpha_scale * latents + sigma_scale * noises)
    target = patchify(jnp.concatenate([alpha_scale * noises - sigma_scale * latents, noises], 1))
    embed_weight = small_piece("embed_weight").reshape(16, D)
    final_weight = small_piece("final_weight").reshape(D, 32)
    table = relative_tables(small_piece("rel_bias").reshape(H, REL))
    spots = spot_table()
    images = own_images
    rows_all = images * TOKS
    mods = modulation[:, : 8 * D].reshape(images, 8, D)

    embed_in = noisy_all.astype(jnp.bfloat16)
    stream_zero = (
        jnp.einsum(
            "ntc,cd->ntd",
            embed_in,
            embed_weight.astype(jnp.bfloat16),
            preferred_element_type=jnp.float32,
        )
        + small_piece("embed_bias")
        + position_table()
    )
    normed_a, _ = layernorm_parts(stream_zero)
    first_in = (
        normed_a * (1.0 + column_of(modulation, 1)) + column_of(modulation, 0)
    ).astype(jnp.bfloat16)
    added = jnp.stack(
        [
            (small_piece("query_bias") + modulation[:, 8 * D : 9 * D]).reshape(images, H, HD),
            jnp.zeros((images, H, HD), jnp.float32),
            (small_piece("value_bias") + modulation[:, 9 * D :]).reshape(images, H, HD),
        ],
        2,
    )
    added = added.reshape(images, mp, joined_width).transpose(1, 0, 2)[:, :, None]
    joined_rows, mixed, log_total = attention_forward(
        first_in, first, lanes, joined_width, added, table, spots
    )
    branch, stream_one, second_in = mixback_forward(
        mixed, mixback, stream_zero, mods, small_piece("out_bias")[None]
    )
    timetwo_narrow, second_in = tie(timetwo_weight.astype(jnp.bfloat16), second_in)
    time_second_all = small_gather(timetwo_narrow, dp_axes, dp)
    active, slope = expand_forward(
        second_in, first, lanes, hidden_width, small_piece("fc1_bias").reshape(mp, 1, hidden_width)
    )
    grad_two, grad_branch_two, sums_c, final_grads, output_sums = narrow_forward(
        active,
        narrow,
        lanes,
        hidden_width,
        stream_one,
        mods,
        small_piece("fc2_bias")[None],
        final_weight.astype(jnp.bfloat16),
        small_piece("final_bias")[None],
        target,
        jnp.broadcast_to(valid_flags[:, None, None], (images, 1, 128)),
    )
    loss_part = jnp.sum(output_sums[:, 1, 0])
    time_second_all, grad_branch_two = tie(time_second_all, grad_branch_two)
    time_second_all = time_second_all.reshape(D, width_mp)

    def flat(values):
        return values.reshape(rows_all, D)

    def in_rows(values):
        return values.reshape(mp, rows_all, values.shape[3])

    narrow_sum, heads_sum = (Exchange(sizes, places_now) for _ in range(2))
    narrow_pairs = [(flat(grad_branch_two), in_rows(active))]
    narrow_sum.gradient(narrow_pairs)
    grad_hidden, hidden_sums, grad_one, grad_branch, sums_b = feed_backward(
        grad_branch_two,
        first,
        narrow,
        lanes,
        hidden_width,
        slope,
        grad_two,
        stream_one,
        branch,
        mods,
        [narrow_sum.sent],
    )
    expand_all = whole_gradient(flat(second_in), in_rows(grad_hidden), dp)
    expand_shard = lax.psum_scatter(expand_all, all_axes, scatter_dimension=0, tiled=True)[0]
    narrow_sum.open_first(narrow_sum.kept_gradient(narrow_pairs, [expand_all]))
    narrow_sum.launch()
    grad_joined, column_sums, shifts = attention_backward(
        grad_branch, mixback, joined_rows, log_total, table, spots, list(narrow_sum.sent)
    )
    heads_pairs = [(flat(first_in), in_rows(grad_joined)), (flat(grad_branch), in_rows(mixed))]
    narrow_sum.arrived, heads_first = tie(narrow_sum.arrived, grad_joined)
    narrow_sum.open_second()
    narrow_sum.launch()
    heads_sum.gradient(heads_pairs, list(narrow_sum.sent))
    sums_a, embed_grads = joined_backward(
        heads_first,
        first,
        lanes,
        grad_one,
        stream_zero,
        mods,
        embed_in,
        [heads_sum.sent],
    )
    sums = (
        column_sums[:, :, 0]
        .reshape(mp, images, H // mp, 3, HD)
        .transpose(3, 1, 0, 2, 4)
        .reshape(3, images, D)
    )
    mods_grads = jnp.concatenate(
        [
            sums_a[:, 0],
            sums_a[:, 1],
            sums_b[:, 2],
            sums_b[:, 0],
            sums_b[:, 1],
            sums_c[:, 2],
            sums_c[:, 0],
            sums_c[:, 1],
            sums[0],
            sums[2],
        ],
        1,
    ).astype(jnp.bfloat16)
    to_owners = mods_grads.reshape(own_images, mp, mod_width).transpose(1, 0, 2)
    returned = lax.all_to_all(
        jnp.broadcast_to(to_owners[None], (dp,) + to_owners.shape).reshape(
            dp * mp, own_images, mod_width
        ),
        all_axes,
        0,
        0,
        tiled=True,
    )
    heads_kept = heads_sum.kept_gradient(heads_pairs, [to_owners])
    narrow_sum.open_last()
    narrow_sum.sent, heads_kept = tie(narrow_sum.sent, heads_kept)
    narrow_sum.launch_last()
    heads_kept, shifts, embed_grads, final_grads = tie(
        heads_kept, shifts, embed_grads, final_grads
    )
    returned, heads_kept = tie(returned, heads_kept)
    heads_sum.open_first(heads_kept)
    heads_sum.sent, returned = tie(heads_sum.sent, returned)
    heads_sum.launch()
    returned = returned.reshape(images_all, mod_width)
    grad_small = {
        "embed_bias": jnp.sum(sums_a[:, 2], 0),
        "query_bias": jnp.sum(sums[0], 0),
        "value_bias": jnp.sum(sums[2], 0),
        "out_bias": jnp.sum(sums_b[:, 3], 0),
        "fc1_bias": hidden_sums.reshape(FF),
        "fc2_bias": jnp.sum(sums_c[:, 3], 0),
        "final_bias": jnp.sum(output_sums[:, 0], 0),
        "embed_weight": jnp.sum(embed_grads, 0).reshape(16 * D),
        "final_weight": jnp.sum(final_grads, 0).T.reshape(32 * D),
        "rel_bias": relative_gradient(shifts[:, :, HD:]),
    }

    is_image = (global_cols < 8 * D)[None, :]
    returned_wide = returned.astype(jnp.float32)
    cond_bias_grad = jnp.sum(returned_wide, 0)
    bucket_sums = jnp.where(
        is_image, 0.0, jnp.sum(returned_wide.reshape(dp, group_size, mod_width), 1)
    )

    def split_rows(image_rows, bucket_rows):
        upper, lower = two_terms(bucket_rows)
        return jnp.concatenate([image_rows.astype(jnp.bfloat16), upper, lower], 0)

    def double_rows(rows):
        return jnp.concatenate([rows, rows[images_all:]], 0)

    grad_mod = split_rows(jnp.where(is_image, returned, jnp.zeros_like(returned)), bucket_sums)
    modulator_grad = dot_tn(double_rows(cond_act), grad_mod)
    cond_part = dot_nt(grad_mod, modulator)
    cond_part = jnp.concatenate(
        [cond_part[:images_all], cond_part[images_all : images_all + dp] + cond_part[images_all + dp :]],
        0,
    )
    grad_act = small_gather(cond_part, mp_axes, mp)
    grad_act, narrow_sum.arrived, expand_shard, grad_small = tie(
        grad_act, narrow_sum.arrived, expand_shard, grad_small
    )
    grad_act = jnp.sum(grad_act, 0)
    _, pullback = jax.vjp(jax.nn.silu, condition)
    grad_cond_own = pullback(grad_act)[0]
    grad_embed_own = split_rows(grad_cond_own[:images_all], grad_cond_own[images_all:])
    timetwo_grad = dot_tn(grad_embed_own, double_rows(hidden_act))
    grad_cond = small_gather(grad_cond_own, dp_axes, dp)
    heads_sum.open_second()
    heads_sum.launch()
    grad_cond, heads_sum.arrived = tie(grad_cond, heads_sum.arrived)
    grad_cond = (
        grad_cond
        .transpose(1, 0, 2)
        .reshape(images_all + dp, D)
    )
    vector = jnp.concatenate([grad_small[key_name] for key_name in TOKEN_SMALLS])
    slice_length = -(-vector.shape[0] // (dp * mp))
    padded = jnp.pad(vector, (0, slice_length * dp * mp - vector.shape[0]))
    padded, grad_cond = tie(padded.reshape(dp * mp, slice_length), grad_cond)
    slice_sum = jnp.sum(lax.all_to_all(padded, all_axes, 0, 0, tiled=True), 0)
    grad_embed = split_rows(grad_cond[:images_all], grad_cond[images_all:])
    bias_two_grad = jnp.sum(grad_embed.astype(jnp.float32), 0)
    grad_hidden_act = dot_nn(grad_embed, time_second_all)
    grad_hidden_act = jnp.concatenate(
        [
            grad_hidden_act[:images_all],
            grad_hidden_act[images_all : images_all + dp] + grad_hidden_act[images_all + dp :],
        ],
        0,
    )
    _, pullback = jax.vjp(jax.nn.silu, hidden_time)
    grad_hidden_time = pullback(grad_hidden_act)[0]
    grad_hidden_time = split_rows(grad_hidden_time[:images_all], grad_hidden_time[images_all:])
    bias_one_grad = jnp.sum(grad_hidden_time.astype(jnp.float32), 0)
    rows_own = lax.dynamic_slice_in_dim(
        rows_in, dp_index * timeone_weight.shape[0], timeone_weight.shape[0], 1
    )
    timeone_grad = dot_tn(double_rows(rows_own), grad_hidden_time)
    label_rows = lax.dynamic_slice_in_dim(grad_cond[:images_all], mp_index * width_mp, width_mp, 1)
    label_upper, label_lower = two_terms(label_rows)
    class_raw = dot_tn(
        jnp.concatenate([onehot, onehot], 0), jnp.concatenate([label_upper, label_lower], 0)
    )

    heads_sum.open_last()
    heads_sum.launch_last()
    heads_grad, narrow_grad = (member.result() for member in (heads_sum, narrow_sum))
    expand_grad = expand_shard.astype(jnp.float32)
    joined_grad, mixback_grad = (heads_grad[:, :joined_width], heads_grad[:, joined_width:])
    mod_slice = -(-mod_width // dp)
    one_slice = -(-width_mp // dp)
    own_cond = lax.dynamic_slice_in_dim(
        jnp.pad(cond_bias_grad, (0, mod_slice * dp - mod_width)), dp_index * mod_slice, mod_slice
    )
    own_one = lax.dynamic_slice_in_dim(
        jnp.pad(bias_one_grad, (0, one_slice * dp - width_mp)), dp_index * one_slice, one_slice
    )
    own_two = lax.dynamic_slice_in_dim(bias_two_grad, column_at, row_width)

    owned = [
        member / token_count
        for member in (
            joined_grad,
            mixback_grad,
            expand_grad,
            narrow_grad,
            timeone_grad,
            timetwo_grad,
            modulator_grad,
        )
    ]
    class_grad = class_raw / token_count
    own_slices = jnp.concatenate([slice_sum, own_cond, own_one]) / token_count
    squares = sum((jnp.sum(member * member) for member in owned)) + jnp.sum(own_slices * own_slices)
    squares = squares + jnp.where(dp_index == 0, jnp.sum(class_grad * class_grad), 0.0)
    own_two = own_two / token_count
    squares = squares + jnp.where(mp_index == 0, jnp.sum(own_two * own_two), 0.0)
    final = small_gather(
        jnp.concatenate([own_slices, squares[None], loss_part[None]]), all_axes, dp * mp
    )
    ends = slice_length + mod_slice + one_slice
    grad_norm = jnp.sqrt(jnp.sum(final[:, ends]))
    loss_sum = jnp.sum(final[:, ends + 1])
    factor = jnp.minimum(1.0, clip_level / grad_norm)
    token_smalls = final[:, :slice_length].reshape(dp * mp * slice_length)
    cond_bias = (
        final[:, slice_length : slice_length + mod_slice]
        .reshape(dp, mp, mod_slice)
        .transpose(1, 0, 2)
        .reshape(mp, dp * mod_slice)[:, :mod_width]
        .reshape(10 * D)
    )
    time_bias_one = (
        final[:, slice_length + mod_slice : ends]
        .reshape(dp, mp, one_slice)
        .transpose(1, 0, 2)
        .reshape(mp, dp * one_slice)[:, :width_mp]
        .reshape(D)
    )
    small_grad = jnp.concatenate(
        [
            token_smalls[:D],
            time_bias_one,
            bias_two_grad / token_count,
            cond_bias,
            token_smalls[D : smalls_weight.shape[0] - 12 * D],
        ]
    )
    gradients = owned + [class_grad, small_grad]
    results = [loss_sum, token_count, grad_norm]
    for master, moment, second, gradient in zip(masters, moments, seconds, gradients):
        results.extend(adamw_update(master, moment, second, gradient * factor))
    return tuple(results)


def solution(mesh):
    dp, mp = (mesh.shape["dp"], mesh.shape["mp"])
    sizes = {"da": dp // 2, "db": 2, "y": mp // 2, "c": 2}
    inner = Mesh(
        mesh.devices.reshape(sizes["da"], sizes["db"], sizes["y"], sizes["c"]),
        ("da", "db", "y", "c"),
    )
    groups, parts = (("da", "db"), ("y", "c"))
    weight_specs = (P(groups, parts),) * 21 + (P(None, parts),) * 3 + (P(),) * 3
    in_specs = (P(groups + parts, None, None),) * 2 + (P(groups),) * 5 + weight_specs
    out_specs = (P(),) * 3 + weight_specs
    return jax.shard_map(
        partial(per_device, sizes),
        mesh=inner,
        in_specs=in_specs,
        out_specs=out_specs,
        check_vma=False,
    )
```
